512 devices in a mesh: replica: 32 (over z, core), tensor: 16 (over x, y).
Axes of the slice: x: 4, y: 4, z: 16, core: 2. Of those that a mesh axis runs over, the one named last changes fastest.
Arguments:
- x_input: bfloat16 [8192, 4096], P('replica', 'tensor'), may hold values from -6 to 6
- z_input: bfloat16 [8192, 4096], P('replica', 'tensor'), may hold values from -6 to 6
- bc_input: bfloat16 [8192, 1024], P('replica'), may hold values from -6 to 6
- dt_raw: float32 [8192, 128], P('replica', 'tensor'), may hold values from -6 to 6
- dt_bias: float32 [128], P('tensor'), may hold values from -3 to -1
- decay_rates: float32 [128], P('tensor'), may hold values from 0.005 to 0.5
- skip_gain: float32 [128], P('tensor'), may hold values from 0.5 to 1.5
- conv_x: float32 [4, 4096], P(None, 'tensor'), may hold values from -3 to 3
- conv_bc: float32 [4, 1024], replicated, may hold values from -3 to 3
- norm_gain: float32 [4096], P('tensor'), may hold values from 0.5 to 1.5
- out_weight: bfloat16 [4096, 4096], P('tensor'), may hold values from -0.09375 to 0.09375
- cached_states: float32 [64, 128, 32, 128], P('replica', 'tensor'), may hold values from -4 to 4
- cached_tail_x: float32 [64, 3, 4096], P('replica', None, 'tensor'), may hold values from -6 to 6
- cached_tail_bc: float32 [64, 3, 1024], P('replica'), may hold values from -6 to 6
- prefix_block: int32 [64], replicated, may hold values from 0 to 63, as said below
- lengths: int32 [64], P('replica'), may hold values from 128 to 128, as said below
Outputs:
- mixed: bfloat16 [8192, 4096], P(('replica', 'tensor'))
- final_states: float32 [64, 128, 32, 128], P('replica', 'tensor')
The draws below stay inside these ranges and needn't reach their ends.
Inputs may be any that keep to these rules, and one draw needn't show every extreme that they name: A permutation: request q (on replica q // 2) starts from cached block prefix_block[q], which replica prefix_block[q] // 2 holds; every cached block feeds exactly one request. `lengths`: every request's suffix fills all 128 of its slots, so every entry is 128.
All inputs are finite; a program needn't handle non-finite values.
Results may differ from the reference program's by a relative error of at most 0.015.
Values may be sent and summed in bfloat16 or wider, within the bound.
A program may use at most 64 MiB of HBM per device.

```python
import math
import jax
import jax.numpy as jnp
from jax import lax

HEADS = 128
HEAD_DIM = 32
STATE = 128
GROUPS = 4
CONV = 4
DOUT = 4096
SPAN = 128
REQ = 2
SLOT_LEN = 128
INNER = 4096
TOKENS = 8192
BLOCKS = 64
N_TENSOR = 16


def draw_lengths(key, part):
    most_blocks = SLOT_LEN // SPAN
    counts = jax.random.randint(jax.random.fold_in(key, 11), (BLOCKS,), 1, most_blocks + 1)
    fullest = jax.random.randint(jax.random.fold_in(key, 12), (), 0, BLOCKS)
    step_away = jax.random.randint(jax.random.fold_in(key, 13), (), 1, BLOCKS)
    shortest = (fullest + step_away) % BLOCKS
    places = jnp.arange(BLOCKS)
    counts = jnp.where(places == fullest, most_blocks, counts)
    counts = jnp.where(places == shortest, 1, counts)
    return (counts * SPAN).astype(jnp.int32)


def draw_prefix_block(key, part):
    replicas = BLOCKS // REQ
    shuffled = jax.random.permutation(jax.random.fold_in(key, 21), BLOCKS).astype(jnp.int32)
    chosen = jax.random.randint(jax.random.fold_in(key, 22), (), 0, BLOCKS).astype(jnp.int32)
    far_slot = jax.random.randint(jax.random.fold_in(key, 23), (), 0, REQ).astype(jnp.int32)
    target = (chosen // REQ + replicas // 2) % replicas * REQ + far_slot
    places = jnp.arange(BLOCKS, dtype=jnp.int32)
    holder = jnp.sum(jnp.where(shuffled == target, places, 0)).astype(jnp.int32)
    previous = jnp.sum(jnp.where(places == chosen, shuffled, 0)).astype(jnp.int32)
    result = jnp.where(places == chosen, target, jnp.where(places == holder, previous, shuffled))
    return result.astype(jnp.int32)


def block_levels(own_key, extent, cuts, low, top_value):
    factor_of = 1.0
    for position, parts in cuts:
        heights = jax.random.uniform(jax.random.fold_in(jax.random.fold_in(own_key, 6), position), (parts,), jnp.float32, low / len(cuts), top_value / len(cuts))
        factor_of = factor_of * jnp.repeat(jnp.exp(heights), extent[position] // parts).reshape((-1,) + (1,) * (len(extent) - 1 - position))
    return factor_of


def scatter_about(rng, dims, width, bound, cuts=(), kind=jnp.bfloat16):
    drawn = width * jax.random.normal(rng, dims, jnp.float32)
    if cuts:
        drawn = drawn * block_levels(rng, dims, cuts, -0.22, 0.18)
    return jnp.clip(drawn, -bound, bound).astype(kind)


def setup_inputs(seed: int = 0) -> dict:
    key_of = jax.random.split(jax.random.key(seed), 17)
    x_input = scatter_about(key_of[0], (TOKENS, INNER), 1.0, 6.0, ((0, 32), (1, 16)))
    z_input = scatter_about(key_of[1], (TOKENS, INNER), 1.0, 6.0, ((0, 32), (1, 16)))
    bc_input = scatter_about(key_of[2], (TOKENS, 2 * GROUPS * STATE), 1.0, 6.0, ((0, 32),))
    dt_raw = scatter_about(key_of[3], (TOKENS, HEADS), 1.0, 6.0, ((0, 32), (1, 16)), jnp.float32)
    dt_bias = jnp.clip(-3.0 + 2.0 * jax.random.uniform(key_of[4], (HEADS,), jnp.float32) ** block_levels(key_of[4], (HEADS,), ((0, 16),), -0.2, 0.2), -3.0, -1.0)
    decay_rates = jnp.clip(jnp.exp(math.log(0.5) - 4.6051702 * jax.random.uniform(key_of[5], (HEADS,), jnp.float32) ** block_levels(key_of[5], (HEADS,), ((0, 16),), -0.2, 0.2)), 0.005, 0.5)
    skip_gain = jnp.clip(0.5 + 1.0 * jax.random.uniform(key_of[6], (HEADS,), jnp.float32) ** block_levels(key_of[6], (HEADS,), ((0, 16),), -0.2, 0.2), 0.5, 1.5)
    conv_x = scatter_about(key_of[7], (CONV, INNER), CONV ** -0.5, 3.0, ((1, 16),), jnp.float32)
    conv_bc = scatter_about(key_of[8], (CONV, 2 * GROUPS * STATE), CONV ** -0.5, 3.0, (), jnp.float32)
    norm_gain = jnp.clip(1.0 + 0.1 * jax.random.normal(key_of[9], (INNER,), jnp.float32), 0.5, 1.5)
    out_weight = scatter_about(key_of[10], (INNER, DOUT), INNER ** -0.5, 0.09375, ((0, 16),))
    cached_states = scatter_about(key_of[11], (BLOCKS, HEADS, HEAD_DIM, STATE), 0.5, 4.0, ((0, 32), (1, 16)), jnp.float32)
    cached_tail_x = scatter_about(key_of[12], (BLOCKS, CONV - 1, INNER), 1.0, 6.0, ((0, 32), (2, 16)), jnp.float32)
    cached_tail_bc = scatter_about(key_of[13], (BLOCKS, CONV - 1, 2 * GROUPS * STATE), 1.0, 6.0, ((0, 32),), jnp.float32)
    prefix_block = draw_prefix_block(jax.random.fold_in(key_of[16], 71), 0)
    lengths = draw_lengths(jax.random.fold_in(key_of[16], 71), 0)
    return {"x_input": x_input, "z_input": z_input, "bc_input": bc_input, "dt_raw": dt_raw, "dt_bias": dt_bias, "decay_rates": decay_rates, "skip_gain": skip_gain, "conv_x": conv_x, "conv_bc": conv_bc, "norm_gain": norm_gain, "out_weight": out_weight, "cached_states": cached_states, "cached_tail_x": cached_tail_x, "cached_tail_bc": cached_tail_bc, "prefix_block": prefix_block, "lengths": lengths}


highest = lax.Precision.HIGHEST
epsilon = 1e-05

def causal_conv(tail_rows, sequence, kernel):
    joined = jnp.concatenate([tail_rows, sequence], axis=0)
    length = sequence.shape[0]
    total = joined[0:length] * kernel[0][None, :]
    for offset in range(1, kernel.shape[0]):
        total = total + joined[offset:offset + length] * kernel[offset][None, :]
    return jax.nn.silu(total)

def span_scan(inputs, b_heads, c_heads, step_sizes, decay_rates, skip_gain, carry_state):
    logdec = -step_sizes * decay_rates[None, :]
    cumulative = jnp.cumsum(logdec, axis=0)
    count_rows = inputs.shape[0]
    causal = jnp.arange(count_rows)[:, None] >= jnp.arange(count_rows)[None, :]
    cum_heads = jnp.transpose(cumulative)
    differ = cum_heads[:, :, None] - cum_heads[:, None, :]
    decays = jnp.where(causal[None, :, :], jnp.exp(jnp.minimum(differ, 0.0)), 0.0)
    scores = jnp.einsum('ihn,jhn->hij', c_heads, b_heads, precision=highest)
    weights = scores * decays * jnp.transpose(step_sizes)[:, None, :]
    inside = jnp.einsum('hij,jhp->ihp', weights, inputs, precision=highest)
    carried = jnp.exp(cumulative)[:, :, None] * jnp.einsum('ihn,hpn->ihp', c_heads, carry_state, precision=highest)
    output = inside + carried + skip_gain[None, :, None] * inputs
    ending = cumulative[-1]
    weigh_in = jnp.exp(ending[None, :] - cumulative) * step_sizes
    new_state = jnp.exp(ending)[:, None, None] * carry_state + jnp.einsum('jh,jhp,jhn->hpn', weigh_in, inputs, b_heads, precision=highest)
    return (output, new_state)

def request_forward(x_seq, bc_seq, dt_seq, length, carry_state, tail_x, tail_bc, conv_x, conv_bc, dt_bias, decay_rates, skip_gain, member):
    count_rows = x_seq.shape[0]
    heads_here = dt_seq.shape[1]
    inputs = causal_conv(tail_x, x_seq.astype(jnp.float32), conv_x).reshape(count_rows, heads_here, HEAD_DIM)
    bc_conv = causal_conv(tail_bc, bc_seq.astype(jnp.float32), conv_bc)
    b_groups = bc_conv[:, :GROUPS * STATE].reshape(count_rows, GROUPS, STATE)
    c_groups = bc_conv[:, GROUPS * STATE:].reshape(count_rows, GROUPS, STATE)
    b_heads = jnp.einsum('lgn,hg->lhn', b_groups, member, precision=highest)
    c_heads = jnp.einsum('lgn,hg->lhn', c_groups, member, precision=highest)
    live = (jnp.arange(count_rows) < length)[:, None]
    step_sizes = jnp.where(live, jax.nn.softplus(dt_seq + dt_bias[None, :]), 0.0)
    pieces = []
    for start in range(0, count_rows, SPAN):
        output, carry_state = span_scan(inputs[start:start + SPAN], b_heads[start:start + SPAN], c_heads[start:start + SPAN], step_sizes[start:start + SPAN], decay_rates, skip_gain, carry_state)
        pieces.append(output)
    return (jnp.concatenate(pieces, axis=0).reshape(count_rows, -1), carry_state)

def reference(x_input, z_input, bc_input, dt_raw, dt_bias, decay_rates, skip_gain, conv_x, conv_bc, norm_gain, out_weight, cached_states, cached_tail_x, cached_tail_bc, prefix_block, lengths):
    member = ((jnp.arange(HEADS) // (HEADS // GROUPS))[:, None] == jnp.arange(GROUPS)[None, :]).astype(jnp.float32)
    start_states = jnp.take(cached_states, prefix_block, axis=0)
    start_tail_x = jnp.take(cached_tail_x, prefix_block, axis=0)
    start_tail_bc = jnp.take(cached_tail_bc, prefix_block, axis=0)

    def one_request(items):
        x_seq, bc_seq, dt_seq, length, carry_state, tail_x, tail_bc = items
        return request_forward(x_seq, bc_seq, dt_seq, length, carry_state, tail_x, tail_bc, conv_x, conv_bc, dt_bias, decay_rates, skip_gain, member)
    outputs, final_states = lax.map(one_request, (x_input.reshape(BLOCKS, SLOT_LEN, INNER), bc_input.reshape(BLOCKS, SLOT_LEN, 2 * GROUPS * STATE), dt_raw.reshape(BLOCKS, SLOT_LEN, HEADS), lengths, start_states, start_tail_x, start_tail_bc))
    outputs = outputs.reshape(TOKENS, INNER)
    live = (jnp.arange(SLOT_LEN)[None, :] < lengths[:, None]).reshape(TOKENS, 1)
    gate_vals = outputs * jax.nn.silu(z_input.astype(jnp.float32))
    grouped = gate_vals.reshape(TOKENS, GROUPS, INNER // GROUPS)
    mean_sq = lax.optimization_barrier(jnp.mean(grouped * grouped, axis=2, keepdims=True))
    normed = (grouped * lax.rsqrt(mean_sq + epsilon)).reshape(TOKENS, INNER) * norm_gain[None, :]
    gated = jnp.where(live, normed, 0.0).astype(jnp.bfloat16)
    block_rows = INNER // N_TENSOR

    def add_block(number, total):
        rows_in = lax.dynamic_slice_in_dim(gated, number * block_rows, block_rows, 1)
        weight_rows = lax.dynamic_slice_in_dim(out_weight, number * block_rows, block_rows, 0)
        part = jnp.dot(rows_in, weight_rows, preferred_element_type=jnp.float32).astype(jnp.bfloat16)
        part = lax.optimization_barrier(part)
        return total + part.astype(jnp.float32)
    mixed = lax.fori_loop(0, N_TENSOR, add_block, jnp.zeros((TOKENS, DOUT), jnp.float32)).astype(jnp.bfloat16)
    return (mixed, final_states)
```

```python
import functools

import jax
import jax.numpy as jnp
from jax import lax
from jax.experimental import pallas as pl
from jax.experimental.pallas import tpu as pltpu
from jax.sharding import PartitionSpec as P

MESH = pl.DeviceIdType.MESH
HIGHEST = lax.Precision.HIGHEST
F32 = jnp.float32
BF16 = jnp.bfloat16
HEAD_DIM = 32
STATE = 128
EPSILON = 1e-05
TAIL_ROWS = 12

NT_DIMS = (((1,), (1,)), ((), ()))
TN_DIMS = (((0,), (0,)), ((), ()))


def dot_nt(a, b, precision=None):
    return lax.dot_general(a, b, NT_DIMS, precision=precision, preferred_element_type=F32)


def dot_tn(a, b, precision=None):
    return lax.dot_general(a, b, TN_DIMS, precision=precision, preferred_element_type=F32)


def iota(shape, axis):
    return lax.broadcasted_iota(jnp.int32, shape, axis)


def silu(a):
    return a / (1.0 + jnp.exp(-a))


def layer_kernel(
    sizes,
    prefix_s,
    lengths_s,
    bias_s,
    rates_s,
    skip_s,
    x_h,
    z_h,
    bc_h,
    dt_h,
    convx_h,
    convbc_h,
    gain_h,
    weight_h,
    states_h,
    tailx_h,
    tailbc_h,
    mixed_o,
    final_o,
    x_v,
    z_v,
    bc_v,
    dt_v,
    convx_v,
    convbc_v,
    gain_v,
    st_v,
    tailx_v,
    tailbc_v,
    send1,
    recv1,
    send2,
    recv2,
    tsend1,
    trecv1,
    tsend2,
    trecv2,
    w_a,
    w_b,
    xraw,
    bcraw,
    gate,
    decay,
    expcum,
    weighin,
    ending,
    v_f,
    v_a,
    v_b,
    r_a,
    r_b,
    ss_send,
    ss_recv,
    o_a,
    o_b,
    ro_a,
    ro_b,
    load_sem,
    own_sem,
    s1_send,
    s1_recv,
    s2_send,
    s2_recv,
    t1_send,
    t1_recv,
    t2_send,
    t2_recv,
    w_send,
    w_recv,
    va_send,
    va_recv,
    vb_send,
    vb_recv,
    ss_ssem,
    ss_rsem,
    oa_send,
    oa_recv,
    ob_send,
    ob_recv,
):
    nr, nx, ny = sizes
    nz = nr // 2
    groups = nx
    tokens, width = x_v.shape
    heads = width // HEAD_DIM
    slot = tokens // 2
    rows_owner = tokens // (nx * ny)
    piece = width // nr
    tail_n = trecv2.shape[0]
    tail_p = TAIL_ROWS // tail_n
    quarter = w_a.shape[2]
    half_cols = 2 * quarter

    me_r = lax.axis_index("replica")
    me_t = lax.axis_index("tensor")
    zi, ci = me_r // 2, me_r % 2
    xi, yi = me_t // ny, me_t % ny

    def each_replica(fn):
        def step(m, carry):
            k = (m + 1) // 2
            dz = nz // 2 + k * (1 - 2 * (m % 2))
            zz = (zi + dz) % nz
            fn(zz * 2)
            fn(zz * 2 + 1)
            return carry

        lax.fori_loop(0, nz - 1, step, 0)
        fn(zi * 2 + 1 - ci)

    def y_peers():
        out = []
        for d in range(ny):
            for dc in range(2):
                if d or dc:
                    out.append(((yi + d) % ny, (ci + dc) % 2))
        return out

    def x_peers():
        out = []
        for d in range(nx):
            for dc in range(2):
                if d or dc:
                    out.append(((xi + d) % nx, (ci + dc) % 2))
        return out

    def tensor_of(xx, yy):
        return xx * ny + yy

    def remote(src, dst, ssem, rsem, rr, tt):
        return pltpu.make_async_remote_copy(
            src_ref=src,
            dst_ref=dst,
            send_sem=ssem,
            recv_sem=rsem,
            device_id=(rr, tt),
            device_id_type=MESH,
        )

    barrier = pltpu.get_barrier_semaphore()

    def greet(rr, tt):
        pl.semaphore_signal(barrier, inc=1, device_id=(rr, tt), device_id_type=MESH)

    each_replica(lambda rr: greet(rr, me_t))
    for d in range(1, ny):
        for cc in range(2):
            greet(zi * 2 + cc, tensor_of(xi, (yi + d) % ny))
    for d in range(1, nx):
        for cc in range(2):
            greet(zi * 2 + cc, tensor_of((xi + d) % nx, yi))
    expected = 2 * (nz - 1) + 1 + 2 * (ny - 1) + 2 * (nx - 1)

    b_lo = pl.multiple_of(xi * STATE, STATE)
    c_lo = pl.multiple_of((groups + xi) * STATE, STATE)
    cols_a = pl.ds(pl.multiple_of(ci * quarter, quarter), quarter)
    cols_b = pl.ds(pl.multiple_of(half_cols + ci * quarter, quarter), quarter)
    lane_b, lane_c = pl.ds(0, STATE), pl.ds(STATE, STATE)
    loads = []

    def load(src, dst):
        copy = pltpu.make_async_copy(src, dst, load_sem.at[len(loads)])
        copy.start()
        loads.append(copy)
        return copy

    load_states = load(states_h, st_v)
    load_tx = load(tailx_h, tailx_v)
    load_tb = load(tailbc_h.at[:, :, pl.ds(b_lo, STATE)], tailbc_v.at[:, :, lane_b])
    load_tc = load(tailbc_h.at[:, :, pl.ds(c_lo, STATE)], tailbc_v.at[:, :, lane_c])
    load_dt = load(dt_h, dt_v)
    load_x = load(x_h, x_v)
    load_b = load(bc_h.at[:, pl.ds(b_lo, STATE)], bc_v.at[:, lane_b])
    load_c = load(bc_h.at[:, pl.ds(c_lo, STATE)], bc_v.at[:, lane_c])
    load_cx = load(convx_h, convx_v)
    load_cb = load(convbc_h.at[:, pl.ds(b_lo, STATE)], convbc_v.at[:, lane_b])
    load_cc = load(convbc_h.at[:, pl.ds(c_lo, STATE)], convbc_v.at[:, lane_c])
    load_z = load(z_h, z_v)
    load_g = load(gain_h, gain_v)
    load_wa = load(weight_h.at[:, cols_a], w_a.at[yi])
    load_wb = load(weight_h.at[:, cols_b], w_b.at[xi])

    load_states.wait()
    packed = st_v[...].reshape(2, nr, piece, STATE)
    for b in range(2):
        send1[:, b * piece : (b + 1) * piece, :] = packed[b].astype(BF16)
    load_tx.wait()
    load_tb.wait()
    load_tc.wait()
    for row in range(TAIL_ROWS):
        t, part = row // 4, row % 4
        for b in range(2):
            src = tailx_v if part < 2 else tailbc_v
            lanes = slice((part % 2) * STATE, (part % 2 + 1) * STATE)
            at = b * tail_p + row % tail_p
            tsend1[row // tail_p, at : at + 1, :] = src[b, t : t + 1, lanes]

    load_dt.wait()
    head_lane = iota((1, heads), 1)
    bias_row = jnp.zeros((1, heads), F32)
    rate_row = jnp.zeros((1, heads), F32)
    skip_row = jnp.zeros((1, heads), F32)
    for h in range(heads):
        bias_row = jnp.where(head_lane == h, bias_s[h], bias_row)
        rate_row = jnp.where(head_lane == h, rates_s[h], rate_row)
        skip_row = jnp.where(head_lane == h, skip_s[h], skip_row)
    spread = (iota((heads, width), 1) // HEAD_DIM == iota((heads, width), 0)).astype(F32)
    eye_h = (iota((heads, heads), 0) == iota((heads, heads), 1)).astype(F32)
    row_i = iota((slot, slot), 0)
    col_i = iota((slot, slot), 1)
    causal = row_i >= col_i
    lower = causal.astype(F32)

    for q in range(2):
        raw = dt_v[q * slot : (q + 1) * slot, :] + bias_row
        soft = jnp.maximum(raw, 0.0) + jnp.log1p(jnp.exp(-jnp.abs(raw)))
        live = iota((slot, heads), 0) < lengths_s[q]
        dt = jnp.where(live, soft, 0.0)
        logdec = -dt * rate_row
        cum = jnp.dot(lower, logdec, precision=HIGHEST, preferred_element_type=F32)
        cum_t = dot_nt(eye_h, cum, HIGHEST)
        dt_t = dot_nt(eye_h, dt, HIGHEST)
        for h in range(heads):
            differ = cum[:, h : h + 1] - cum_t[h : h + 1, :]
            value = jnp.where(causal, jnp.exp(jnp.minimum(differ, 0.0)), 0.0)
            decay[q, h] = value * dt_t[h : h + 1, :]
        expcum[q] = jnp.dot(jnp.exp(cum), spread, precision=HIGHEST, preferred_element_type=F32)
        last = cum[slot - 1 : slot, :]
        weigh = jnp.exp(last - cum) * dt
        weighin[q] = jnp.dot(weigh, spread, precision=HIGHEST, preferred_element_type=F32)
        end_t = jnp.broadcast_to(jnp.exp(cum_t[:, slot - 1 : slot]), (heads, STATE))
        ending[q] = dot_tn(spread, end_t, HIGHEST)
    skip_wide = jnp.dot(skip_row, spread, precision=HIGHEST, preferred_element_type=F32)

    def raw_conv(seq, taps):
        total = seq * taps[3:4, :]
        at = iota(seq.shape, 0)
        for n in range(1, 4):
            moved = jnp.where(at >= n, pltpu.roll(seq, n, 0), 0.0)
            total = total + moved * taps[3 - n : 4 - n, :]
        return total

    load_x.wait()
    load_cx.wait()
    load_b.wait()
    load_c.wait()
    load_cb.wait()
    load_cc.wait()
    load_z.wait()
    for q in range(2):
        part = slice(q * slot, (q + 1) * slot)
        xraw[q] = raw_conv(x_v[part, :].astype(F32), convx_v[...])
        bcraw[q] = raw_conv(bc_v[part, :].astype(F32), convbc_v[...])
        gate[q] = silu(z_v[part, :].astype(F32))
    load_g.wait()
    load_wa.wait()
    load_wb.wait()

    pl.semaphore_wait(barrier, expected)

    def first_copy(rr):
        return remote(send1.at[rr], recv1.at[me_r], s1_send.at[rr], s1_recv.at[me_r], rr, me_t)

    def first_tail(rr):
        return remote(tsend1.at[rr], trecv1.at[me_r], t1_send.at[rr], t1_recv.at[me_r], rr, me_t)

    def start_first(rr):
        first_copy(rr).start()

        @pl.when(rr < tail_n)
        def _():
            first_tail(rr).start()

    each_replica(start_first)
    own1 = pltpu.make_async_copy(send1.at[me_r], recv1.at[me_r], own_sem.at[0])
    own1.start()

    @pl.when(me_r < tail_n)
    def _():
        copy = pltpu.make_async_copy(tsend1.at[me_r], trecv1.at[me_r], own_sem.at[1])
        copy.start()
        copy.wait()

    up_y, dn_y = (yi + 1) % ny, (yi + ny - 1) % ny
    up_x, dn_x = (xi + 1) % nx, (xi + nx - 1) % nx
    fill = w_a.shape[1] // 2

    def weight_copy(buf, at, lo, size, index, tt):
        ref = buf.at[at, pl.ds(lo, size), :]
        return remote(ref, ref, w_send.at[index], w_recv.at[index], me_r, tt)

    whole = 2 * fill
    wa_up = weight_copy(w_a, yi, 0, whole, 0, tensor_of(xi, up_y))
    wb_up = weight_copy(w_b, xi, 0, whole, 2, tensor_of(up_x, yi))
    wa_up.start()
    wb_up.start()
    if ny > 2:
        wa_dn = weight_copy(w_a, yi, 0, whole, 1, tensor_of(xi, dn_y))
        wa_dn.start()
    if nx > 2:
        wb_dn = weight_copy(w_b, xi, 0, whole, 3, tensor_of(dn_x, yi))
        wb_dn.start()

    def wait_first(rr):
        remote(send1.at[rr], recv1.at[rr], s1_send.at[rr], s1_recv.at[rr], rr, me_t).wait_recv()

        @pl.when(me_r < tail_n)
        def _():
            remote(
                tsend1.at[0], trecv1.at[rr], t1_send.at[0], t1_recv.at[rr], rr, me_t
            ).wait_recv()

    own1.wait()
    each_replica(wait_first)

    def pick(block):
        both = recv1[block // 2].astype(F32)
        return jnp.where(block % 2 == 1, both[piece:, :], both[:piece, :])

    def choose(rr, carry):
        first = pick(prefix_s[2 * rr])
        second = pick(prefix_s[2 * rr + 1])
        send2[rr] = jnp.concatenate([first, second], axis=0).astype(BF16)
        return carry

    lax.fori_loop(0, nr, choose, 0)

    @pl.when(me_r < tail_n)
    def _():
        def choose_tail(rr, carry):
            for s in range(2):
                block = prefix_s[2 * rr + s]
                both = trecv1[block // 2]
                tsend2[rr, s * tail_p : (s + 1) * tail_p, :] = jnp.where(
                    block % 2 == 1, both[tail_p:, :], both[:tail_p, :]
                )
            return carry

        lax.fori_loop(0, nr, choose_tail, 0)

    def start_second(rr):
        remote(
            send2.at[rr], recv2.at[me_r], s2_send.at[rr], s2_recv.at[me_r], rr, me_t
        ).start()

        @pl.when(me_r < tail_n)
        def _():
            remote(
                tsend2.at[rr], trecv2.at[me_r], t2_send.at[rr], t2_recv.at[me_r], rr, me_t
            ).start()

    each_replica(start_second)
    own2 = pltpu.make_async_copy(send2.at[me_r], recv2.at[me_r], own_sem.at[2])
    own2.start()

    @pl.when(me_r < tail_n)
    def _():
        copy = pltpu.make_async_copy(tsend2.at[me_r], trecv2.at[me_r], own_sem.at[3])
        copy.start()
        copy.wait()

    def weight_wait(buf, at, lo, size, index):
        weight_copy(buf, at, lo, size, index, me_t).wait_recv()

    weight_wait(w_a, dn_y, 0, whole, 0)
    weight_wait(w_b, dn_x, 0, whole, 2)
    forwards = []
    if ny > 2:
        weight_wait(w_a, up_y, 0, whole, 1)
        forwards.append(weight_copy(w_a, dn_y, 0, fill, 4, tensor_of(xi, up_y)))
        forwards.append(weight_copy(w_a, up_y, fill, fill, 5, tensor_of(xi, dn_y)))
    if nx > 2:
        weight_wait(w_b, up_x, 0, whole, 3)
        forwards.append(weight_copy(w_b, dn_x, 0, fill, 6, tensor_of(up_x, yi)))
        forwards.append(weight_copy(w_b, up_x, fill, fill, 7, tensor_of(dn_x, yi)))
    for copy in forwards:
        copy.start()

    def wait_second(rr):
        remote(send2.at[rr], recv2.at[rr], s2_send.at[rr], s2_recv.at[rr], rr, me_t).wait_recv()

        @pl.when(rr < tail_n)
        def _():
            remote(
                tsend2.at[0], trecv2.at[rr], t2_send.at[0], t2_recv.at[rr], rr, me_t
            ).wait_recv()

    own2.wait()
    each_replica(wait_second)

    lane_head = iota((1, width), 1) // HEAD_DIM
    saved = []
    for q in range(2):
        start_at = recv2[...].astype(F32)[:, q * piece : (q + 1) * piece, :]
        start_at = start_at.reshape(width, STATE)
        at8 = iota((8, STATE), 0)

        def tail_tile(part):
            tile = jnp.zeros((8, STATE), F32)
            for t in range(3):
                row = t * 4 + part
                at = q * tail_p + row % tail_p
                line = trecv2[row // tail_p, at : at + 1, :]
                tile = jnp.where(at8 == t, line, tile)
            return tile

        def tail_fix(tile, taps):
            total = tile * taps[0:1, :]
            rolled = jnp.where(at8 < 3, pltpu.roll(tile, 7, 0), 0.0)
            total = total + rolled * taps[1:2, :]
            rolled = jnp.where(at8 < 3, pltpu.roll(tile, 6, 0), 0.0)
            return total + rolled * taps[2:3, :]

        for part in range(2):
            lanes = slice(part * STATE, (part + 1) * STATE)
            xraw[q, 0:8, lanes] += tail_fix(tail_tile(part), convx_v[:, lanes])
            bcraw[q, 0:8, lanes] += tail_fix(tail_tile(part + 2), convbc_v[:, lanes])
        xc = silu(xraw[q])
        bcc = silu(bcraw[q])
        b_low = bcc[:, :STATE].astype(BF16)
        c_low = bcc[:, STATE:].astype(BF16)
        scores = dot_nt(c_low, b_low)
        y = expcum[q] * dot_nt(c_low, start_at.astype(BF16)) + skip_wide * xc
        for hp in range(heads // 2):
            left, right = 2 * hp, 2 * hp + 1
            mixing = jnp.concatenate([scores * decay[q, left], scores * decay[q, right]], axis=1)
            held = jnp.concatenate(
                [jnp.where(lane_head == left, xc, 0.0), jnp.where(lane_head == right, xc, 0.0)],
                axis=0,
            )
            y = y + jnp.dot(mixing.astype(BF16), held.astype(BF16), preferred_element_type=F32)
        v = y * gate[q]
        ss_send[:, q * slot : (q + 1) * slot] = dot_nt(jnp.ones((8, width), F32), v * v, HIGHEST)
        live = iota((slot, width), 0) < lengths_s[q]
        v = jnp.where(live, v * gain_v[...], 0.0)
        v_f[q] = v
        owners = slot // rows_owner // ny
        v_a[q * owners : (q + 1) * owners] = v.astype(BF16).reshape(owners, ny, rows_owner, width)
        saved.append((start_at, xc, b_low))

    def ss_copy(yy, cc):
        return remote(
            ss_send,
            ss_recv.at[ci, yi],
            ss_ssem.at[cc, yy],
            ss_rsem.at[ci, yi],
            zi * 2 + cc,
            tensor_of(xi, yy),
        )

    def va_copy(yy, cc):
        return remote(
            v_a.at[:, yy],
            r_a.at[ci, yi],
            va_send.at[cc, yy],
            va_recv.at[ci, yi],
            zi * 2 + cc,
            tensor_of(xi, yy),
        )

    for yy, cc in y_peers():
        ss_copy(yy, cc).start()
    for yy, cc in y_peers():
        va_copy(yy, cc).start()
    ss_recv[ci, yi] = ss_send[...]
    own_a = pltpu.make_async_copy(v_a.at[:, yi], r_a.at[ci, yi], own_sem.at[4])
    own_a.start()

    for q in range(2):
        start_at, xc, b_low = saved[q]
        weighed = (xc * weighin[q]).astype(BF16)
        final_o[q] = ending[q] * start_at + dot_tn(weighed, b_low)

    def ss_wait(yy, cc):
        remote(
            ss_send,
            ss_recv.at[cc, yy],
            ss_ssem.at[cc, yy],
            ss_rsem.at[cc, yy],
            zi * 2 + cc,
            tensor_of(xi, yy),
        ).wait_recv()

    for yy, cc in y_peers():
        ss_wait(yy, cc)
    scale_t = []
    for cc in range(2):
        total = ss_recv[cc, 0]
        for yy in range(1, ny):
            total = total + ss_recv[cc, yy]
        scale_t.append(lax.rsqrt(total / (ny * width) + EPSILON))
    mine = jnp.where(ci == 0, scale_t[0], scale_t[1])
    eye_t = (iota((tokens, tokens), 0) == iota((tokens, tokens), 1)).astype(F32)
    column = dot_nt(eye_t, mine, HIGHEST)
    for q in range(2):
        scaled = v_f[q] * column[q * slot : (q + 1) * slot, 0:1]
        v_b[q * owners : (q + 1) * owners] = scaled.astype(BF16).reshape(
            owners, ny, rows_owner, width
        )

    def vb_copy(xx, cc):
        return remote(
            v_b.at[xx],
            r_b.at[ci, xi],
            vb_send.at[cc, xx],
            vb_recv.at[ci, xi],
            zi * 2 + cc,
            tensor_of(xx, yi),
        )

    for xx, cc in x_peers():
        vb_copy(xx, cc).start()
    own_b = pltpu.make_async_copy(v_b.at[xi], r_b.at[ci, xi], own_sem.at[5])
    own_b.start()

    if ny > 2:
        opp_y = (yi + 2) % ny
        weight_wait(w_a, opp_y, 0, fill, 4)
        weight_wait(w_a, opp_y, fill, fill, 5)
    for yy, cc in y_peers():
        remote(
            v_a.at[:, yi],
            r_a.at[cc, yy],
            va_send.at[cc, yy],
            va_recv.at[cc, yy],
            zi * 2 + cc,
            tensor_of(xi, yy),
        ).wait_recv()
    own_a.wait()
    rows_a = 2 * nx * rows_owner
    acc = jnp.zeros((rows_a, quarter), F32)
    for yy in range(ny):
        lhs = r_a[:, yy].reshape(rows_a, width)
        acc = acc + jnp.dot(lhs, w_a[yy], preferred_element_type=F32)
    per = nx * rows_owner
    where_row = iota((per, tokens), 0)
    wanted = (where_row // rows_owner * ny + yi) * rows_owner + where_row % rows_owner
    pick_rows = (iota((per, tokens), 1) == wanted).astype(F32)
    for cc in range(2):
        col = dot_nt(pick_rows, scale_t[cc], HIGHEST)[:, 0:1]
        part = acc[cc * per : (cc + 1) * per, :] * col
        o_a[cc] = part.astype(BF16).reshape(nx, rows_owner, quarter)

    for xx, cc in x_peers():
        remote(
            o_a.at[cc, xx],
            ro_a.at[xi, ci],
            oa_send.at[xx, cc],
            oa_recv.at[xi, ci],
            zi * 2 + cc,
            tensor_of(xx, yi),
        ).start()
    own_oa = pltpu.make_async_copy(o_a.at[ci, xi], ro_a.at[xi, ci], own_sem.at[6])
    own_oa.start()

    if nx > 2:
        opp_x = (xi + 2) % nx
        weight_wait(w_b, opp_x, 0, fill, 6)
        weight_wait(w_b, opp_x, fill, fill, 7)
    for xx, cc in x_peers():
        remote(
            v_b.at[xi],
            r_b.at[cc, xx],
            vb_send.at[cc, xx],
            vb_recv.at[cc, xx],
            zi * 2 + cc,
            tensor_of(xx, yi),
        ).wait_recv()
    own_b.wait()
    rows_b = 2 * ny * rows_owner
    acc = jnp.zeros((rows_b, quarter), F32)
    for xx in range(nx):
        lhs = r_b[:, xx].reshape(rows_b, width)
        acc = acc + jnp.dot(lhs, w_b[xx], preferred_element_type=F32)
    o_b[...] = acc.astype(BF16).reshape(2, ny, rows_owner, quarter)
    for yy, cc in y_peers():
        remote(
            o_b.at[cc, yy],
            ro_b.at[yi, ci],
            ob_send.at[yy, cc],
            ob_recv.at[yi, ci],
            zi * 2 + cc,
            tensor_of(xi, yy),
        ).start()
    own_ob = pltpu.make_async_copy(o_b.at[ci, yi], ro_b.at[yi, ci], own_sem.at[7])
    own_ob.start()

    for xx, cc in x_peers():
        remote(
            o_a.at[cc, xx],
            ro_a.at[xx, cc],
            oa_send.at[xx, cc],
            oa_recv.at[xx, cc],
            zi * 2 + cc,
            tensor_of(xx, yi),
        ).wait_recv()
    own_oa.wait()
    for cc in range(2):
        total = ro_a[0, cc].astype(F32)
        for xx in range(1, nx):
            total = total + ro_a[xx, cc].astype(F32)
        mixed_o[:, cc * quarter : (cc + 1) * quarter] = total.astype(BF16)
    for yy, cc in y_peers():
        remote(
            o_b.at[cc, yy],
            ro_b.at[yy, cc],
            ob_send.at[yy, cc],
            ob_recv.at[yy, cc],
            zi * 2 + cc,
            tensor_of(xi, yy),
        ).wait_recv()
    own_ob.wait()
    for cc in range(2):
        total = ro_b[0, cc].astype(F32)
        for yy in range(1, ny):
            total = total + ro_b[yy, cc].astype(F32)
        lo = half_cols + cc * quarter
        mixed_o[:, lo : lo + quarter] = total.astype(BF16)

    def sent(rr):
        first_copy(rr).wait_send()
        remote(
            send2.at[rr], recv2.at[me_r], s2_send.at[rr], s2_recv.at[me_r], rr, me_t
        ).wait_send()

        @pl.when(rr < tail_n)
        def _():
            first_tail(rr).wait_send()

        @pl.when(me_r < tail_n)
        def _():
            remote(
                tsend2.at[rr], trecv2.at[me_r], t2_send.at[rr], t2_recv.at[me_r], rr, me_t
            ).wait_send()

    each_replica(sent)
    wa_up.wait_send()
    wb_up.wait_send()
    if ny > 2:
        wa_dn.wait_send()
    if nx > 2:
        wb_dn.wait_send()
    for copy in forwards:
        copy.wait_send()
    for yy, cc in y_peers():
        ss_copy(yy, cc).wait_send()
        va_copy(yy, cc).wait_send()
        remote(
            o_b.at[cc, yy],
            ro_b.at[yi, ci],
            ob_send.at[yy, cc],
            ob_recv.at[yi, ci],
            zi * 2 + cc,
            tensor_of(xi, yy),
        ).wait_send()
    for xx, cc in x_peers():
        vb_copy(xx, cc).wait_send()
        remote(
            o_a.at[cc, xx],
            ro_a.at[xi, ci],
            oa_send.at[xx, cc],
            oa_recv.at[xi, ci],
            zi * 2 + cc,
            tensor_of(xx, yi),
        ).wait_send()


def local(
    sizes,
    x_input,
    z_input,
    bc_input,
    dt_raw,
    dt_bias,
    decay_rates,
    skip_gain,
    conv_x,
    conv_bc,
    norm_gain,
    out_weight,
    cached_states,
    cached_tail_x,
    cached_tail_bc,
    prefix_block,
    lengths,
):
    nr, nx, ny = sizes
    tokens, width = x_input.shape
    heads = dt_raw.shape[1]
    slot = tokens // 2
    out_cols = out_weight.shape[1]
    quarter = out_cols // 4
    rows_owner = tokens // (nx * ny)
    piece = width // nr
    tail_n = min(nr, TAIL_ROWS)
    tail_p = TAIL_ROWS // tail_n
    vmem = pltpu.VMEM
    dma = pltpu.SemaphoreType.DMA
    smem_spec = pl.BlockSpec(memory_space=pltpu.SMEM)
    any_spec = pl.BlockSpec(memory_space=pl.ANY)
    vmem_spec = pl.BlockSpec(memory_space=pltpu.VMEM)
    scratch = [
        vmem((tokens, width), BF16),
        vmem((tokens, width), BF16),
        vmem((tokens, 2 * STATE), BF16),
        vmem((tokens, heads), F32),
        vmem((4, width), F32),
        vmem((4, 2 * STATE), F32),
        vmem((1, width), F32),
        vmem((2, width, STATE), F32),
        vmem((2, 3, width), F32),
        vmem((2, 3, 2 * STATE), F32),
        vmem((nr, 2 * piece, STATE), BF16),
        vmem((nr, 2 * piece, STATE), BF16),
        vmem((nr, 2 * piece, STATE), BF16),
        vmem((nr, 2 * piece, STATE), BF16),
        vmem((tail_n, 2 * tail_p, STATE), F32),
        vmem((nr, 2 * tail_p, STATE), F32),
        vmem((nr, 2 * tail_p, STATE), F32),
        vmem((tail_n, 2 * tail_p, STATE), F32),
        vmem((ny, width, quarter), BF16),
        vmem((nx, width, quarter), BF16),
        vmem((2, slot, width), F32),
        vmem((2, slot, 2 * STATE), F32),
        vmem((2, slot, width), F32),
        vmem((2, heads, slot, slot), F32),
        vmem((2, slot, width), F32),
        vmem((2, slot, width), F32),
        vmem((2, width, STATE), F32),
        vmem((2, slot, width), F32),
        vmem((nx, ny, rows_owner, width), BF16),
        vmem((nx, ny, rows_owner, width), BF16),
        vmem((2, ny, nx, rows_owner, width), BF16),
        vmem((2, nx, ny, rows_owner, width), BF16),
        vmem((8, tokens), F32),
        vmem((2, ny, 8, tokens), F32),
        vmem((2, nx, rows_owner, quarter), BF16),
        vmem((2, ny, rows_owner, quarter), BF16),
        vmem((nx, 2, rows_owner, quarter), BF16),
        vmem((ny, 2, rows_owner, quarter), BF16),
        dma((15,)),
        dma((8,)),
        dma((nr,)),
        dma((nr,)),
        dma((nr,)),
        dma((nr,)),
        dma((nr,)),
        dma((nr,)),
        dma((nr,)),
        dma((nr,)),
        dma((8,)),
        dma((8,)),
        dma((2, ny)),
        dma((2, ny)),
        dma((2, nx)),
        dma((2, nx)),
        dma((2, ny)),
        dma((2, ny)),
        dma((nx, 2)),
        dma((nx, 2)),
        dma((ny, 2)),
        dma((ny, 2)),
    ]
    mixed, final_states = pl.pallas_call(
        functools.partial(layer_kernel, sizes),
        out_shape=(
            jax.ShapeDtypeStruct((rows_owner, out_cols), BF16),
            jax.ShapeDtypeStruct((2, width, STATE), F32),
        ),
        in_specs=[smem_spec] * 5 + [any_spec] * 11,
        out_specs=(vmem_spec, vmem_spec),
        scratch_shapes=scratch,
        compiler_params=pltpu.CompilerParams(
            collective_id=0, has_side_effects=True, vmem_limit_bytes=56 * 1024 * 1024
        ),
        name="prefill_layer",
    )(
        prefix_block,
        lengths,
        dt_bias,
        decay_rates,
        skip_gain,
        x_input,
        z_input,
        bc_input,
        dt_raw,
        conv_x,
        conv_bc,
        norm_gain.reshape(1, width),
        out_weight,
        cached_states.reshape(2, width, STATE),
        cached_tail_x,
        cached_tail_bc,
    )
    return mixed, final_states.reshape(2, heads, HEAD_DIM, STATE)


def tensor_grid(count):
    side = 1
    while side * side < count:
        side *= 2
    return side, count // side


def solution(mesh):
    placed = (
        P("replica", "tensor"),
        P("replica", "tensor"),
        P("replica", None),
        P("replica", "tensor"),
        P("tensor"),
        P("tensor"),
        P("tensor"),
        P(None, "tensor"),
        P(),
        P("tensor"),
        P("tensor", None),
        P("replica", "tensor", None, None),
        P("replica", None, "tensor"),
        P("replica", None, None),
        P(),
        P("replica"),
    )
    sizes = (mesh.shape["replica"],) + tensor_grid(mesh.shape["tensor"])
    return jax.shard_map(
        functools.partial(local, sizes),
        mesh=mesh,
        in_specs=placed,
        out_specs=(P(("replica", "tensor"), None), P("replica", "tensor", None, None)),
        check_vma=False,
    )
```

```python
import functools

import jax
import jax.numpy as jnp
from jax import lax
from jax.experimental import pallas as pl
from jax.experimental.pallas import tpu as pltpu
from jax.sharding import PartitionSpec as P

MESH = pl.DeviceIdType.MESH
HIGHEST = lax.Precision.HIGHEST
F32 = jnp.float32
BF16 = jnp.bfloat16
HEAD_DIM = 32
STATE = 128
EPSILON = 1e-05
TAIL_ROWS = 12

NT_DIMS = (((1,), (1,)), ((), ()))
TN_DIMS = (((0,), (0,)), ((), ()))


def dot_nt(a, b, precision=None):
    return lax.dot_general(a, b, NT_DIMS, precision=precision, preferred_element_type=F32)


def dot_tn(a, b, precision=None):
    return lax.dot_general(a, b, TN_DIMS, precision=precision, preferred_element_type=F32)


def iota(shape, axis):
    return lax.broadcasted_iota(jnp.int32, shape, axis)


def silu(a):
    return a / (1.0 + jnp.exp(-a))


def layer_kernel(
    sizes,
    prefix_s,
    lengths_s,
    bias_s,
    rates_s,
    skip_s,
    x_h,
    z_h,
    bc_h,
    dt_h,
    convx_h,
    convbc_h,
    gain_h,
    weight_h,
    states_h,
    tailx_h,
    tailbc_h,
    mixed_o,
    final_o,
    x_v,
    z_v,
    bc_v,
    dt_v,
    convx_v,
    convbc_v,
    gain_v,
    st_v,
    tailx_v,
    tailbc_v,
    send1,
    recv1,
    send2,
    recv2,
    tsend1,
    trecv1,
    tsend2,
    trecv2,
    w_a,
    w_b,
    xraw,
    bcraw,
    gate,
    decay,
    expcum,
    weighin,
    ending,
    v_f,
    v_a,
    v_b,
    r_a,
    r_b,
    ss_send,
    ss_recv,
    o_a,
    o_b,
    ro_a,
    ro_b,
    load_sem,
    own_sem,
    s1_send,
    s1_recv,
    s2_send,
    s2_recv,
    t1_send,
    t1_recv,
    t2_send,
    t2_recv,
    w_send,
    w_recv,
    va_send,
    va_recv,
    vb_send,
    vb_recv,
    ss_ssem,
    ss_rsem,
    oa_send,
    oa_recv,
    ob_send,
    ob_recv,
):
    nr, nx, ny = sizes
    nz = nr // 2
    groups = nx
    tokens, width = x_v.shape
    heads = width // HEAD_DIM
    slot = tokens // 2
    rows_owner = tokens // (nx * ny)
    piece = width // nr
    tail_n = trecv2.shape[0]
    tail_p = TAIL_ROWS // tail_n
    quarter = w_a.shape[2]
    half_cols = 2 * quarter

    me_r = lax.axis_index("replica")
    me_t = lax.axis_index("tensor")
    zi, ci = me_r // 2, me_r % 2
    xi, yi = me_t // ny, me_t % ny

    def each_replica(fn):
        def step(m, carry):
            k = (m + 1) // 2
            dz = nz // 2 + k * (1 - 2 * (m % 2))
            zz = (zi + dz) % nz
            fn(zz * 2)
            fn(zz * 2 + 1)
            return carry

        lax.fori_loop(0, nz - 1, step, 0)
        fn(zi * 2 + 1 - ci)

    def y_peers():
        out = []
        for d in range(ny):
            for dc in range(2):
                if d or dc:
                    out.append(((yi + d) % ny, (ci + dc) % 2))
        return out

    def x_peers():
        out = []
        for d in range(nx):
            for dc in range(2):
                if d or dc:
                    out.append(((xi + d) % nx, (ci + dc) % 2))
        return out

    def tensor_of(xx, yy):
        return xx * ny + yy

    def remote(src, dst, ssem, rsem, rr, tt):
        return pltpu.make_async_remote_copy(
            src_ref=src,
            dst_ref=dst,
            send_sem=ssem,
            recv_sem=rsem,
            device_id=(rr, tt),
            device_id_type=MESH,
        )

    barrier = pltpu.get_barrier_semaphore()

    def greet(rr, tt):
        pl.semaphore_signal(barrier, inc=1, device_id=(rr, tt), device_id_type=MESH)

    each_replica(lambda rr: greet(rr, me_t))
    for d in range(1, ny):
        for cc in range(2):
            greet(zi * 2 + cc, tensor_of(xi, (yi + d) % ny))
    for d in range(1, nx):
        for cc in range(2):
            greet(zi * 2 + cc, tensor_of((xi + d) % nx, yi))
    expected = 2 * (nz - 1) + 1 + 2 * (ny - 1) + 2 * (nx - 1)

    b_lo = pl.multiple_of(xi * STATE, STATE)
    c_lo = pl.multiple_of((groups + xi) * STATE, STATE)
    cols_a = pl.ds(pl.multiple_of(ci * quarter, quarter), quarter)
    cols_b = pl.ds(pl.multiple_of(half_cols + ci * quarter, quarter), quarter)
    lane_b, lane_c = pl.ds(0, STATE), pl.ds(STATE, STATE)
    loads = []

    def load(src, dst):
        copy = pltpu.make_async_copy(src, dst, load_sem.at[len(loads)])
        copy.start()
        loads.append(copy)
        return copy

    load_states = load(states_h, st_v)
    load_tx = load(tailx_h, tailx_v)
    load_tb = load(tailbc_h.at[:, :, pl.ds(b_lo, STATE)], tailbc_v.at[:, :, lane_b])
    load_tc = load(tailbc_h.at[:, :, pl.ds(c_lo, STATE)], tailbc_v.at[:, :, lane_c])
    load_dt = load(dt_h, dt_v)
    load_x = load(x_h, x_v)
    load_b = load(bc_h.at[:, pl.ds(b_lo, STATE)], bc_v.at[:, lane_b])
    load_c = load(bc_h.at[:, pl.ds(c_lo, STATE)], bc_v.at[:, lane_c])
    load_cx = load(convx_h, convx_v)
    load_cb = load(convbc_h.at[:, pl.ds(b_lo, STATE)], convbc_v.at[:, lane_b])
    load_cc = load(convbc_h.at[:, pl.ds(c_lo, STATE)], convbc_v.at[:, lane_c])
    load_z = load(z_h, z_v)
    load_g = load(gain_h, gain_v)
    load_wa = load(weight_h.at[:, cols_a], w_a.at[yi])
    load_wb = load(weight_h.at[:, cols_b], w_b.at[xi])

    load_states.wait()
    packed = st_v[...].reshape(2, nr, piece, STATE)
    for b in range(2):
        send1[:, b * piece : (b + 1) * piece, :] = packed[b].astype(BF16)
    load_tx.wait()
    load_tb.wait()
    load_tc.wait()
    for row in range(TAIL_ROWS):
        t, part = row // 4, row % 4
        for b in range(2):
            src = tailx_v if part < 2 else tailbc_v
            lanes = slice((part % 2) * STATE, (part % 2 + 1) * STATE)
            at = b * tail_p + row % tail_p
            tsend1[row // tail_p, at : at + 1, :] = src[t, b : b + 1, lanes]

    pl.semaphore_wait(barrier, expected)

    def first_copy(rr):
        return remote(send1.at[rr], recv1.at[me_r], s1_send.at[rr], s1_recv.at[me_r], rr, me_t)

    def first_tail(rr):
        return remote(tsend1.at[rr], trecv1.at[me_r], t1_send.at[rr], t1_recv.at[me_r], rr, me_t)

    def start_first(rr):
        first_copy(rr).start()

        @pl.when(rr < tail_n)
        def _():
            first_tail(rr).start()

    each_replica(start_first)
    own1 = pltpu.make_async_copy(send1.at[me_r], recv1.at[me_r], own_sem.at[0])
    own1.start()

    @pl.when(me_r < tail_n)
    def _():
        copy = pltpu.make_async_copy(tsend1.at[me_r], trecv1.at[me_r], own_sem.at[1])
        copy.start()
        copy.wait()

    up_y, dn_y = (yi + 1) % ny, (yi + ny - 1) % ny
    up_x, dn_x = (xi + 1) % nx, (xi + nx - 1) % nx
    fill = w_a.shape[1] // 2

    def weight_copy(buf, at, lo, size, index, tt):
        ref = buf.at[at, pl.ds(lo, size), :]
        return remote(ref, ref, w_send.at[index], w_recv.at[index], me_r, tt)

    whole = 2 * fill
    load_wa.wait()
    load_wb.wait()
    wa_up = weight_copy(w_a, yi, 0, whole, 0, tensor_of(xi, up_y))
    wb_up = weight_copy(w_b, xi, 0, whole, 2, tensor_of(up_x, yi))
    wa_up.start()
    wb_up.start()
    if ny > 2:
        wa_dn = weight_copy(w_a, yi, 0, whole, 1, tensor_of(xi, dn_y))
        wa_dn.start()
    if nx > 2:
        wb_dn = weight_copy(w_b, xi, 0, whole, 3, tensor_of(dn_x, yi))
        wb_dn.start()

    load_dt.wait()
    head_row = iota((heads, 1), 0)
    head_lane = iota((1, heads), 1)
    bias_col = jnp.zeros((heads, 1), F32)
    rate_col = jnp.zeros((heads, 1), F32)
    skip_row = jnp.zeros((1, heads), F32)
    for h in range(heads):
        bias_col = jnp.where(head_row == h, bias_s[h], bias_col)
        rate_col = jnp.where(head_row == h, rates_s[h], rate_col)
        skip_row = jnp.where(head_lane == h, skip_s[h], skip_row)
    spread = (iota((heads, width), 1) // HEAD_DIM == iota((heads, width), 0)).astype(F32)
    row_i = iota((slot, slot), 0)
    col_i = iota((slot, slot), 1)
    causal = row_i >= col_i
    lower = causal.astype(F32)

    for q in range(2):
        raw = dt_v[:, q * slot : (q + 1) * slot] + bias_col
        soft = jnp.maximum(raw, 0.0) + jnp.log1p(jnp.exp(-jnp.abs(raw)))
        live = iota((heads, slot), 1) < lengths_s[q]
        dt_t = jnp.where(live, soft, 0.0)
        logdec = -dt_t * rate_col
        cum = dot_nt(lower, logdec, HIGHEST)
        cum_t = dot_nt(logdec, lower, HIGHEST)
        for h in range(heads):
            differ = cum[:, h : h + 1] - cum_t[h : h + 1, :]
            value = jnp.where(causal, jnp.exp(jnp.minimum(differ, 0.0)), 0.0)
            decay[q, h] = value * dt_t[h : h + 1, :]
        expcum[q] = dot_tn(jnp.exp(cum_t), spread, HIGHEST)
        last = cum_t[:, slot - 1 : slot]
        weighin[q] = dot_tn(jnp.exp(last - cum_t) * dt_t, spread, HIGHEST)
        ending[q] = dot_tn(spread, jnp.broadcast_to(jnp.exp(last), (heads, STATE)), HIGHEST)
    skip_wide = jnp.dot(skip_row, spread, precision=HIGHEST, preferred_element_type=F32)

    def raw_conv(seq, taps):
        total = seq * taps[3:4, :]
        at = iota(seq.shape, 0)
        for n in range(1, 4):
            moved = jnp.where(at >= n, pltpu.roll(seq, n, 0), 0.0)
            total = total + moved * taps[3 - n : 4 - n, :]
        return total

    load_x.wait()
    load_cx.wait()
    load_b.wait()
    load_c.wait()
    load_cb.wait()
    load_cc.wait()
    load_z.wait()
    for q in range(2):
        part = slice(q * slot, (q + 1) * slot)
        xraw[q] = raw_conv(x_v[part, :].astype(F32), convx_v[...])
        bcraw[q] = raw_conv(bc_v[part, :].astype(F32), convbc_v[...])
        gate[q] = silu(z_v[part, :].astype(F32))
    load_g.wait()

    def wait_first(rr):
        remote(send1.at[rr], recv1.at[rr], s1_send.at[rr], s1_recv.at[rr], rr, me_t).wait_recv()

        @pl.when(me_r < tail_n)
        def _():
            remote(
                tsend1.at[0], trecv1.at[rr], t1_send.at[0], t1_recv.at[rr], rr, me_t
            ).wait_recv()

    own1.wait()
    each_replica(wait_first)

    def pick(block):
        both = recv1[block // 2].astype(F32)
        return jnp.where(block % 2 == 1, both[piece:, :], both[:piece, :])

    def choose(rr, carry):
        first = pick(prefix_s[2 * rr])
        second = pick(prefix_s[2 * rr + 1])
        send2[rr] = jnp.concatenate([first, second], axis=0).astype(BF16)
        return carry

    lax.fori_loop(0, nr, choose, 0)

    @pl.when(me_r < tail_n)
    def _():
        def choose_tail(rr, carry):
            for s in range(2):
                block = prefix_s[2 * rr + s]
                both = trecv1[block // 2]
                tsend2[rr, s * tail_p : (s + 1) * tail_p, :] = jnp.where(
                    block % 2 == 1, both[tail_p:, :], both[:tail_p, :]
                )
            return carry

        lax.fori_loop(0, nr, choose_tail, 0)

    def start_second(rr):
        remote(
            send2.at[rr], recv2.at[me_r], s2_send.at[rr], s2_recv.at[me_r], rr, me_t
        ).start()

        @pl.when(me_r < tail_n)
        def _():
            remote(
                tsend2.at[rr], trecv2.at[me_r], t2_send.at[rr], t2_recv.at[me_r], rr, me_t
            ).start()

    each_replica(start_second)
    own2 = pltpu.make_async_copy(send2.at[me_r], recv2.at[me_r], own_sem.at[2])
    own2.start()

    @pl.when(me_r < tail_n)
    def _():
        copy = pltpu.make_async_copy(tsend2.at[me_r], trecv2.at[me_r], own_sem.at[3])
        copy.start()
        copy.wait()

    def weight_wait(buf, at, lo, size, index):
        weight_copy(buf, at, lo, size, index, me_t).wait_recv()

    weight_wait(w_a, dn_y, 0, whole, 0)
    weight_wait(w_b, dn_x, 0, whole, 2)
    forwards = []
    if ny > 2:
        weight_wait(w_a, up_y, 0, whole, 1)
        forwards.append(weight_copy(w_a, dn_y, 0, fill, 4, tensor_of(xi, up_y)))
        forwards.append(weight_copy(w_a, up_y, fill, fill, 5, tensor_of(xi, dn_y)))
    if nx > 2:
        weight_wait(w_b, up_x, 0, whole, 3)
        forwards.append(weight_copy(w_b, dn_x, 0, fill, 6, tensor_of(up_x, yi)))
        forwards.append(weight_copy(w_b, up_x, fill, fill, 7, tensor_of(dn_x, yi)))
    for copy in forwards:
        copy.start()

    def wait_second(rr):
        remote(send2.at[rr], recv2.at[rr], s2_send.at[rr], s2_recv.at[rr], rr, me_t).wait_recv()

        @pl.when(rr < tail_n)
        def _():
            remote(
                tsend2.at[0], trecv2.at[rr], t2_send.at[0], t2_recv.at[rr], rr, me_t
            ).wait_recv()

    own2.wait()
    each_replica(wait_second)

    lane_head = iota((1, width), 1) // HEAD_DIM
    saved = []
    for q in range(2):
        start_at = recv2[...].astype(F32)[:, q * piece : (q + 1) * piece, :]
        start_at = start_at.reshape(width, STATE)
        at8 = iota((8, STATE), 0)

        def tail_tile(part):
            tile = jnp.zeros((8, STATE), F32)
            for t in range(3):
                row = t * 4 + part
                at = q * tail_p + row % tail_p
                line = trecv2[row // tail_p, at : at + 1, :]
                tile = jnp.where(at8 == t, line, tile)
            return tile

        def tail_fix(tile, taps):
            total = tile * taps[0:1, :]
            rolled = jnp.where(at8 < 3, pltpu.roll(tile, 7, 0), 0.0)
            total = total + rolled * taps[1:2, :]
            rolled = jnp.where(at8 < 3, pltpu.roll(tile, 6, 0), 0.0)
            return total + rolled * taps[2:3, :]

        for part in range(2):
            lanes = slice(part * STATE, (part + 1) * STATE)
            xraw[q, 0:8, lanes] += tail_fix(tail_tile(part), convx_v[:, lanes])
            bcraw[q, 0:8, lanes] += tail_fix(tail_tile(part + 2), convbc_v[:, lanes])
        xc = silu(xraw[q])
        bcc = silu(bcraw[q])
        b_low = bcc[:, :STATE].astype(BF16)
        c_low = bcc[:, STATE:].astype(BF16)
        scores = dot_nt(c_low, b_low)
        y = expcum[q] * dot_nt(c_low, start_at.astype(BF16)) + skip_wide * xc
        for hp in range(heads // 2):
            left, right = 2 * hp, 2 * hp + 1
            mixing = jnp.concatenate([scores * decay[q, left], scores * decay[q, right]], axis=1)
            held = jnp.concatenate(
                [jnp.where(lane_head == left, xc, 0.0), jnp.where(lane_head == right, xc, 0.0)],
                axis=0,
            )
            y = y + jnp.dot(mixing.astype(BF16), held.astype(BF16), preferred_element_type=F32)
        v = y * gate[q]
        ss_send[:, q * slot : (q + 1) * slot] = dot_nt(jnp.ones((8, width), F32), v * v, HIGHEST)
        live = iota((slot, width), 0) < lengths_s[q]
        v = jnp.where(live, v * gain_v[...], 0.0)
        v_f[q] = v
        owners = slot // rows_owner // ny
        v_a[q * owners : (q + 1) * owners] = v.astype(BF16).reshape(owners, ny, rows_owner, width)
        saved.append((start_at, xc, b_low))

    def ss_copy(yy, cc):
        return remote(
            ss_send,
            ss_recv.at[ci, yi],
            ss_ssem.at[cc, yy],
            ss_rsem.at[ci, yi],
            zi * 2 + cc,
            tensor_of(xi, yy),
        )

    def va_copy(yy, cc):
        return remote(
            v_a.at[:, yy],
            r_a.at[ci, yi],
            va_send.at[cc, yy],
            va_recv.at[ci, yi],
            zi * 2 + cc,
            tensor_of(xi, yy),
        )

    for yy, cc in y_peers():
        ss_copy(yy, cc).start()
    for yy, cc in y_peers():
        va_copy(yy, cc).start()
    ss_recv[ci, yi] = ss_send[...]
    own_a = pltpu.make_async_copy(v_a.at[:, yi], r_a.at[ci, yi], own_sem.at[4])
    own_a.start()

    for q in range(2):
        start_at, xc, b_low = saved[q]
        weighed = (xc * weighin[q]).astype(BF16)
        final_o[q] = ending[q] * start_at + dot_tn(weighed, b_low)

    def ss_wait(yy, cc):
        remote(
            ss_send,
            ss_recv.at[cc, yy],
            ss_ssem.at[cc, yy],
            ss_rsem.at[cc, yy],
            zi * 2 + cc,
            tensor_of(xi, yy),
        ).wait_recv()

    for yy, cc in y_peers():
        ss_wait(yy, cc)
    scale_t = []
    for cc in range(2):
        total = ss_recv[cc, 0]
        for yy in range(1, ny):
            total = total + ss_recv[cc, yy]
        scale_t.append(lax.rsqrt(total / (ny * width) + EPSILON))
    mine = jnp.where(ci == 0, scale_t[0], scale_t[1])
    eye_t = (iota((tokens, tokens), 0) == iota((tokens, tokens), 1)).astype(F32)
    column = dot_nt(eye_t, mine, HIGHEST)
    for q in range(2):
        scaled = v_f[q] * column[q * slot : (q + 1) * slot, 0:1]
        v_b[q * owners : (q + 1) * owners] = scaled.astype(BF16).reshape(
            owners, ny, rows_owner, width
        )

    def vb_copy(xx, cc):
        return remote(
            v_b.at[xx],
            r_b.at[ci, xi],
            vb_send.at[cc, xx],
            vb_recv.at[ci, xi],
            zi * 2 + cc,
            tensor_of(xx, yi),
        )

    for xx, cc in x_peers():
        vb_copy(xx, cc).start()
    own_b = pltpu.make_async_copy(v_b.at[xi], r_b.at[ci, xi], own_sem.at[5])
    own_b.start()

    if ny > 2:
        opp_y = (yi + 2) % ny
        weight_wait(w_a, opp_y, 0, fill, 4)
        weight_wait(w_a, opp_y, fill, fill, 5)
    for yy, cc in y_peers():
        remote(
            v_a.at[:, yi],
            r_a.at[cc, yy],
            va_send.at[cc, yy],
            va_recv.at[cc, yy],
            zi * 2 + cc,
            tensor_of(xi, yy),
        ).wait_recv()
    own_a.wait()
    rows_a = 2 * nx * rows_owner
    acc = jnp.zeros((rows_a, quarter), F32)
    for yy in range(ny):
        lhs = r_a[:, yy].reshape(rows_a, width)
        acc = acc + jnp.dot(lhs, w_a[yy], preferred_element_type=F32)
    per = nx * rows_owner
    where_row = iota((per, tokens), 0)
    wanted = (where_row // rows_owner * ny + yi) * rows_owner + where_row % rows_owner
    pick_rows = (iota((per, tokens), 1) == wanted).astype(F32)
    for cc in range(2):
        col = dot_nt(pick_rows, scale_t[cc], HIGHEST)[:, 0:1]
        part = acc[cc * per : (cc + 1) * per, :] * col
        o_a[cc] = part.astype(BF16).reshape(nx, rows_owner, quarter)

    for xx, cc in x_peers():
        remote(
            o_a.at[cc, xx],
            ro_a.at[xi, ci],
            oa_send.at[xx, cc],
            oa_recv.at[xi, ci],
            zi * 2 + cc,
            tensor_of(xx, yi),
        ).start()
    own_oa = pltpu.make_async_copy(o_a.at[ci, xi], ro_a.at[xi, ci], own_sem.at[6])
    own_oa.start()

    if nx > 2:
        opp_x = (xi + 2) % nx
        weight_wait(w_b, opp_x, 0, fill, 6)
        weight_wait(w_b, opp_x, fill, fill, 7)
    for xx, cc in x_peers():
        remote(
            v_b.at[xi],
            r_b.at[cc, xx],
            vb_send.at[cc, xx],
            vb_recv.at[cc, xx],
            zi * 2 + cc,
            tensor_of(xx, yi),
        ).wait_recv()
    own_b.wait()
    rows_b = 2 * ny * rows_owner
    acc = jnp.zeros((rows_b, quarter), F32)
    for xx in range(nx):
        lhs = r_b[:, xx].reshape(rows_b, width)
        acc = acc + jnp.dot(lhs, w_b[xx], preferred_element_type=F32)
    o_b[...] = acc.astype(BF16).reshape(2, ny, rows_owner, quarter)
    for yy, cc in y_peers():
        remote(
            o_b.at[cc, yy],
            ro_b.at[yi, ci],
            ob_send.at[yy, cc],
            ob_recv.at[yi, ci],
            zi * 2 + cc,
            tensor_of(xi, yy),
        ).start()
    own_ob = pltpu.make_async_copy(o_b.at[ci, yi], ro_b.at[yi, ci], own_sem.at[7])
    own_ob.start()

    for xx, cc in x_peers():
        remote(
            o_a.at[cc, xx],
            ro_a.at[xx, cc],
            oa_send.at[xx, cc],
            oa_recv.at[xx, cc],
            zi * 2 + cc,
            tensor_of(xx, yi),
        ).wait_recv()
    own_oa.wait()
    for cc in range(2):
        total = ro_a[0, cc].astype(F32)
        for xx in range(1, nx):
            total = total + ro_a[xx, cc].astype(F32)
        mixed_o[:, cc * quarter : (cc + 1) * quarter] = total.astype(BF16)
    for yy, cc in y_peers():
        remote(
            o_b.at[cc, yy],
            ro_b.at[yy, cc],
            ob_send.at[yy, cc],
            ob_recv.at[yy, cc],
            zi * 2 + cc,
            tensor_of(xi, yy),
        ).wait_recv()
    own_ob.wait()
    for cc in range(2):
        total = ro_b[0, cc].astype(F32)
        for yy in range(1, ny):
            total = total + ro_b[yy, cc].astype(F32)
        lo = half_cols + cc * quarter
        mixed_o[:, lo : lo + quarter] = total.astype(BF16)

    def sent(rr):
        first_copy(rr).wait_send()
        remote(
            send2.at[rr], recv2.at[me_r], s2_send.at[rr], s2_recv.at[me_r], rr, me_t
        ).wait_send()

        @pl.when(rr < tail_n)
        def _():
            first_tail(rr).wait_send()

        @pl.when(me_r < tail_n)
        def _():
            remote(
                tsend2.at[rr], trecv2.at[me_r], t2_send.at[rr], t2_recv.at[me_r], rr, me_t
            ).wait_send()

    each_replica(sent)
    wa_up.wait_send()
    wb_up.wait_send()
    if ny > 2:
        wa_dn.wait_send()
    if nx > 2:
        wb_dn.wait_send()
    for copy in forwards:
        copy.wait_send()
    for yy, cc in y_peers():
        ss_copy(yy, cc).wait_send()
        va_copy(yy, cc).wait_send()
        remote(
            o_b.at[cc, yy],
            ro_b.at[yi, ci],
            ob_send.at[yy, cc],
            ob_recv.at[yi, ci],
            zi * 2 + cc,
            tensor_of(xi, yy),
        ).wait_send()
    for xx, cc in x_peers():
        vb_copy(xx, cc).wait_send()
        remote(
            o_a.at[cc, xx],
            ro_a.at[xi, ci],
            oa_send.at[xx, cc],
            oa_recv.at[xi, ci],
            zi * 2 + cc,
            tensor_of(xx, yi),
        ).wait_send()


def store_kernel(mixed_v, final_v, mixed_o, final_o, sem):
    first = pltpu.make_async_copy(mixed_v, mixed_o, sem.at[0])
    second = pltpu.make_async_copy(final_v, final_o, sem.at[1])
    first.start()
    second.start()
    first.wait()
    second.wait()


def local(
    sizes,
    x_input,
    z_input,
    bc_input,
    dt_raw,
    dt_bias,
    decay_rates,
    skip_gain,
    conv_x,
    conv_bc,
    norm_gain,
    out_weight,
    cached_states,
    cached_tail_x,
    cached_tail_bc,
    prefix_block,
    lengths,
):
    nr, nx, ny = sizes
    tokens, width = x_input.shape
    heads = dt_raw.shape[1]
    slot = tokens // 2
    out_cols = out_weight.shape[1]
    quarter = out_cols // 4
    rows_owner = tokens // (nx * ny)
    piece = width // nr
    tail_n = min(nr, TAIL_ROWS)
    tail_p = TAIL_ROWS // tail_n
    vmem = pltpu.VMEM
    dma = pltpu.SemaphoreType.DMA
    smem_spec = pl.BlockSpec(memory_space=pltpu.SMEM)
    hbm_spec = pl.BlockSpec(memory_space=pl.ANY)
    vmem_spec = pl.BlockSpec(memory_space=pltpu.VMEM)
    scratch = [
        vmem((tokens, width), BF16),
        vmem((tokens, width), BF16),
        vmem((tokens, 2 * STATE), BF16),
        vmem((heads, tokens), F32),
        vmem((4, width), F32),
        vmem((4, 2 * STATE), F32),
        vmem((1, width), F32),
        vmem((2, width, STATE), F32),
        vmem((3, 2, width), F32),
        vmem((3, 2, 2 * STATE), F32),
        vmem((nr, 2 * piece, STATE), BF16),
        vmem((nr, 2 * piece, STATE), BF16),
        vmem((nr, 2 * piece, STATE), BF16),
        vmem((nr, 2 * piece, STATE), BF16),
        vmem((tail_n, 2 * tail_p, STATE), F32),
        vmem((nr, 2 * tail_p, STATE), F32),
        vmem((nr, 2 * tail_p, STATE), F32),
        vmem((tail_n, 2 * tail_p, STATE), F32),
        vmem((ny, width, quarter), BF16),
        vmem((nx, width, quarter), BF16),
        vmem((2, slot, width), F32),
        vmem((2, slot, 2 * STATE), F32),
        vmem((2, slot, width), F32),
        vmem((2, heads, slot, slot), F32),
        vmem((2, slot, width), F32),
        vmem((2, slot, width), F32),
        vmem((2, width, STATE), F32),
        vmem((2, slot, width), F32),
        vmem((nx, ny, rows_owner, width), BF16),
        vmem((nx, ny, rows_owner, width), BF16),
        vmem((2, ny, nx, rows_owner, width), BF16),
        vmem((2, nx, ny, rows_owner, width), BF16),
        vmem((8, tokens), F32),
        vmem((2, ny, 8, tokens), F32),
        vmem((2, nx, rows_owner, quarter), BF16),
        vmem((2, ny, rows_owner, quarter), BF16),
        vmem((nx, 2, rows_owner, quarter), BF16),
        vmem((ny, 2, rows_owner, quarter), BF16),
        dma((15,)),
        dma((8,)),
        dma((nr,)),
        dma((nr,)),
        dma((nr,)),
        dma((nr,)),
        dma((nr,)),
        dma((nr,)),
        dma((nr,)),
        dma((nr,)),
        dma((8,)),
        dma((8,)),
        dma((2, ny)),
        dma((2, ny)),
        dma((2, nx)),
        dma((2, nx)),
        dma((2, ny)),
        dma((2, ny)),
        dma((nx, 2)),
        dma((nx, 2)),
        dma((ny, 2)),
        dma((ny, 2)),
    ]
    mixed, final_states = pl.pallas_call(
        functools.partial(layer_kernel, sizes),
        out_shape=(vmem((rows_owner, out_cols), BF16), vmem((2, width, STATE), F32)),
        in_specs=[smem_spec] * 5 + [hbm_spec] * 11,
        out_specs=(vmem_spec, vmem_spec),
        scratch_shapes=scratch,
        compiler_params=pltpu.CompilerParams(
            collective_id=0, has_side_effects=True, vmem_limit_bytes=56 * 1024 * 1024
        ),
        name="prefill_layer",
    )(
        prefix_block,
        lengths,
        dt_bias,
        decay_rates,
        skip_gain,
        x_input,
        z_input,
        bc_input,
        dt_raw.T,
        conv_x,
        conv_bc,
        norm_gain.reshape(1, width),
        out_weight,
        cached_states.reshape(2, width, STATE),
        jnp.transpose(cached_tail_x, (1, 0, 2)),
        jnp.transpose(cached_tail_bc, (1, 0, 2)),
    )
    mixed, final_states = pl.pallas_call(
        store_kernel,
        out_shape=(
            jax.ShapeDtypeStruct((rows_owner, out_cols), BF16),
            jax.ShapeDtypeStruct((2, width, STATE), F32),
        ),
        in_specs=[vmem_spec] * 2,
        out_specs=(hbm_spec, hbm_spec),
        scratch_shapes=[dma((2,))],
        compiler_params=pltpu.CompilerParams(vmem_limit_bytes=4 * 1024 * 1024),
        name="store_results",
    )(mixed, final_states)
    return mixed, final_states.reshape(2, heads, HEAD_DIM, STATE)


def tensor_grid(count):
    side = 1
    while side * side < count:
        side *= 2
    return side, count // side


def solution(mesh):
    placed = (
        P("replica", "tensor"),
        P("replica", "tensor"),
        P("replica", None),
        P("replica", "tensor"),
        P("tensor"),
        P("tensor"),
        P("tensor"),
        P(None, "tensor"),
        P(),
        P("tensor"),
        P("tensor", None),
        P("replica", "tensor", None, None),
        P("replica", None, "tensor"),
        P("replica", None, None),
        P(),
        P("replica"),
    )
    sizes = (mesh.shape["replica"],) + tensor_grid(mesh.shape["tensor"])
    return jax.shard_map(
        functools.partial(local, sizes),
        mesh=mesh,
        in_specs=placed,
        out_specs=(P(("replica", "tensor"), None), P("replica", "tensor", None, None)),
        check_vma=False,
    )
```

```python
import functools

import jax
import jax.numpy as jnp
from jax import lax
from jax.experimental import pallas as pl
from jax.experimental.pallas import tpu as pltpu
from jax.sharding import PartitionSpec as P

MESH = pl.DeviceIdType.MESH
HIGHEST = lax.Precision.HIGHEST
F32 = jnp.float32
BF16 = jnp.bfloat16
HEAD_DIM = 32
STATE = 128
EPSILON = 1e-05
TAIL_ROWS = 12

NT_DIMS = (((1,), (1,)), ((), ()))
TN_DIMS = (((0,), (0,)), ((), ()))


def dot_nt(a, b, precision=None):
    return lax.dot_general(a, b, NT_DIMS, precision=precision, preferred_element_type=F32)


def dot_tn(a, b, precision=None):
    return lax.dot_general(a, b, TN_DIMS, precision=precision, preferred_element_type=F32)


def iota(shape, axis):
    return lax.broadcasted_iota(jnp.int32, shape, axis)


def silu(a):
    return a / (1.0 + jnp.exp(-a))


def layer_kernel(
    sizes,
    prefix_s,
    lengths_s,
    bias_s,
    rates_s,
    skip_s,
    x_h,
    z_h,
    bc_h,
    dt_h,
    convx_h,
    convbc_h,
    gain_h,
    weight_h,
    states_h,
    tailx_h,
    tailbc_h,
    mixed_o,
    final_o,
    x_v,
    z_v,
    bc_v,
    dt_v,
    convx_v,
    convbc_v,
    gain_v,
    st_v,
    tailx_v,
    tailbc_v,
    send1,
    recv1,
    send2,
    recv2,
    tsend1,
    trecv1,
    tsend2,
    trecv2,
    w_a,
    w_b,
    xraw,
    bcraw,
    gate,
    decay,
    expcum,
    weighin,
    ending,
    v_a,
    r_a,
    r_b,
    ss_send,
    ss_recv,
    o_a,
    o_b,
    ro_a,
    ro_b,
    load_sem,
    own_sem,
    s1_send,
    s1_recv,
    s2_send,
    s2_recv,
    t1_send,
    t1_recv,
    t2_send,
    t2_recv,
    w_send,
    w_recv,
    va_send,
    va_recv,
    vb_send,
    vb_recv,
    ss_ssem,
    ss_rsem,
    oa_send,
    oa_recv,
    ob_send,
    ob_recv,
):
    nr, nx, ny = sizes
    nz = nr // 2
    groups = nx
    tokens, width = x_v.shape
    heads = width // HEAD_DIM
    slot = tokens // 2
    rows_owner = tokens // (nx * ny)
    piece = width // nr
    tail_n = trecv2.shape[0]
    tail_p = TAIL_ROWS // tail_n
    quarter = w_a.shape[2]
    half_cols = 2 * quarter

    me_r = lax.axis_index("replica")
    me_t = lax.axis_index("tensor")
    zi, ci = me_r // 2, me_r % 2
    xi, yi = me_t // ny, me_t % ny

    def far_pair(m):
        k = (m + 1) // 2
        dz = nz // 2 + k * (1 - 2 * (m % 2))
        return (zi + dz) % nz * 2

    def each_replica(fn):
        def step(m, carry):
            base = far_pair(m)
            fn(base)
            fn(base + 1)
            return carry

        lax.fori_loop(0, nz - 1, step, 0)
        fn(zi * 2 + 1 - ci)

    def y_peers():
        out = []
        for d in range(ny):
            for dc in range(2):
                if d or dc:
                    out.append(((yi + d) % ny, (ci + dc) % 2))
        return out

    def x_peers():
        out = []
        for d in range(nx):
            for dc in range(2):
                if d or dc:
                    out.append(((xi + d) % nx, (ci + dc) % 2))
        return out

    def grid_peers():
        out = []
        for dx in range(nx):
            for dy in range(ny):
                for cc in range(2):
                    if dx or dy:
                        out.append(((xi + dx) % nx, (yi + dy) % ny, cc))
        return out

    def tensor_of(xx, yy):
        return xx * ny + yy

    def remote(src, dst, ssem, rsem, rr, tt):
        return pltpu.make_async_remote_copy(
            src_ref=src,
            dst_ref=dst,
            send_sem=ssem,
            recv_sem=rsem,
            device_id=(rr, tt),
            device_id_type=MESH,
        )

    barrier = pltpu.get_barrier_semaphore()

    def greet(rr, tt):
        pl.semaphore_signal(barrier, inc=1, device_id=(rr, tt), device_id_type=MESH)

    each_replica(lambda rr: greet(rr, me_t))
    for xx, yy, cc in grid_peers():
        greet(zi * 2 + cc, tensor_of(xx, yy))
    expected = 2 * (nz - 1) + 1 + 2 * (nx * ny - 1)

    b_lo = pl.multiple_of(xi * STATE, STATE)
    c_lo = pl.multiple_of((groups + xi) * STATE, STATE)
    cols_a = pl.ds(pl.multiple_of(ci * quarter, quarter), quarter)
    cols_b = pl.ds(pl.multiple_of(half_cols + ci * quarter, quarter), quarter)
    lane_b, lane_c = pl.ds(0, STATE), pl.ds(STATE, STATE)
    loads = []

    def load(src, dst):
        copy = pltpu.make_async_copy(src, dst, load_sem.at[len(loads)])
        copy.start()
        loads.append(copy)
        return copy

    load_states = load(states_h, st_v)
    load_tx = load(tailx_h, tailx_v)
    load_tb = load(tailbc_h.at[:, :, pl.ds(b_lo, STATE)], tailbc_v.at[:, :, lane_b])
    load_tc = load(tailbc_h.at[:, :, pl.ds(c_lo, STATE)], tailbc_v.at[:, :, lane_c])
    load_dt = load(dt_h, dt_v)
    load_x = load(x_h, x_v)
    load_b = load(bc_h.at[:, pl.ds(b_lo, STATE)], bc_v.at[:, lane_b])
    load_c = load(bc_h.at[:, pl.ds(c_lo, STATE)], bc_v.at[:, lane_c])
    load_cx = load(convx_h, convx_v)
    load_cb = load(convbc_h.at[:, pl.ds(b_lo, STATE)], convbc_v.at[:, lane_b])
    load_cc = load(convbc_h.at[:, pl.ds(c_lo, STATE)], convbc_v.at[:, lane_c])
    load_z = load(z_h, z_v)
    load_g = load(gain_h, gain_v)
    load_wa = load(weight_h.at[:, cols_a], w_a.at[yi])
    load_wb = load(weight_h.at[:, cols_b], w_b.at[xi])

    load_states.wait()
    packed = st_v[...].reshape(2, nr, piece, STATE)
    for b in range(2):
        send1[:, b * piece : (b + 1) * piece, :] = packed[b].astype(BF16)
    load_tx.wait()
    load_tb.wait()
    load_tc.wait()
    for row in range(TAIL_ROWS):
        t, part = row // 4, row % 4
        for b in range(2):
            src = tailx_v if part < 2 else tailbc_v
            lanes = slice((part % 2) * STATE, (part % 2 + 1) * STATE)
            at = b * tail_p + row % tail_p
            tsend1[row // tail_p, at : at + 1, :] = src[t, b : b + 1, lanes]

    pl.semaphore_wait(barrier, expected)

    def first_copy(rr):
        return remote(send1.at[rr], recv1.at[me_r], s1_send.at[rr], s1_recv.at[me_r], rr, me_t)

    def first_tail(rr):
        return remote(tsend1.at[rr], trecv1.at[me_r], t1_send.at[rr], t1_recv.at[me_r], rr, me_t)

    def start_first(rr):
        first_copy(rr).start()

        @pl.when(rr < tail_n)
        def _():
            first_tail(rr).start()

    each_replica(start_first)
    own1 = pltpu.make_async_copy(send1.at[me_r], recv1.at[me_r], own_sem.at[0])
    own1.start()

    @pl.when(me_r < tail_n)
    def _():
        copy = pltpu.make_async_copy(tsend1.at[me_r], trecv1.at[me_r], own_sem.at[1])
        copy.start()
        copy.wait()

    up_y, dn_y = (yi + 1) % ny, (yi + ny - 1) % ny
    up_x, dn_x = (xi + 1) % nx, (xi + nx - 1) % nx
    fill = w_a.shape[1] // 2

    def weight_copy(buf, at, lo, size, index, tt):
        ref = buf.at[at, pl.ds(lo, size), :]
        return remote(ref, ref, w_send.at[index], w_recv.at[index], me_r, tt)

    load_wa.wait()
    load_wb.wait()
    started = []

    def weight_start(copy):
        copy.start()
        started.append(copy)

    lows = (0, fill)
    for turn in range(2):
        lo, hi = lows[turn], lows[1 - turn]
        weight_start(weight_copy(w_a, yi, lo, fill, turn, tensor_of(xi, up_y)))
        weight_start(weight_copy(w_b, xi, lo, fill, 4 + turn, tensor_of(up_x, yi)))
        if ny > 2:
            weight_start(weight_copy(w_a, yi, hi, fill, 2 + turn, tensor_of(xi, dn_y)))
        if nx > 2:
            weight_start(weight_copy(w_b, xi, hi, fill, 6 + turn, tensor_of(dn_x, yi)))

    load_dt.wait()
    head_row = iota((heads, 1), 0)
    head_lane = iota((1, heads), 1)
    bias_col = jnp.zeros((heads, 1), F32)
    rate_col = jnp.zeros((heads, 1), F32)
    skip_row = jnp.zeros((1, heads), F32)
    for h in range(heads):
        bias_col = jnp.where(head_row == h, bias_s[h], bias_col)
        rate_col = jnp.where(head_row == h, rates_s[h], rate_col)
        skip_row = jnp.where(head_lane == h, skip_s[h], skip_row)
    spread = (iota((heads, width), 1) // HEAD_DIM == iota((heads, width), 0)).astype(F32)
    row_i = iota((slot, slot), 0)
    col_i = iota((slot, slot), 1)
    causal = row_i >= col_i
    lower = causal.astype(F32)

    for q in range(2):
        raw = dt_v[:, q * slot : (q + 1) * slot] + bias_col
        soft = jnp.maximum(raw, 0.0) + jnp.log1p(jnp.exp(-jnp.abs(raw)))
        live = iota((heads, slot), 1) < lengths_s[q]
        dt_t = jnp.where(live, soft, 0.0)
        logdec = -dt_t * rate_col
        cum = dot_nt(lower, logdec, HIGHEST)
        cum_t = dot_nt(logdec, lower, HIGHEST)
        for h in range(heads):
            differ = cum[:, h : h + 1] - cum_t[h : h + 1, :]
            value = jnp.where(causal, jnp.exp(jnp.minimum(differ, 0.0)), 0.0)
            decay[q, h] = value * dt_t[h : h + 1, :]
        expcum[q] = dot_tn(jnp.exp(cum_t), spread, HIGHEST)
        last = cum_t[:, slot - 1 : slot]
        weighin[q] = dot_tn(jnp.exp(last - cum_t) * dt_t, spread, HIGHEST)
        ending[q] = dot_tn(spread, jnp.broadcast_to(jnp.exp(last), (heads, STATE)), HIGHEST)
    skip_wide = jnp.dot(skip_row, spread, precision=HIGHEST, preferred_element_type=F32)

    def raw_conv(seq, taps):
        total = seq * taps[3:4, :]
        at = iota(seq.shape, 0)
        for n in range(1, 4):
            moved = jnp.where(at >= n, pltpu.roll(seq, n, 0), 0.0)
            total = total + moved * taps[3 - n : 4 - n, :]
        return total

    load_x.wait()
    load_cx.wait()
    load_b.wait()
    load_c.wait()
    load_cb.wait()
    load_cc.wait()
    load_z.wait()
    for q in range(2):
        part = slice(q * slot, (q + 1) * slot)
        xraw[q] = raw_conv(x_v[part, :].astype(F32), convx_v[...])
        bcraw[q] = raw_conv(bc_v[part, :].astype(F32), convbc_v[...])
        gate[q] = silu(z_v[part, :].astype(F32))
    load_g.wait()

    def wait_first(rr):
        remote(send1.at[rr], recv1.at[rr], s1_send.at[rr], s1_recv.at[rr], rr, me_t).wait_recv()

        @pl.when(me_r < tail_n)
        def _():
            remote(
                tsend1.at[0], trecv1.at[rr], t1_send.at[0], t1_recv.at[rr], rr, me_t
            ).wait_recv()

    own1.wait()
    each_replica(wait_first)

    def pick(block):
        both = recv1[block // 2].astype(F32)
        return jnp.where(block % 2 == 1, both[piece:, :], both[:piece, :])

    def choose(rr):
        first = pick(prefix_s[2 * rr])
        second = pick(prefix_s[2 * rr + 1])
        send2[rr] = jnp.concatenate([first, second], axis=0).astype(BF16)

        @pl.when(me_r < tail_n)
        def _():
            for s in range(2):
                block = prefix_s[2 * rr + s]
                both = trecv1[block // 2]
                tsend2[rr, s * tail_p : (s + 1) * tail_p, :] = jnp.where(
                    block % 2 == 1, both[tail_p:, :], both[:tail_p, :]
                )

    def second_copy(rr):
        return remote(send2.at[rr], recv2.at[me_r], s2_send.at[rr], s2_recv.at[me_r], rr, me_t)

    def second_tail(rr):
        return remote(tsend2.at[rr], trecv2.at[me_r], t2_send.at[rr], t2_recv.at[me_r], rr, me_t)

    def start_second(rr):
        second_copy(rr).start()

        @pl.when(me_r < tail_n)
        def _():
            second_tail(rr).start()

    def second_step(m, carry):
        base = far_pair(m)
        choose(base)
        choose(base + 1)

        @pl.when(m > 0)
        def _():
            before = far_pair(m - 1)
            start_second(before)
            start_second(before + 1)

        return carry

    lax.fori_loop(0, nz - 1, second_step, 0)
    choose(zi * 2)
    choose(zi * 2 + 1)
    start_second(far_pair(nz - 2))
    start_second(far_pair(nz - 2) + 1)
    start_second(zi * 2 + 1 - ci)
    own2 = pltpu.make_async_copy(send2.at[me_r], recv2.at[me_r], own_sem.at[2])
    own2.start()

    @pl.when(me_r < tail_n)
    def _():
        copy = pltpu.make_async_copy(tsend2.at[me_r], trecv2.at[me_r], own_sem.at[3])
        copy.start()
        copy.wait()

    def weight_wait(buf, at, lo, size, index):
        weight_copy(buf, at, lo, size, index, me_t).wait_recv()

    weight_wait(w_a, dn_y, 0, fill, 0)
    if ny > 2:
        weight_start(weight_copy(w_a, dn_y, 0, fill, 8, tensor_of(xi, up_y)))
        weight_wait(w_a, up_y, fill, fill, 2)
        weight_start(weight_copy(w_a, up_y, fill, fill, 9, tensor_of(xi, dn_y)))
    weight_wait(w_b, dn_x, 0, fill, 4)
    if nx > 2:
        weight_start(weight_copy(w_b, dn_x, 0, fill, 10, tensor_of(up_x, yi)))
        weight_wait(w_b, up_x, fill, fill, 6)
        weight_start(weight_copy(w_b, up_x, fill, fill, 11, tensor_of(dn_x, yi)))

    def wait_second(rr):
        remote(send2.at[rr], recv2.at[rr], s2_send.at[rr], s2_recv.at[rr], rr, me_t).wait_recv()

        @pl.when(rr < tail_n)
        def _():
            remote(
                tsend2.at[0], trecv2.at[rr], t2_send.at[0], t2_recv.at[rr], rr, me_t
            ).wait_recv()

    own2.wait()
    each_replica(wait_second)

    lane_head = iota((1, width), 1) // HEAD_DIM
    saved = []
    for q in range(2):
        start_at = recv2[...].astype(F32)[:, q * piece : (q + 1) * piece, :]
        start_at = start_at.reshape(width, STATE)
        at8 = iota((8, STATE), 0)

        def tail_tile(part):
            tile = jnp.zeros((8, STATE), F32)
            for t in range(3):
                row = t * 4 + part
                at = q * tail_p + row % tail_p
                line = trecv2[row // tail_p, at : at + 1, :]
                tile = jnp.where(at8 == t, line, tile)
            return tile

        def tail_fix(tile, taps):
            total = tile * taps[0:1, :]
            rolled = jnp.where(at8 < 3, pltpu.roll(tile, 7, 0), 0.0)
            total = total + rolled * taps[1:2, :]
            rolled = jnp.where(at8 < 3, pltpu.roll(tile, 6, 0), 0.0)
            return total + rolled * taps[2:3, :]

        for part in range(2):
            lanes = slice(part * STATE, (part + 1) * STATE)
            xraw[q, 0:8, lanes] += tail_fix(tail_tile(part), convx_v[:, lanes])
            bcraw[q, 0:8, lanes] += tail_fix(tail_tile(part + 2), convbc_v[:, lanes])
        xc = silu(xraw[q])
        bcc = silu(bcraw[q])
        b_low = bcc[:, :STATE].astype(BF16)
        c_low = bcc[:, STATE:].astype(BF16)
        scores = dot_nt(c_low, b_low)
        y = expcum[q] * dot_nt(c_low, start_at.astype(BF16)) + skip_wide * xc
        for hp in range(heads // 2):
            left, right = 2 * hp, 2 * hp + 1
            mixing = jnp.concatenate([scores * decay[q, left], scores * decay[q, right]], axis=1)
            held = jnp.concatenate(
                [jnp.where(lane_head == left, xc, 0.0), jnp.where(lane_head == right, xc, 0.0)],
                axis=0,
            )
            y = y + jnp.dot(mixing.astype(BF16), held.astype(BF16), preferred_element_type=F32)
        v = y * gate[q]
        ss_send[:, q * slot : (q + 1) * slot] = dot_nt(
            jnp.ones((8, width), F32), v * v, HIGHEST
        )[0:1]
        live = iota((slot, width), 0) < lengths_s[q]
        v = jnp.where(live, v * gain_v[...], 0.0)
        owners = slot // rows_owner // ny
        v_a[q * owners : (q + 1) * owners] = v.astype(BF16).reshape(owners, ny, rows_owner, width)
        saved.append((start_at, xc, b_low))

    def ss_copy(xx, yy, cc):
        return remote(
            ss_send,
            ss_recv.at[ci * nx + xi, yi],
            ss_ssem.at[cc * nx + xx, yy],
            ss_rsem.at[ci * nx + xi, yi],
            zi * 2 + cc,
            tensor_of(xx, yy),
        )

    def va_copy(yy, cc):
        return remote(
            v_a.at[:, yy],
            r_a.at[ci, yi],
            va_send.at[cc, yy],
            va_recv.at[ci, yi],
            zi * 2 + cc,
            tensor_of(xi, yy),
        )

    def vb_copy(xx, cc):
        return remote(
            v_a.at[xx],
            r_b.at[ci, xi],
            vb_send.at[cc, xx],
            vb_recv.at[ci, xi],
            zi * 2 + cc,
            tensor_of(xx, yi),
        )

    ss_peers = grid_peers() + [(xi, yi, 1 - ci)]
    for xx, yy, cc in ss_peers:
        ss_copy(xx, yy, cc).start()
    for d in (2, 1, 3, 0):
        for dc in range(2):
            if (d or dc) and d < ny:
                va_copy((yi + d) % ny, (ci + dc) % 2).start()
            if (d or dc) and d < nx:
                vb_copy((xi + d) % nx, (ci + dc) % 2).start()
    ss_recv[ci * nx + xi, yi] = ss_send[...]
    own_a = pltpu.make_async_copy(v_a.at[:, yi], r_a.at[ci, yi], own_sem.at[4])
    own_a.start()
    own_b = pltpu.make_async_copy(v_a.at[xi], r_b.at[ci, xi], own_sem.at[5])
    own_b.start()

    for q in range(2):
        start_at, xc, b_low = saved[q]
        weighed = (xc * weighin[q]).astype(BF16)
        final_o[q] = ending[q] * start_at + dot_tn(weighed, b_low)

    if ny > 2:
        weight_wait(w_a, up_y, 0, fill, 3)
    weight_wait(w_a, dn_y, fill, fill, 1)
    if nx > 2:
        weight_wait(w_b, up_x, 0, fill, 7)
    weight_wait(w_b, dn_x, fill, fill, 5)
    if ny > 2:
        opp_y = (yi + 2) % ny
        weight_wait(w_a, opp_y, 0, fill, 8)
        weight_wait(w_a, opp_y, fill, fill, 9)
    for yy, cc in y_peers():
        remote(
            v_a.at[:, yi],
            r_a.at[cc, yy],
            va_send.at[cc, yy],
            va_recv.at[cc, yy],
            zi * 2 + cc,
            tensor_of(xi, yy),
        ).wait_recv()
    own_a.wait()
    rows_a = 2 * nx * rows_owner
    acc = jnp.zeros((rows_a, quarter), F32)
    for yy in range(ny):
        lhs = r_a[:, yy].reshape(rows_a, width)
        acc = acc + jnp.dot(lhs, w_a[yy], preferred_element_type=F32)
    for xx, yy, cc in ss_peers:
        remote(
            ss_send,
            ss_recv.at[cc * nx + xx, yy],
            ss_ssem.at[cc * nx + xx, yy],
            ss_rsem.at[cc * nx + xx, yy],
            zi * 2 + cc,
            tensor_of(xx, yy),
        ).wait_recv()

    def scale_row(k):
        total = ss_recv[k, 0]
        for yy in range(1, ny):
            total = total + ss_recv[k, yy]
        return lax.rsqrt(total / (ny * width) + EPSILON)

    scale_all = jnp.concatenate([scale_row(k) for k in range(2 * nx)], axis=0)
    scale_mine = jnp.concatenate([scale_row(xi), scale_row(nx + xi)], axis=0)
    per = nx * rows_owner
    where_row = iota((per, tokens), 0)
    wanted = (where_row // rows_owner * ny + yi) * rows_owner + where_row % rows_owner
    pick_rows = (iota((per, tokens), 1) == wanted).astype(F32)
    col_a = dot_nt(pick_rows, scale_mine, HIGHEST)
    for cc in range(2):
        part = acc[cc * per : (cc + 1) * per, :] * col_a[:, cc : cc + 1]
        o_a[cc] = part.astype(BF16).reshape(nx, rows_owner, quarter)

    for xx, cc in x_peers():
        remote(
            o_a.at[cc, xx],
            ro_a.at[xi, ci],
            oa_send.at[xx, cc],
            oa_recv.at[xi, ci],
            zi * 2 + cc,
            tensor_of(xx, yi),
        ).start()
    own_oa = pltpu.make_async_copy(o_a.at[ci, xi], ro_a.at[xi, ci], own_sem.at[6])
    own_oa.start()

    if nx > 2:
        opp_x = (xi + 2) % nx
        weight_wait(w_b, opp_x, 0, fill, 10)
        weight_wait(w_b, opp_x, fill, fill, 11)
    for xx, cc in x_peers():
        remote(
            v_a.at[xi],
            r_b.at[cc, xx],
            vb_send.at[cc, xx],
            vb_recv.at[cc, xx],
            zi * 2 + cc,
            tensor_of(xx, yi),
        ).wait_recv()
    own_b.wait()
    rows_b = 2 * ny * rows_owner
    acc = jnp.zeros((rows_b, quarter), F32)
    per = ny * rows_owner
    pick_rows = (iota((per, tokens), 1) == iota((per, tokens), 0) + xi * per).astype(F32)
    col_b = dot_nt(pick_rows, scale_all, HIGHEST)
    for xx in range(nx):
        lhs = r_b[:, xx].reshape(rows_b, width)
        col = jnp.concatenate([col_b[:, xx : xx + 1], col_b[:, nx + xx : nx + xx + 1]], axis=0)
        acc = acc + jnp.dot(lhs, w_b[xx], preferred_element_type=F32) * col
    o_b[...] = acc.astype(BF16).reshape(2, ny, rows_owner, quarter)
    for yy, cc in y_peers():
        remote(
            o_b.at[cc, yy],
            ro_b.at[yi, ci],
            ob_send.at[yy, cc],
            ob_recv.at[yi, ci],
            zi * 2 + cc,
            tensor_of(xi, yy),
        ).start()
    own_ob = pltpu.make_async_copy(o_b.at[ci, yi], ro_b.at[yi, ci], own_sem.at[7])
    own_ob.start()

    for xx, cc in x_peers():
        remote(
            o_a.at[cc, xx],
            ro_a.at[xx, cc],
            oa_send.at[xx, cc],
            oa_recv.at[xx, cc],
            zi * 2 + cc,
            tensor_of(xx, yi),
        ).wait_recv()
    own_oa.wait()
    for cc in range(2):
        total = ro_a[0, cc].astype(F32)
        for xx in range(1, nx):
            total = total + ro_a[xx, cc].astype(F32)
        mixed_o[:, cc * quarter : (cc + 1) * quarter] = total.astype(BF16)
    for yy, cc in y_peers():
        remote(
            o_b.at[cc, yy],
            ro_b.at[yy, cc],
            ob_send.at[yy, cc],
            ob_recv.at[yy, cc],
            zi * 2 + cc,
            tensor_of(xi, yy),
        ).wait_recv()
    own_ob.wait()
    for cc in range(2):
        total = ro_b[0, cc].astype(F32)
        for yy in range(1, ny):
            total = total + ro_b[yy, cc].astype(F32)
        lo = half_cols + cc * quarter
        mixed_o[:, lo : lo + quarter] = total.astype(BF16)

    def sent(rr):
        first_copy(rr).wait_send()
        second_copy(rr).wait_send()

        @pl.when(rr < tail_n)
        def _():
            first_tail(rr).wait_send()

        @pl.when(me_r < tail_n)
        def _():
            second_tail(rr).wait_send()

    each_replica(sent)
    for copy in started:
        copy.wait_send()
    for xx, yy, cc in ss_peers:
        ss_copy(xx, yy, cc).wait_send()
    for yy, cc in y_peers():
        va_copy(yy, cc).wait_send()
        remote(
            o_b.at[cc, yy],
            ro_b.at[yi, ci],
            ob_send.at[yy, cc],
            ob_recv.at[yi, ci],
            zi * 2 + cc,
            tensor_of(xi, yy),
        ).wait_send()
    for xx, cc in x_peers():
        vb_copy(xx, cc).wait_send()
        remote(
            o_a.at[cc, xx],
            ro_a.at[xi, ci],
            oa_send.at[xx, cc],
            oa_recv.at[xi, ci],
            zi * 2 + cc,
            tensor_of(xx, yi),
        ).wait_send()


def store_kernel(mixed_v, final_v, mixed_o, final_o, sem):
    first = pltpu.make_async_copy(mixed_v, mixed_o, sem.at[0])
    second = pltpu.make_async_copy(final_v, final_o, sem.at[1])
    first.start()
    second.start()
    first.wait()
    second.wait()


def local(
    sizes,
    x_input,
    z_input,
    bc_input,
    dt_raw,
    dt_bias,
    decay_rates,
    skip_gain,
    conv_x,
    conv_bc,
    norm_gain,
    out_weight,
    cached_states,
    cached_tail_x,
    cached_tail_bc,
    prefix_block,
    lengths,
):
    nr, nx, ny = sizes
    tokens, width = x_input.shape
    heads = dt_raw.shape[1]
    slot = tokens // 2
    out_cols = out_weight.shape[1]
    quarter = out_cols // 4
    rows_owner = tokens // (nx * ny)
    piece = width // nr
    tail_n = min(nr, TAIL_ROWS)
    tail_p = TAIL_ROWS // tail_n
    vmem = pltpu.VMEM
    dma = pltpu.SemaphoreType.DMA
    smem_spec = pl.BlockSpec(memory_space=pltpu.SMEM)
    hbm_spec = pl.BlockSpec(memory_space=pl.ANY)
    vmem_spec = pl.BlockSpec(memory_space=pltpu.VMEM)
    scratch = [
        vmem((tokens, width), BF16),
        vmem((tokens, width), BF16),
        vmem((tokens, 2 * STATE), BF16),
        vmem((heads, tokens), F32),
        vmem((4, width), F32),
        vmem((4, 2 * STATE), F32),
        vmem((1, width), F32),
        vmem((2, width, STATE), F32),
        vmem((3, 2, width), F32),
        vmem((3, 2, 2 * STATE), F32),
        vmem((nr, 2 * piece, STATE), BF16),
        vmem((nr, 2 * piece, STATE), BF16),
        vmem((nr, 2 * piece, STATE), BF16),
        vmem((nr, 2 * piece, STATE), BF16),
        vmem((tail_n, 2 * tail_p, STATE), F32),
        vmem((nr, 2 * tail_p, STATE), F32),
        vmem((nr, 2 * tail_p, STATE), F32),
        vmem((tail_n, 2 * tail_p, STATE), F32),
        vmem((ny, width, quarter), BF16),
        vmem((nx, width, quarter), BF16),
        vmem((2, slot, width), F32),
        vmem((2, slot, 2 * STATE), F32),
        vmem((2, slot, width), F32),
        vmem((2, heads, slot, slot), F32),
        vmem((2, slot, width), F32),
        vmem((2, slot, width), F32),
        vmem((2, width, STATE), F32),
        vmem((nx, ny, rows_owner, width), BF16),
        vmem((2, ny, nx, rows_owner, width), BF16),
        vmem((2, nx, ny, rows_owner, width), BF16),
        vmem((1, tokens), F32),
        vmem((2 * nx, ny, 1, tokens), F32),
        vmem((2, nx, rows_owner, quarter), BF16),
        vmem((2, ny, rows_owner, quarter), BF16),
        vmem((nx, 2, rows_owner, quarter), BF16),
        vmem((ny, 2, rows_owner, quarter), BF16),
        dma((15,)),
        dma((8,)),
        dma((nr,)),
        dma((nr,)),
        dma((nr,)),
        dma((nr,)),
        dma((nr,)),
        dma((nr,)),
        dma((nr,)),
        dma((nr,)),
        dma((12,)),
        dma((12,)),
        dma((2, ny)),
        dma((2, ny)),
        dma((2, nx)),
        dma((2, nx)),
        dma((2 * nx, ny)),
        dma((2 * nx, ny)),
        dma((nx, 2)),
        dma((nx, 2)),
        dma((ny, 2)),
        dma((ny, 2)),
    ]
    mixed, final_states = pl.pallas_call(
        functools.partial(layer_kernel, sizes),
        out_shape=(vmem((rows_owner, out_cols), BF16), vmem((2, width, STATE), F32)),
        in_specs=[smem_spec] * 5 + [hbm_spec] * 11,
        out_specs=(vmem_spec, vmem_spec),
        scratch_shapes=scratch,
        compiler_params=pltpu.CompilerParams(
            collective_id=0, has_side_effects=True, vmem_limit_bytes=56 * 1024 * 1024
        ),
        name="prefill_layer",
    )(
        prefix_block,
        lengths,
        dt_bias,
        decay_rates,
        skip_gain,
        x_input,
        z_input,
        bc_input,
        dt_raw.T,
        conv_x,
        conv_bc,
        norm_gain.reshape(1, width),
        out_weight,
        cached_states.reshape(2, width, STATE),
        jnp.transpose(cached_tail_x, (1, 0, 2)),
        jnp.transpose(cached_tail_bc, (1, 0, 2)),
    )
    mixed, final_states = pl.pallas_call(
        store_kernel,
        out_shape=(
            jax.ShapeDtypeStruct((rows_owner, out_cols), BF16),
            jax.ShapeDtypeStruct((2, width, STATE), F32),
        ),
        in_specs=[vmem_spec] * 2,
        out_specs=(hbm_spec, hbm_spec),
        scratch_shapes=[dma((2,))],
        compiler_params=pltpu.CompilerParams(vmem_limit_bytes=4 * 1024 * 1024),
        name="store_results",
    )(mixed, final_states)
    return mixed, final_states.reshape(2, heads, HEAD_DIM, STATE)


def tensor_grid(count):
    side = 1
    while side * side < count:
        side *= 2
    return side, count // side


def solution(mesh):
    placed = (
        P("replica", "tensor"),
        P("replica", "tensor"),
        P("replica", None),
        P("replica", "tensor"),
        P("tensor"),
        P("tensor"),
        P("tensor"),
        P(None, "tensor"),
        P(),
        P("tensor"),
        P("tensor", None),
        P("replica", "tensor", None, None),
        P("replica", None, "tensor"),
        P("replica", None, None),
        P(),
        P("replica"),
    )
    sizes = (mesh.shape["replica"],) + tensor_grid(mesh.shape["tensor"])
    return jax.shard_map(
        functools.partial(local, sizes),
        mesh=mesh,
        in_specs=placed,
        out_specs=(P(("replica", "tensor"), None), P("replica", "tensor", None, None)),
        check_vma=False,
    )
```

```python
import functools

import jax
import jax.numpy as jnp
from jax import lax
from jax.experimental import pallas as pl
from jax.experimental.pallas import tpu as pltpu
from jax.sharding import PartitionSpec as P

MESH = pl.DeviceIdType.MESH
HIGHEST = lax.Precision.HIGHEST
F32 = jnp.float32
BF16 = jnp.bfloat16
HEAD_DIM = 32
STATE = 128
EPSILON = 1e-05
TAIL_ROWS = 12

NT_DIMS = (((1,), (1,)), ((), ()))
TN_DIMS = (((0,), (0,)), ((), ()))


def dot_nt(a, b, precision=None):
    return lax.dot_general(a, b, NT_DIMS, precision=precision, preferred_element_type=F32)


def dot_tn(a, b, precision=None):
    return lax.dot_general(a, b, TN_DIMS, precision=precision, preferred_element_type=F32)


def iota(shape, axis):
    return lax.broadcasted_iota(jnp.int32, shape, axis)


def silu(a):
    return a / (1.0 + jnp.exp(-a))


def layer_kernel(
    sizes,
    prefix_h,
    lengths_h,
    bias_h,
    rates_h,
    skip_h,
    x_h,
    z_h,
    bc_h,
    dt_h,
    convx_h,
    convbc_h,
    gain_h,
    weight_h,
    states_h,
    tailx_h,
    tailbc_h,
    mixed_o,
    final_o,
    prefix_s,
    lengths_s,
    bias_s,
    rates_s,
    skip_s,
    x_v,
    z_v,
    bc_v,
    dt_v,
    convx_v,
    convbc_v,
    gain_v,
    st_v,
    tailx_v,
    tailbc_v,
    send1,
    recv1,
    send2,
    recv2,
    tsend1,
    trecv1,
    tsend2,
    trecv2,
    w_a,
    w_b,
    xraw,
    bcraw,
    gate,
    decay,
    expcum,
    weighin,
    ending,
    v_a,
    r_a,
    r_b,
    ss_send,
    ss_recv,
    o_a,
    o_b,
    ro_a,
    ro_b,
    load_sem,
    own_sem,
    s1_send,
    s1_recv,
    s2_send,
    s2_recv,
    t1_send,
    t1_recv,
    t2_send,
    t2_recv,
    w_send,
    w_recv,
    va_send,
    va_recv,
    vb_send,
    vb_recv,
    ss_ssem,
    ss_rsem,
    oa_send,
    oa_recv,
    ob_send,
    ob_recv,
):
    nr, nx, ny = sizes
    nz = nr // 2
    groups = nx
    tokens, width = x_v.shape
    heads = width // HEAD_DIM
    slot = tokens // 2
    rows_owner = tokens // (nx * ny)
    piece = width // nr
    tail_n = trecv2.shape[0]
    tail_p = TAIL_ROWS // tail_n
    quarter = w_a.shape[2]
    half_cols = 2 * quarter

    me_r = lax.axis_index("replica")
    me_t = lax.axis_index("tensor")
    zi, ci = me_r // 2, me_r % 2
    xi, yi = me_t // ny, me_t % ny

    def far_pair(m):
        k = (m + 1) // 2
        dz = nz // 2 + k * (1 - 2 * (m % 2))
        return (zi + dz) % nz * 2

    def each_replica(fn):
        def step(m, carry):
            base = far_pair(m)
            fn(base)
            fn(base + 1)
            return carry

        lax.fori_loop(0, nz - 1, step, 0)
        fn(zi * 2 + 1 - ci)

    def y_peers():
        out = []
        for d in range(ny):
            for dc in range(2):
                if d or dc:
                    out.append(((yi + d) % ny, (ci + dc) % 2))
        return out

    def x_peers():
        out = []
        for d in range(nx):
            for dc in range(2):
                if d or dc:
                    out.append(((xi + d) % nx, (ci + dc) % 2))
        return out

    def grid_peers():
        out = []
        for dx in range(nx):
            for dy in range(ny):
                for cc in range(2):
                    if dx or dy:
                        out.append(((xi + dx) % nx, (yi + dy) % ny, cc))
        return out

    def tensor_of(xx, yy):
        return xx * ny + yy

    def tail_slot(rr):
        return (rr * tail_n + nr - 1) // nr

    def has_tail(rr):
        return tail_slot(rr) * nr // tail_n == rr

    def remote(src, dst, ssem, rsem, rr, tt):
        return pltpu.make_async_remote_copy(
            src_ref=src,
            dst_ref=dst,
            send_sem=ssem,
            recv_sem=rsem,
            device_id=(rr, tt),
            device_id_type=MESH,
        )

    barrier = pltpu.get_barrier_semaphore()

    def greet(rr, tt):
        pl.semaphore_signal(barrier, inc=1, device_id=(rr, tt), device_id_type=MESH)

    each_replica(lambda rr: greet(rr, me_t))
    for xx, yy, cc in grid_peers():
        greet(zi * 2 + cc, tensor_of(xx, yy))
    expected = 2 * (nz - 1) + 1 + 2 * (nx * ny - 1)

    b_lo = pl.multiple_of(xi * STATE, STATE)
    c_lo = pl.multiple_of((groups + xi) * STATE, STATE)
    cols_a = pl.ds(pl.multiple_of(ci * quarter, quarter), quarter)
    cols_b = pl.ds(pl.multiple_of(half_cols + ci * quarter, quarter), quarter)
    lane_b, lane_c = pl.ds(0, STATE), pl.ds(STATE, STATE)
    loads = []

    def load(src, dst):
        copy = pltpu.make_async_copy(src, dst, load_sem.at[len(loads)])
        copy.start()
        loads.append(copy)
        return copy

    load_states = load(states_h, st_v)
    load_tx = load(tailx_h, tailx_v)
    scalars = [
        load(prefix_h, prefix_s),
        load(lengths_h, lengths_s),
        load(bias_h, bias_s),
        load(rates_h, rates_s),
        load(skip_h, skip_s),
    ]
    load_tb = load(tailbc_h.at[:, :, pl.ds(b_lo, STATE)], tailbc_v.at[:, :, lane_b])
    load_tc = load(tailbc_h.at[:, :, pl.ds(c_lo, STATE)], tailbc_v.at[:, :, lane_c])
    load_dt = load(dt_h, dt_v)
    load_x = load(x_h, x_v)
    load_b = load(bc_h.at[:, pl.ds(b_lo, STATE)], bc_v.at[:, lane_b])
    load_c = load(bc_h.at[:, pl.ds(c_lo, STATE)], bc_v.at[:, lane_c])
    load_cx = load(convx_h, convx_v)
    load_cb = load(convbc_h.at[:, pl.ds(b_lo, STATE)], convbc_v.at[:, lane_b])
    load_cc = load(convbc_h.at[:, pl.ds(c_lo, STATE)], convbc_v.at[:, lane_c])
    load_z = load(z_h, z_v)
    load_g = load(gain_h, gain_v)
    load_wa = load(weight_h.at[:, cols_a], w_a.at[yi])
    load_wb = load(weight_h.at[:, cols_b], w_b.at[xi])

    load_states.wait()
    packed = st_v[...].reshape(2, nr, piece, STATE)
    for b in range(2):
        send1[:, b * piece : (b + 1) * piece, :] = packed[b].astype(BF16)
    load_tx.wait()
    load_tb.wait()
    load_tc.wait()
    for row in range(TAIL_ROWS):
        t, part = row // 4, row % 4
        for b in range(2):
            src = tailx_v if part < 2 else tailbc_v
            lanes = slice((part % 2) * STATE, (part % 2 + 1) * STATE)
            at = b * tail_p + row % tail_p
            tsend1[row // tail_p, at : at + 1, :] = src[t, b : b + 1, lanes]

    for copy in scalars:
        copy.wait()
    pl.semaphore_wait(barrier, expected)

    def first_copy(rr):
        return remote(send1.at[rr], recv1.at[me_r], s1_send.at[rr], s1_recv.at[me_r], rr, me_t)

    def first_tail(rr):
        return remote(tsend1.at[tail_slot(rr)], trecv1.at[me_r], t1_send.at[rr], t1_recv.at[me_r], rr, me_t)

    def start_first(rr):
        first_copy(rr).start()

        @pl.when(has_tail(rr))
        def _():
            first_tail(rr).start()

    each_replica(start_first)
    own1 = pltpu.make_async_copy(send1.at[me_r], recv1.at[me_r], own_sem.at[0])
    own1.start()

    @pl.when(has_tail(me_r))
    def _():
        copy = pltpu.make_async_copy(
            tsend1.at[tail_slot(me_r)], trecv1.at[me_r], own_sem.at[1]
        )
        copy.start()
        copy.wait()

    up_y, dn_y = (yi + 1) % ny, (yi + ny - 1) % ny
    up_x, dn_x = (xi + 1) % nx, (xi + nx - 1) % nx
    fill = w_a.shape[1] // 2

    def weight_copy(buf, at, lo, size, index, tt):
        ref = buf.at[at, pl.ds(lo, size), :]
        return remote(ref, ref, w_send.at[index], w_recv.at[index], me_r, tt)

    load_wa.wait()
    load_wb.wait()
    started = []

    def weight_start(copy):
        copy.start()
        started.append(copy)

    lows = (0, fill)
    for turn in range(2):
        lo, hi = lows[turn], lows[1 - turn]
        weight_start(weight_copy(w_a, yi, lo, fill, turn, tensor_of(xi, up_y)))
        weight_start(weight_copy(w_b, xi, lo, fill, 4 + turn, tensor_of(up_x, yi)))
        if ny > 2:
            weight_start(weight_copy(w_a, yi, hi, fill, 2 + turn, tensor_of(xi, dn_y)))
        if nx > 2:
            weight_start(weight_copy(w_b, xi, hi, fill, 6 + turn, tensor_of(dn_x, yi)))

    def raw_conv(seq, taps):
        total = seq * taps[3:4, :]
        at = iota(seq.shape, 0)
        for n in range(1, 4):
            moved = jnp.where(at >= n, pltpu.roll(seq, n, 0), 0.0)
            total = total + moved * taps[3 - n : 4 - n, :]
        return total

    load_x.wait()
    load_cx.wait()
    load_b.wait()
    load_c.wait()
    load_cb.wait()
    load_cc.wait()
    load_z.wait()
    for q in range(2):
        part = slice(q * slot, (q + 1) * slot)
        xraw[q] = raw_conv(x_v[part, :].astype(F32), convx_v[...])
        bcraw[q] = raw_conv(bc_v[part, :].astype(F32), convbc_v[...])
        gate[q] = silu(z_v[part, :].astype(F32))
    load_g.wait()

    def wait_first(rr):
        remote(send1.at[rr], recv1.at[rr], s1_send.at[rr], s1_recv.at[rr], rr, me_t).wait_recv()

        @pl.when(has_tail(me_r))
        def _():
            remote(
                tsend1.at[0], trecv1.at[rr], t1_send.at[0], t1_recv.at[rr], rr, me_t
            ).wait_recv()

    own1.wait()
    each_replica(wait_first)

    def pick(block):
        both = recv1[block // 2].astype(F32)
        return jnp.where(block % 2 == 1, both[piece:, :], both[:piece, :])

    def choose(rr):
        first = pick(prefix_s[2 * rr])
        second = pick(prefix_s[2 * rr + 1])
        send2[rr] = jnp.concatenate([first, second], axis=0).astype(BF16)

        @pl.when(has_tail(me_r))
        def _():
            for s in range(2):
                block = prefix_s[2 * rr + s]
                both = trecv1[block // 2]
                tsend2[rr, s * tail_p : (s + 1) * tail_p, :] = jnp.where(
                    block % 2 == 1, both[tail_p:, :], both[:tail_p, :]
                )

    def second_copy(rr):
        return remote(send2.at[rr], recv2.at[me_r], s2_send.at[rr], s2_recv.at[me_r], rr, me_t)

    def second_tail(rr):
        return remote(
            tsend2.at[rr],
            trecv2.at[tail_slot(me_r)],
            t2_send.at[rr],
            t2_recv.at[tail_slot(me_r)],
            rr,
            me_t,
        )

    def start_second(rr):
        second_copy(rr).start()

        @pl.when(has_tail(me_r))
        def _():
            second_tail(rr).start()

    def second_step(m, carry):
        base = far_pair(m)
        choose(base)
        choose(base + 1)

        @pl.when(m > 0)
        def _():
            before = far_pair(m - 1)
            start_second(before)
            start_second(before + 1)

        return carry

    lax.fori_loop(0, nz - 1, second_step, 0)
    choose(zi * 2)
    choose(zi * 2 + 1)
    start_second(far_pair(nz - 2))
    start_second(far_pair(nz - 2) + 1)
    start_second(zi * 2 + 1 - ci)
    own2 = pltpu.make_async_copy(send2.at[me_r], recv2.at[me_r], own_sem.at[2])
    own2.start()

    @pl.when(has_tail(me_r))
    def _():
        copy = pltpu.make_async_copy(
            tsend2.at[me_r], trecv2.at[tail_slot(me_r)], own_sem.at[3]
        )
        copy.start()
        copy.wait()

    def weight_wait(buf, at, lo, size, index):
        weight_copy(buf, at, lo, size, index, me_t).wait_recv()

    weight_wait(w_a, dn_y, 0, fill, 0)
    if ny > 2:
        weight_start(weight_copy(w_a, dn_y, 0, fill, 8, tensor_of(xi, up_y)))
        weight_wait(w_a, up_y, fill, fill, 2)
        weight_start(weight_copy(w_a, up_y, fill, fill, 9, tensor_of(xi, dn_y)))
    weight_wait(w_b, dn_x, 0, fill, 4)
    if nx > 2:
        weight_start(weight_copy(w_b, dn_x, 0, fill, 10, tensor_of(up_x, yi)))
        weight_wait(w_b, up_x, fill, fill, 6)
        weight_start(weight_copy(w_b, up_x, fill, fill, 11, tensor_of(dn_x, yi)))

    load_dt.wait()
    head_row = iota((heads, 1), 0)
    head_lane = iota((1, heads), 1)
    bias_col = jnp.zeros((heads, 1), F32)
    rate_col = jnp.zeros((heads, 1), F32)
    skip_row = jnp.zeros((1, heads), F32)
    for h in range(heads):
        bias_col = jnp.where(head_row == h, bias_s[h], bias_col)
        rate_col = jnp.where(head_row == h, rates_s[h], rate_col)
        skip_row = jnp.where(head_lane == h, skip_s[h], skip_row)
    spread = (iota((heads, width), 1) // HEAD_DIM == iota((heads, width), 0)).astype(F32)
    row_i = iota((slot, slot), 0)
    col_i = iota((slot, slot), 1)
    causal = row_i >= col_i
    lower = causal.astype(F32)

    for q in range(2):
        raw = dt_v[:, q * slot : (q + 1) * slot] + bias_col
        soft = jnp.maximum(raw, 0.0) + jnp.log1p(jnp.exp(-jnp.abs(raw)))
        live = iota((heads, slot), 1) < lengths_s[q]
        dt_t = jnp.where(live, soft, 0.0)
        logdec = -dt_t * rate_col
        cum = dot_nt(lower, logdec, HIGHEST)
        cum_t = dot_nt(logdec, lower, HIGHEST)
        for h in range(heads):
            differ = cum[:, h : h + 1] - cum_t[h : h + 1, :]
            value = jnp.where(causal, jnp.exp(jnp.minimum(differ, 0.0)), 0.0)
            decay[q, h] = value * dt_t[h : h + 1, :]
        expcum[q] = dot_tn(jnp.exp(cum_t), spread, HIGHEST)
        last = cum_t[:, slot - 1 : slot]
        weighin[q] = dot_tn(jnp.exp(last - cum_t) * dt_t, spread, HIGHEST)
        ending[q] = dot_tn(spread, jnp.broadcast_to(jnp.exp(last), (heads, STATE)), HIGHEST)
    skip_wide = jnp.dot(skip_row, spread, precision=HIGHEST, preferred_element_type=F32)

    def wait_second(rr):
        remote(send2.at[rr], recv2.at[rr], s2_send.at[rr], s2_recv.at[rr], rr, me_t).wait_recv()

        @pl.when(has_tail(rr))
        def _():
            remote(
                tsend2.at[0],
                trecv2.at[tail_slot(rr)],
                t2_send.at[0],
                t2_recv.at[tail_slot(rr)],
                rr,
                me_t,
            ).wait_recv()

    own2.wait()
    each_replica(wait_second)

    lane_head = iota((1, width), 1) // HEAD_DIM
    saved = []
    for q in range(2):
        start_at = recv2[...].astype(F32)[:, q * piece : (q + 1) * piece, :]
        start_at = start_at.reshape(width, STATE)
        at8 = iota((8, STATE), 0)

        def tail_tile(part):
            tile = jnp.zeros((8, STATE), F32)
            for t in range(3):
                row = t * 4 + part
                at = q * tail_p + row % tail_p
                line = trecv2[row // tail_p, at : at + 1, :]
                tile = jnp.where(at8 == t, line, tile)
            return tile

        def tail_fix(tile, taps):
            total = tile * taps[0:1, :]
            rolled = jnp.where(at8 < 3, pltpu.roll(tile, 7, 0), 0.0)
            total = total + rolled * taps[1:2, :]
            rolled = jnp.where(at8 < 3, pltpu.roll(tile, 6, 0), 0.0)
            return total + rolled * taps[2:3, :]

        for part in range(2):
            lanes = slice(part * STATE, (part + 1) * STATE)
            xraw[q, 0:8, lanes] += tail_fix(tail_tile(part), convx_v[:, lanes])
            bcraw[q, 0:8, lanes] += tail_fix(tail_tile(part + 2), convbc_v[:, lanes])
        xc = silu(xraw[q])
        bcc = silu(bcraw[q])
        b_low = bcc[:, :STATE].astype(BF16)
        c_low = bcc[:, STATE:].astype(BF16)
        scores = dot_nt(c_low, b_low)
        y = expcum[q] * dot_nt(c_low, start_at.astype(BF16)) + skip_wide * xc
        for hp in range(heads // 2):
            left, right = 2 * hp, 2 * hp + 1
            mixing = jnp.concatenate([scores * decay[q, left], scores * decay[q, right]], axis=1)
            held = jnp.concatenate(
                [jnp.where(lane_head == left, xc, 0.0), jnp.where(lane_head == right, xc, 0.0)],
                axis=0,
            )
            y = y + jnp.dot(mixing.astype(BF16), held.astype(BF16), preferred_element_type=F32)
        v = y * gate[q]
        ss_send[:, q * slot : (q + 1) * slot] = dot_nt(
            jnp.ones((8, width), F32), v * v, HIGHEST
        )[0:1]
        live = iota((slot, width), 0) < lengths_s[q]
        v = jnp.where(live, v * gain_v[...], 0.0)
        owners = slot // rows_owner // ny
        v_a[q * owners : (q + 1) * owners] = v.astype(BF16).reshape(owners, ny, rows_owner, width)
        saved.append((start_at, xc, b_low))

    def ss_copy(xx, yy, cc):
        return remote(
            ss_send,
            ss_recv.at[ci * nx + xi, yi],
            ss_ssem.at[cc * nx + xx, yy],
            ss_rsem.at[ci * nx + xi, yi],
            zi * 2 + cc,
            tensor_of(xx, yy),
        )

    def va_copy(yy, cc):
        return remote(
            v_a.at[:, yy],
            r_a.at[ci, yi],
            va_send.at[cc, yy],
            va_recv.at[ci, yi],
            zi * 2 + cc,
            tensor_of(xi, yy),
        )

    def vb_copy(xx, cc):
        return remote(
            v_a.at[xx],
            r_b.at[ci, xi],
            vb_send.at[cc, xx],
            vb_recv.at[ci, xi],
            zi * 2 + cc,
            tensor_of(xx, yi),
        )

    ss_peers = grid_peers() + [(xi, yi, 1 - ci)]
    for xx, yy, cc in ss_peers:
        ss_copy(xx, yy, cc).start()
    for d in (2, 1, 3, 0):
        for dc in range(2):
            if (d or dc) and d < ny:
                va_copy((yi + d) % ny, (ci + dc) % 2).start()
            if (d or dc) and d < nx:
                vb_copy((xi + d) % nx, (ci + dc) % 2).start()
    ss_recv[ci * nx + xi, yi] = ss_send[...]
    own_a = pltpu.make_async_copy(v_a.at[:, yi], r_a.at[ci, yi], own_sem.at[4])
    own_a.start()
    own_b = pltpu.make_async_copy(v_a.at[xi], r_b.at[ci, xi], own_sem.at[5])
    own_b.start()

    for q in range(2):
        start_at, xc, b_low = saved[q]
        weighed = (xc * weighin[q]).astype(BF16)
        final_o[q] = ending[q] * start_at + dot_tn(weighed, b_low)

    def wait_va(yy, cores):
        for cc in cores:
            remote(
                v_a.at[:, yi],
                r_a.at[cc, yy],
                va_send.at[cc, yy],
                va_recv.at[cc, yy],
                zi * 2 + cc,
                tensor_of(xi, yy),
            ).wait_recv()

    def wait_vb(xx, cores):
        for cc in cores:
            remote(
                v_a.at[xi],
                r_b.at[cc, xx],
                vb_send.at[cc, xx],
                vb_recv.at[cc, xx],
                zi * 2 + cc,
                tensor_of(xx, yi),
            ).wait_recv()

    per_a = nx * rows_owner
    per_b = ny * rows_owner

    half = quarter // 2
    x_order = x_peers()[::-1]
    y_order = y_peers()[::-1]
    if nx > 2:
        x_order = [((xi + d) % nx, (ci + e) % 2) for d in (2, 1, 3) for e in range(2)]
        x_order.append((xi, 1 - ci))
    if ny > 2:
        y_order = [((yi + d) % ny, (ci + e) % 2) for d in (2, 1, 3) for e in range(2)]
        y_order.append((yi, 1 - ci))

    def block_a(yy, cols):
        lhs = jnp.concatenate(
            [r_a[0, yy].reshape(per_a, width), r_a[1, yy].reshape(per_a, width)], axis=0
        )
        return jnp.dot(lhs, w_a[yy, :, cols], preferred_element_type=F32)

    def block_b(at, cols):
        xx = at
        lhs = jnp.concatenate(
            [r_b[0, xx].reshape(per_b, width), r_b[1, xx].reshape(per_b, width)], axis=0
        )
        col = jnp.concatenate([col_b[:, at : at + 1], col_b[:, nx + at : nx + at + 1]], axis=0)
        return jnp.dot(lhs, w_b[xx, :, cols], preferred_element_type=F32) * col

    for xx, yy, cc in ss_peers:
        remote(
            ss_send,
            ss_recv.at[cc * nx + xx, yy],
            ss_ssem.at[cc * nx + xx, yy],
            ss_rsem.at[cc * nx + xx, yy],
            zi * 2 + cc,
            tensor_of(xx, yy),
        ).wait_recv()

    def scale_row(k):
        total = ss_recv[k, 0]
        for yy in range(1, ny):
            total = total + ss_recv[k, yy]
        return total

    scale_all = jnp.concatenate(
        [scale_row(cc * nx + xx) for cc in range(2) for xx in range(nx)], axis=0
    )
    scale_all = lax.rsqrt(scale_all / (ny * width) + EPSILON)
    pick_b = (iota((per_b, tokens), 1) == iota((per_b, tokens), 0) + xi * per_b).astype(F32)
    col_b = dot_nt(pick_b, scale_all, HIGHEST)
    where_row = iota((per_a, tokens), 0)
    wanted = (where_row // rows_owner * ny + yi) * rows_owner + where_row % rows_owner
    pick_a = (iota((per_a, tokens), 1) == wanted).astype(F32)
    scale_mine = jnp.concatenate([scale_row(xi), scale_row(nx + xi)], axis=0)
    scale_mine = lax.rsqrt(scale_mine / (ny * width) + EPSILON)
    col_a = dot_nt(pick_a, scale_mine, HIGHEST)

    weight_wait(w_a, dn_y, fill, fill, 1)
    if ny > 2:
        weight_wait(w_a, up_y, 0, fill, 3)
        opp_y = (yi + 2) % ny
        weight_wait(w_a, opp_y, 0, fill, 8)
        weight_wait(w_a, opp_y, fill, fill, 9)
    for yy, cc in y_peers():
        wait_va(yy, (cc,))
    own_a.wait()
    own_b.wait()
    wait_vb(xi, (1 - ci,))
    weight_wait(w_b, dn_x, fill, fill, 5)
    if nx > 2:
        weight_wait(w_b, up_x, 0, fill, 7)
        opp_x = (xi + 2) % nx
        weight_wait(w_b, opp_x, 0, fill, 10)
        weight_wait(w_b, opp_x, fill, fill, 11)
    for xx, cc in x_peers()[1:]:
        wait_vb(xx, (cc,))

    def oa_copy(h, xx, cc):
        return remote(
            o_a.at[h, cc, xx],
            ro_a.at[h, xi, ci],
            oa_send.at[h, xx, cc],
            oa_recv.at[h, xi, ci],
            zi * 2 + cc,
            tensor_of(xx, yi),
        )

    def ob_copy(h, yy, cc):
        return remote(
            o_b.at[h, cc, yy],
            ro_b.at[h, yi, ci],
            ob_send.at[h, yy, cc],
            ob_recv.at[h, yi, ci],
            zi * 2 + cc,
            tensor_of(xi, yy),
        )

    for h in range(2):
        cols = slice(h * half, (h + 1) * half)
        total = block_a(0, cols)
        for yy in range(1, ny):
            total = total + block_a(yy, cols)
        for cc in range(2):
            part = total[cc * per_a : (cc + 1) * per_a, :] * col_a[:, cc : cc + 1]
            o_a[h, cc] = part.astype(BF16).reshape(nx, rows_owner, half)
        for xx, cc in x_order:
            oa_copy(h, xx, cc).start()
        total = block_b(0, cols)
        for at in range(1, nx):
            total = total + block_b(at, cols)
        o_b[h] = total.astype(BF16).reshape(2, ny, rows_owner, half)
        for yy, cc in y_order:
            ob_copy(h, yy, cc).start()
    own_out = []
    for h in range(2):
        own_out.append(
            pltpu.make_async_copy(o_a.at[h, ci, xi], ro_a.at[h, xi, ci], own_sem.at[6 + h])
        )
        own_out.append(
            pltpu.make_async_copy(o_b.at[h, ci, yi], ro_b.at[h, yi, ci], own_sem.at[8 + h])
        )
    for copy in own_out:
        copy.start()
    for copy in own_out:
        copy.wait()

    for h in range(2):
        for xx, cc in x_peers():
            remote(
                o_a.at[h, cc, xx],
                ro_a.at[h, xx, cc],
                oa_send.at[h, xx, cc],
                oa_recv.at[h, xx, cc],
                zi * 2 + cc,
                tensor_of(xx, yi),
            ).wait_recv()
        for cc in range(2):
            total = ro_a[h, 0, cc].astype(F32)
            for xx in range(1, nx):
                total = total + ro_a[h, xx, cc].astype(F32)
            lo = cc * quarter + h * half
            mixed_o[:, lo : lo + half] = total.astype(BF16)
        for yy, cc in y_peers():
            remote(
                o_b.at[h, cc, yy],
                ro_b.at[h, yy, cc],
                ob_send.at[h, yy, cc],
                ob_recv.at[h, yy, cc],
                zi * 2 + cc,
                tensor_of(xi, yy),
            ).wait_recv()
        for cc in range(2):
            total = ro_b[h, 0, cc].astype(F32)
            for yy in range(1, ny):
                total = total + ro_b[h, yy, cc].astype(F32)
            lo = half_cols + cc * quarter + h * half
            mixed_o[:, lo : lo + half] = total.astype(BF16)

    def sent(rr):
        first_copy(rr).wait_send()
        second_copy(rr).wait_send()

        @pl.when(has_tail(rr))
        def _():
            first_tail(rr).wait_send()

        @pl.when(has_tail(me_r))
        def _():
            second_tail(rr).wait_send()

    each_replica(sent)
    for copy in started:
        copy.wait_send()
    for xx, yy, cc in ss_peers:
        ss_copy(xx, yy, cc).wait_send()
    for yy, cc in y_peers():
        va_copy(yy, cc).wait_send()
        for h in range(2):
            ob_copy(h, yy, cc).wait_send()
    for xx, cc in x_peers():
        vb_copy(xx, cc).wait_send()
        for h in range(2):
            oa_copy(h, xx, cc).wait_send()


def store_kernel(mixed_v, final_v, mixed_o, final_o, sem):
    first = pltpu.make_async_copy(mixed_v, mixed_o, sem.at[0])
    second = pltpu.make_async_copy(final_v, final_o, sem.at[1])
    first.start()
    second.start()
    first.wait()
    second.wait()


def local(
    sizes,
    x_input,
    z_input,
    bc_input,
    dt_raw,
    dt_bias,
    decay_rates,
    skip_gain,
    conv_x,
    conv_bc,
    norm_gain,
    out_weight,
    cached_states,
    cached_tail_x,
    cached_tail_bc,
    prefix_block,
    lengths,
):
    nr, nx, ny = sizes
    tokens, width = x_input.shape
    heads = dt_raw.shape[1]
    slot = tokens // 2
    out_cols = out_weight.shape[1]
    quarter = out_cols // 4
    rows_owner = tokens // (nx * ny)
    piece = width // nr
    tail_n = min(nr, TAIL_ROWS)
    tail_p = TAIL_ROWS // tail_n
    vmem = pltpu.VMEM
    dma = pltpu.SemaphoreType.DMA
    smem = pltpu.SMEM
    hbm_spec = pl.BlockSpec(memory_space=pl.ANY)
    vmem_spec = pl.BlockSpec(memory_space=pltpu.VMEM)
    scratch = [
        smem(prefix_block.shape, jnp.int32),
        smem(lengths.shape, jnp.int32),
        smem((heads,), F32),
        smem((heads,), F32),
        smem((heads,), F32),
        vmem((tokens, width), BF16),
        vmem((tokens, width), BF16),
        vmem((tokens, 2 * STATE), BF16),
        vmem((heads, tokens), F32),
        vmem((4, width), F32),
        vmem((4, 2 * STATE), F32),
        vmem((1, width), F32),
        vmem((2, width, STATE), F32),
        vmem((3, 2, width), F32),
        vmem((3, 2, 2 * STATE), F32),
        vmem((nr, 2 * piece, STATE), BF16),
        vmem((nr, 2 * piece, STATE), BF16),
        vmem((nr, 2 * piece, STATE), BF16),
        vmem((nr, 2 * piece, STATE), BF16),
        vmem((tail_n, 2 * tail_p, STATE), F32),
        vmem((nr, 2 * tail_p, STATE), F32),
        vmem((nr, 2 * tail_p, STATE), F32),
        vmem((tail_n, 2 * tail_p, STATE), F32),
        vmem((ny, width, quarter), BF16),
        vmem((nx, width, quarter), BF16),
        vmem((2, slot, width), F32),
        vmem((2, slot, 2 * STATE), F32),
        vmem((2, slot, width), F32),
        vmem((2, heads, slot, slot), F32),
        vmem((2, slot, width), F32),
        vmem((2, slot, width), F32),
        vmem((2, width, STATE), F32),
        vmem((nx, ny, rows_owner, width), BF16),
        vmem((2, ny, nx, rows_owner, width), BF16),
        vmem((2, nx, ny, rows_owner, width), BF16),
        vmem((1, tokens), F32),
        vmem((2 * nx, ny, 1, tokens), F32),
        vmem((2, 2, nx, rows_owner, quarter // 2), BF16),
        vmem((2, 2, ny, rows_owner, quarter // 2), BF16),
        vmem((2, nx, 2, rows_owner, quarter // 2), BF16),
        vmem((2, ny, 2, rows_owner, quarter // 2), BF16),
        dma((20,)),
        dma((10,)),
        dma((nr,)),
        dma((nr,)),
        dma((nr,)),
        dma((nr,)),
        dma((nr,)),
        dma((nr,)),
        dma((nr,)),
        dma((nr,)),
        dma((12,)),
        dma((12,)),
        dma((2, ny)),
        dma((2, ny)),
        dma((2, nx)),
        dma((2, nx)),
        dma((2 * nx, ny)),
        dma((2 * nx, ny)),
        dma((2, nx, 2)),
        dma((2, nx, 2)),
        dma((2, ny, 2)),
        dma((2, ny, 2)),
    ]
    mixed, final_states = pl.pallas_call(
        functools.partial(layer_kernel, sizes),
        out_shape=(vmem((rows_owner, out_cols), BF16), vmem((2, width, STATE), F32)),
        in_specs=[hbm_spec] * 16,
        out_specs=(vmem_spec, vmem_spec),
        scratch_shapes=scratch,
        compiler_params=pltpu.CompilerParams(
            collective_id=0, has_side_effects=True, vmem_limit_bytes=56 * 1024 * 1024
        ),
        name="prefill_layer",
    )(
        prefix_block,
        lengths,
        dt_bias,
        decay_rates,
        skip_gain,
        x_input,
        z_input,
        bc_input,
        dt_raw.T,
        conv_x,
        conv_bc,
        norm_gain.reshape(1, width),
        out_weight,
        cached_states.reshape(2, width, STATE),
        jnp.transpose(cached_tail_x, (1, 0, 2)),
        jnp.transpose(cached_tail_bc, (1, 0, 2)),
    )
    mixed, final_states = pl.pallas_call(
        store_kernel,
        out_shape=(
            jax.ShapeDtypeStruct((rows_owner, out_cols), BF16),
            jax.ShapeDtypeStruct((2, width, STATE), F32),
        ),
        in_specs=[vmem_spec] * 2,
        out_specs=(hbm_spec, hbm_spec),
        scratch_shapes=[dma((2,))],
        compiler_params=pltpu.CompilerParams(vmem_limit_bytes=4 * 1024 * 1024),
        name="store_results",
    )(mixed, final_states)
    return mixed, final_states.reshape(2, heads, HEAD_DIM, STATE)


def tensor_grid(count):
    side = 1
    while side * side < count:
        side *= 2
    return side, count // side


def solution(mesh):
    placed = (
        P("replica", "tensor"),
        P("replica", "tensor"),
        P("replica", None),
        P("replica", "tensor"),
        P("tensor"),
        P("tensor"),
        P("tensor"),
        P(None, "tensor"),
        P(),
        P("tensor"),
        P("tensor", None),
        P("replica", "tensor", None, None),
        P("replica", None, "tensor"),
        P("replica", None, None),
        P(),
        P("replica"),
    )
    sizes = (mesh.shape["replica"],) + tensor_grid(mesh.shape["tensor"])
    return jax.shard_map(
        functools.partial(local, sizes),
        mesh=mesh,
        in_specs=placed,
        out_specs=(P(("replica", "tensor"), None), P("replica", "tensor", None, None)),
        check_vma=False,
    )
```

```python
import functools

import jax
import jax.numpy as jnp
from jax import lax
from jax.experimental import pallas as pl
from jax.experimental.pallas import tpu as pltpu
from jax.sharding import PartitionSpec as P

MESH = pl.DeviceIdType.MESH
HIGHEST = lax.Precision.HIGHEST
F32 = jnp.float32
BF16 = jnp.bfloat16
HEAD_DIM = 32
STATE = 128
EPSILON = 1e-05
TAIL_ROWS = 12

NT_DIMS = (((1,), (1,)), ((), ()))
TN_DIMS = (((0,), (0,)), ((), ()))


def dot_nt(a, b, precision=None):
    return lax.dot_general(a, b, NT_DIMS, precision=precision, preferred_element_type=F32)


def dot_tn(a, b, precision=None):
    return lax.dot_general(a, b, TN_DIMS, precision=precision, preferred_element_type=F32)


def iota(shape, axis):
    return lax.broadcasted_iota(jnp.int32, shape, axis)


def silu(a):
    return a / (1.0 + jnp.exp(-a))


def layer_kernel(
    sizes,
    prefix_h,
    lengths_h,
    bias_h,
    rates_h,
    skip_h,
    x_h,
    z_h,
    bc_h,
    dt_h,
    convx_h,
    convbc_h,
    gain_h,
    weight_h,
    states_h,
    tailx_h,
    tailbc_h,
    mixed_o,
    final_o,
    prefix_s,
    lengths_s,
    bias_s,
    rates_s,
    skip_s,
    x_v,
    z_v,
    bc_v,
    dt_v,
    convx_v,
    convbc_v,
    gain_v,
    st_v,
    tailx_v,
    tailbc_v,
    send1,
    recv1,
    send2,
    recv2,
    tsend1,
    trecv1,
    tsend2,
    trecv2,
    w_a,
    w_b,
    xraw,
    bcraw,
    gate,
    decay,
    expcum,
    weighin,
    ending,
    v_a,
    r_a,
    r_b,
    ss_send,
    ss_recv,
    o_a,
    o_b,
    ro_a,
    ro_b,
    load_sem,
    own_sem,
    s1_send,
    s1_recv,
    s2_send,
    s2_recv,
    t1_send,
    t1_recv,
    t2_send,
    t2_recv,
    w_send,
    w_recv,
    va_send,
    va_recv,
    vb_send,
    vb_recv,
    ss_ssem,
    ss_rsem,
    oa_send,
    oa_recv,
    ob_send,
    ob_recv,
):
    nr, nx, ny = sizes
    nz = nr // 2
    groups = nx
    tokens, width = x_v.shape
    heads = width // HEAD_DIM
    slot = tokens // 2
    rows_owner = tokens // (nx * ny)
    piece = width // nr
    tail_n = trecv2.shape[0]
    tail_p = TAIL_ROWS // tail_n
    quarter = w_a.shape[2]
    half_cols = 2 * quarter

    me_r = lax.axis_index("replica")
    me_t = lax.axis_index("tensor")
    zi, ci = me_r // 2, me_r % 2
    xi, yi = me_t // ny, me_t % ny

    def far_pair(m):
        k = (m + 1) // 2
        dz = nz // 2 + k * (1 - 2 * (m % 2))
        return (zi + dz) % nz * 2

    def each_replica(fn):
        def step(m, carry):
            base = far_pair(m)
            fn(base)
            fn(base + 1)
            return carry

        lax.fori_loop(0, nz - 1, step, 0)
        fn(zi * 2 + 1 - ci)

    def y_peers():
        out = []
        for d in range(ny):
            for dc in range(2):
                if d or dc:
                    out.append(((yi + d) % ny, (ci + dc) % 2))
        return out

    def x_peers():
        out = []
        for d in range(nx):
            for dc in range(2):
                if d or dc:
                    out.append(((xi + d) % nx, (ci + dc) % 2))
        return out

    def grid_peers():
        out = []
        for dx in range(nx):
            for dy in range(ny):
                for cc in range(2):
                    if dx or dy:
                        out.append(((xi + dx) % nx, (yi + dy) % ny, cc))
        return out

    def tensor_of(xx, yy):
        return xx * ny + yy

    def tail_slot(rr):
        return (rr * tail_n + nr - 1) // nr

    def has_tail(rr):
        return tail_slot(rr) * nr // tail_n == rr

    def remote(src, dst, ssem, rsem, rr, tt):
        return pltpu.make_async_remote_copy(
            src_ref=src,
            dst_ref=dst,
            send_sem=ssem,
            recv_sem=rsem,
            device_id=(rr, tt),
            device_id_type=MESH,
        )

    barrier = pltpu.get_barrier_semaphore()

    def greet(rr, tt):
        pl.semaphore_signal(barrier, inc=1, device_id=(rr, tt), device_id_type=MESH)

    each_replica(lambda rr: greet(rr, me_t))
    for xx, yy, cc in grid_peers():
        greet(zi * 2 + cc, tensor_of(xx, yy))
    expected = 2 * (nz - 1) + 1 + 2 * (nx * ny - 1)

    b_lo = pl.multiple_of(xi * STATE, STATE)
    c_lo = pl.multiple_of((groups + xi) * STATE, STATE)
    cols_a = pl.ds(pl.multiple_of(ci * quarter, quarter), quarter)
    cols_b = pl.ds(pl.multiple_of(half_cols + ci * quarter, quarter), quarter)
    lane_b, lane_c = pl.ds(0, STATE), pl.ds(STATE, STATE)
    loads = []

    def load(src, dst):
        copy = pltpu.make_async_copy(src, dst, load_sem.at[len(loads)])
        copy.start()
        loads.append(copy)
        return copy

    load_states = load(states_h, st_v)
    load_tx = load(tailx_h, tailx_v)
    scalars = [
        load(prefix_h, prefix_s),
        load(lengths_h, lengths_s),
        load(bias_h, bias_s),
        load(rates_h, rates_s),
        load(skip_h, skip_s),
    ]
    load_tb = load(tailbc_h.at[:, :, pl.ds(b_lo, STATE)], tailbc_v.at[:, :, lane_b])
    load_tc = load(tailbc_h.at[:, :, pl.ds(c_lo, STATE)], tailbc_v.at[:, :, lane_c])
    load_dt = load(dt_h, dt_v)
    load_x = load(x_h, x_v)
    load_b = load(bc_h.at[:, pl.ds(b_lo, STATE)], bc_v.at[:, lane_b])
    load_c = load(bc_h.at[:, pl.ds(c_lo, STATE)], bc_v.at[:, lane_c])
    load_cx = load(convx_h, convx_v)
    load_cb = load(convbc_h.at[:, pl.ds(b_lo, STATE)], convbc_v.at[:, lane_b])
    load_cc = load(convbc_h.at[:, pl.ds(c_lo, STATE)], convbc_v.at[:, lane_c])
    load_z = load(z_h, z_v)
    load_g = load(gain_h, gain_v)
    load_wa = load(weight_h.at[:, cols_a], w_a.at[yi])
    load_wb = load(weight_h.at[:, cols_b], w_b.at[xi])

    load_states.wait()
    packed = st_v[...].reshape(2, nr, piece, STATE)
    for b in range(2):
        send1[:, b * piece : (b + 1) * piece, :] = packed[b].astype(BF16)
    load_tx.wait()
    load_tb.wait()
    load_tc.wait()
    for j in range(tail_n):
        lines = []
        for b in range(2):
            for row in range(j * tail_p, (j + 1) * tail_p):
                t, part = row // 4, row % 4
                src = tailx_v if part < 2 else tailbc_v
                lanes = slice((part % 2) * STATE, (part % 2 + 1) * STATE)
                lines.append(src[t, b : b + 1, lanes])
        tsend1[j] = jnp.concatenate(lines, axis=0).astype(BF16)

    for copy in scalars:
        copy.wait()
    pl.semaphore_wait(barrier, expected)

    def first_copy(rr):
        return remote(send1.at[rr], recv1.at[me_r], s1_send.at[rr], s1_recv.at[me_r], rr, me_t)

    def first_tail(rr):
        return remote(tsend1.at[tail_slot(rr)], trecv1.at[me_r], t1_send.at[rr], t1_recv.at[me_r], rr, me_t)

    def start_first(rr):
        first_copy(rr).start()

        @pl.when(has_tail(rr))
        def _():
            first_tail(rr).start()

    each_replica(start_first)
    own1 = pltpu.make_async_copy(send1.at[me_r], recv1.at[me_r], own_sem.at[0])
    own1.start()

    @pl.when(has_tail(me_r))
    def _():
        copy = pltpu.make_async_copy(
            tsend1.at[tail_slot(me_r)], trecv1.at[me_r], own_sem.at[1]
        )
        copy.start()
        copy.wait()

    up_y, dn_y = (yi + 1) % ny, (yi + ny - 1) % ny
    up_x, dn_x = (xi + 1) % nx, (xi + nx - 1) % nx
    fill = w_a.shape[1] // 2

    def weight_copy(buf, at, lo, size, index, tt):
        ref = buf.at[at, pl.ds(lo, size), :]
        return remote(ref, ref, w_send.at[index], w_recv.at[index], me_r, tt)

    load_wa.wait()
    load_wb.wait()
    started = []

    def weight_start(copy):
        copy.start()
        started.append(copy)

    lows = (0, fill)
    for turn in range(2):
        lo, hi = lows[turn], lows[1 - turn]
        weight_start(weight_copy(w_a, yi, lo, fill, turn, tensor_of(xi, up_y)))
        weight_start(weight_copy(w_b, xi, lo, fill, 4 + turn, tensor_of(up_x, yi)))
        if ny > 2:
            weight_start(weight_copy(w_a, yi, hi, fill, 2 + turn, tensor_of(xi, dn_y)))
        if nx > 2:
            weight_start(weight_copy(w_b, xi, hi, fill, 6 + turn, tensor_of(dn_x, yi)))

    def raw_conv(seq, taps):
        total = seq * taps[3:4, :]
        at = iota(seq.shape, 0)
        for n in range(1, 4):
            moved = jnp.where(at >= n, pltpu.roll(seq, n, 0), 0.0)
            total = total + moved * taps[3 - n : 4 - n, :]
        return total

    load_x.wait()
    load_cx.wait()
    load_b.wait()
    load_c.wait()
    load_cb.wait()
    load_cc.wait()
    load_z.wait()
    for q in range(2):
        part = slice(q * slot, (q + 1) * slot)
        xraw[q] = raw_conv(x_v[part, :].astype(F32), convx_v[...])
        bcraw[q] = raw_conv(bc_v[part, :].astype(F32), convbc_v[...])
        gate[q] = silu(z_v[part, :].astype(F32))
    load_g.wait()

    def wait_first(rr):
        remote(send1.at[rr], recv1.at[rr], s1_send.at[rr], s1_recv.at[rr], rr, me_t).wait_recv()

        @pl.when(has_tail(me_r))
        def _():
            remote(
                tsend1.at[0], trecv1.at[rr], t1_send.at[0], t1_recv.at[rr], rr, me_t
            ).wait_recv()

    own1.wait()
    each_replica(wait_first)

    def pick(block):
        both = recv1[block // 2].astype(F32)
        return jnp.where(block % 2 == 1, both[piece:, :], both[:piece, :])

    def choose(rr):
        first = pick(prefix_s[2 * rr])
        second = pick(prefix_s[2 * rr + 1])
        send2[rr] = jnp.concatenate([first, second], axis=0).astype(BF16)

        @pl.when(has_tail(me_r))
        def _():
            chosen = []
            for s in range(2):
                block = prefix_s[2 * rr + s]
                both = trecv1[block // 2].astype(F32)
                chosen.append(jnp.where(block % 2 == 1, both[tail_p:, :], both[:tail_p, :]))
            tsend2[rr] = jnp.concatenate(chosen, axis=0).astype(BF16)

    def second_copy(rr):
        return remote(send2.at[rr], recv2.at[me_r], s2_send.at[rr], s2_recv.at[me_r], rr, me_t)

    def second_tail(rr):
        return remote(
            tsend2.at[rr],
            trecv2.at[tail_slot(me_r)],
            t2_send.at[rr],
            t2_recv.at[tail_slot(me_r)],
            rr,
            me_t,
        )

    def start_second(rr):
        second_copy(rr).start()

        @pl.when(has_tail(me_r))
        def _():
            second_tail(rr).start()

    def second_step(m, carry):
        base = far_pair(m)
        choose(base)
        choose(base + 1)

        @pl.when(m > 0)
        def _():
            before = far_pair(m - 1)
            start_second(before)
            start_second(before + 1)

        return carry

    lax.fori_loop(0, nz - 1, second_step, 0)
    choose(zi * 2)
    choose(zi * 2 + 1)
    start_second(far_pair(nz - 2))
    start_second(far_pair(nz - 2) + 1)
    start_second(zi * 2 + 1 - ci)
    own2 = pltpu.make_async_copy(send2.at[me_r], recv2.at[me_r], own_sem.at[2])
    own2.start()

    @pl.when(has_tail(me_r))
    def _():
        copy = pltpu.make_async_copy(
            tsend2.at[me_r], trecv2.at[tail_slot(me_r)], own_sem.at[3]
        )
        copy.start()
        copy.wait()

    def weight_wait(buf, at, lo, size, index):
        weight_copy(buf, at, lo, size, index, me_t).wait_recv()

    weight_wait(w_a, dn_y, 0, fill, 0)
    if ny > 2:
        weight_start(weight_copy(w_a, dn_y, 0, fill, 8, tensor_of(xi, up_y)))
        weight_wait(w_a, up_y, fill, fill, 2)
        weight_start(weight_copy(w_a, up_y, fill, fill, 9, tensor_of(xi, dn_y)))
    weight_wait(w_b, dn_x, 0, fill, 4)
    if nx > 2:
        weight_start(weight_copy(w_b, dn_x, 0, fill, 10, tensor_of(up_x, yi)))
        weight_wait(w_b, up_x, fill, fill, 6)
        weight_start(weight_copy(w_b, up_x, fill, fill, 11, tensor_of(dn_x, yi)))

    load_dt.wait()
    head_row = iota((heads, 1), 0)
    head_lane = iota((1, heads), 1)
    bias_col = jnp.zeros((heads, 1), F32)
    rate_col = jnp.zeros((heads, 1), F32)
    skip_row = jnp.zeros((1, heads), F32)
    for h in range(heads):
        bias_col = jnp.where(head_row == h, bias_s[h], bias_col)
        rate_col = jnp.where(head_row == h, rates_s[h], rate_col)
        skip_row = jnp.where(head_lane == h, skip_s[h], skip_row)
    spread = (iota((heads, width), 1) // HEAD_DIM == iota((heads, width), 0)).astype(F32)
    row_i = iota((slot, slot), 0)
    col_i = iota((slot, slot), 1)
    causal = row_i >= col_i
    lower = causal.astype(F32)

    for q in range(2):
        raw = dt_v[:, q * slot : (q + 1) * slot] + bias_col
        soft = jnp.maximum(raw, 0.0) + jnp.log1p(jnp.exp(-jnp.abs(raw)))
        live = iota((heads, slot), 1) < lengths_s[q]
        dt_t = jnp.where(live, soft, 0.0)
        logdec = -dt_t * rate_col
        cum = dot_nt(lower, logdec, HIGHEST)
        cum_t = dot_nt(logdec, lower, HIGHEST)
        for h in range(heads):
            differ = cum[:, h : h + 1] - cum_t[h : h + 1, :]
            value = jnp.where(causal, jnp.exp(jnp.minimum(differ, 0.0)), 0.0)
            decay[q, h] = value * dt_t[h : h + 1, :]
        expcum[q] = dot_tn(jnp.exp(cum_t), spread, HIGHEST)
        last = cum_t[:, slot - 1 : slot]
        weighin[q] = dot_tn(jnp.exp(last - cum_t) * dt_t, spread, HIGHEST)
        ending[q] = dot_tn(spread, jnp.broadcast_to(jnp.exp(last), (heads, STATE)), HIGHEST)
    skip_wide = jnp.dot(skip_row, spread, precision=HIGHEST, preferred_element_type=F32)

    def wait_second(rr):
        remote(send2.at[rr], recv2.at[rr], s2_send.at[rr], s2_recv.at[rr], rr, me_t).wait_recv()

        @pl.when(has_tail(rr))
        def _():
            remote(
                tsend2.at[0],
                trecv2.at[tail_slot(rr)],
                t2_send.at[0],
                t2_recv.at[tail_slot(rr)],
                rr,
                me_t,
            ).wait_recv()

    own2.wait()
    each_replica(wait_second)

    lane_head = iota((1, width), 1) // HEAD_DIM
    saved = []
    for q in range(2):
        start_at = recv2[...].astype(F32)[:, q * piece : (q + 1) * piece, :]
        start_at = start_at.reshape(width, STATE)
        at8 = iota((8, STATE), 0)

        def tail_tile(part):
            tile = jnp.zeros((8, STATE), F32)
            for t in range(3):
                row = t * 4 + part
                at = q * tail_p + row % tail_p
                line = trecv2[row // tail_p].astype(F32)[at : at + 1, :]
                tile = jnp.where(at8 == t, line, tile)
            return tile

        def tail_fix(tile, taps):
            total = tile * taps[0:1, :]
            rolled = jnp.where(at8 < 3, pltpu.roll(tile, 7, 0), 0.0)
            total = total + rolled * taps[1:2, :]
            rolled = jnp.where(at8 < 3, pltpu.roll(tile, 6, 0), 0.0)
            return total + rolled * taps[2:3, :]

        for part in range(2):
            lanes = slice(part * STATE, (part + 1) * STATE)
            xraw[q, 0:8, lanes] += tail_fix(tail_tile(part), convx_v[:, lanes])
            bcraw[q, 0:8, lanes] += tail_fix(tail_tile(part + 2), convbc_v[:, lanes])
        xc = silu(xraw[q])
        bcc = silu(bcraw[q])
        b_low = bcc[:, :STATE].astype(BF16)
        c_low = bcc[:, STATE:].astype(BF16)
        scores = dot_nt(c_low, b_low)
        y = expcum[q] * dot_nt(c_low, start_at.astype(BF16)) + skip_wide * xc
        for hp in range(heads // 2):
            left, right = 2 * hp, 2 * hp + 1
            mixing = jnp.concatenate([scores * decay[q, left], scores * decay[q, right]], axis=1)
            held = jnp.concatenate(
                [jnp.where(lane_head == left, xc, 0.0), jnp.where(lane_head == right, xc, 0.0)],
                axis=0,
            )
            y = y + jnp.dot(mixing.astype(BF16), held.astype(BF16), preferred_element_type=F32)
        v = y * gate[q]
        ss_send[:, q * slot : (q + 1) * slot] = dot_nt(
            jnp.ones((8, width), F32), v * v, HIGHEST
        )[0:1]
        live = iota((slot, width), 0) < lengths_s[q]
        v = jnp.where(live, v * gain_v[...], 0.0)
        owners = slot // rows_owner // ny
        v_a[q * owners : (q + 1) * owners] = v.astype(BF16).reshape(owners, ny, rows_owner, width)
        saved.append((start_at, xc, b_low))

    def ss_copy(xx, yy, cc):
        return remote(
            ss_send,
            ss_recv.at[ci * nx + xi, yi],
            ss_ssem.at[cc * nx + xx, yy],
            ss_rsem.at[ci * nx + xi, yi],
            zi * 2 + cc,
            tensor_of(xx, yy),
        )

    def va_copy(yy, cc):
        return remote(
            v_a.at[:, yy],
            r_a.at[ci, yi],
            va_send.at[cc, yy],
            va_recv.at[ci, yi],
            zi * 2 + cc,
            tensor_of(xi, yy),
        )

    def vb_copy(xx, cc):
        return remote(
            v_a.at[xx],
            r_b.at[ci, xi],
            vb_send.at[cc, xx],
            vb_recv.at[ci, xi],
            zi * 2 + cc,
            tensor_of(xx, yi),
        )

    ss_peers = grid_peers() + [(xi, yi, 1 - ci)]
    for xx, yy, cc in ss_peers:
        ss_copy(xx, yy, cc).start()
    for d in (2, 1, 3, 0):
        for dc in range(2):
            if (d or dc) and d < ny:
                va_copy((yi + d) % ny, (ci + dc) % 2).start()
            if (d or dc) and d < nx:
                vb_copy((xi + d) % nx, (ci + dc) % 2).start()
    ss_recv[ci * nx + xi, yi] = ss_send[...]
    own_a = pltpu.make_async_copy(v_a.at[:, yi], r_a.at[ci, yi], own_sem.at[4])
    own_a.start()
    own_b = pltpu.make_async_copy(v_a.at[xi], r_b.at[ci, xi], own_sem.at[5])
    own_b.start()

    for q in range(2):
        start_at, xc, b_low = saved[q]
        weighed = (xc * weighin[q]).astype(BF16)
        final_o[q] = ending[q] * start_at + dot_tn(weighed, b_low)

    def wait_va(yy, cores):
        for cc in cores:
            remote(
                v_a.at[:, yi],
                r_a.at[cc, yy],
                va_send.at[cc, yy],
                va_recv.at[cc, yy],
                zi * 2 + cc,
                tensor_of(xi, yy),
            ).wait_recv()

    def wait_vb(xx, cores):
        for cc in cores:
            remote(
                v_a.at[xi],
                r_b.at[cc, xx],
                vb_send.at[cc, xx],
                vb_recv.at[cc, xx],
                zi * 2 + cc,
                tensor_of(xx, yi),
            ).wait_recv()

    per_a = nx * rows_owner
    per_b = ny * rows_owner

    half = quarter // 2
    x_order = x_peers()[::-1]
    y_order = y_peers()[::-1]
    if nx > 2:
        x_order = [((xi + d) % nx, (ci + e) % 2) for d in (2, 1, 3) for e in range(2)]
        x_order.append((xi, 1 - ci))
    if ny > 2:
        y_order = [((yi + d) % ny, (ci + e) % 2) for d in (2, 1, 3) for e in range(2)]
        y_order.append((yi, 1 - ci))

    def block_a(yy, cols):
        lhs = jnp.concatenate(
            [r_a[0, yy].reshape(per_a, width), r_a[1, yy].reshape(per_a, width)], axis=0
        )
        return jnp.dot(lhs, w_a[yy, :, cols], preferred_element_type=F32)

    def block_b(at, cols):
        xx = at
        lhs = jnp.concatenate(
            [r_b[0, xx].reshape(per_b, width), r_b[1, xx].reshape(per_b, width)], axis=0
        )
        col = jnp.concatenate([col_b[:, at : at + 1], col_b[:, nx + at : nx + at + 1]], axis=0)
        return jnp.dot(lhs, w_b[xx, :, cols], preferred_element_type=F32) * col

    for xx, yy, cc in ss_peers:
        remote(
            ss_send,
            ss_recv.at[cc * nx + xx, yy],
            ss_ssem.at[cc * nx + xx, yy],
            ss_rsem.at[cc * nx + xx, yy],
            zi * 2 + cc,
            tensor_of(xx, yy),
        ).wait_recv()

    def scale_row(k):
        total = ss_recv[k, 0]
        for yy in range(1, ny):
            total = total + ss_recv[k, yy]
        return total

    scale_all = jnp.concatenate(
        [scale_row(cc * nx + xx) for cc in range(2) for xx in range(nx)], axis=0
    )
    scale_all = lax.rsqrt(scale_all / (ny * width) + EPSILON)
    pick_b = (iota((per_b, tokens), 1) == iota((per_b, tokens), 0) + xi * per_b).astype(F32)
    col_b = dot_nt(pick_b, scale_all, HIGHEST)
    where_row = iota((per_a, tokens), 0)
    wanted = (where_row // rows_owner * ny + yi) * rows_owner + where_row % rows_owner
    pick_a = (iota((per_a, tokens), 1) == wanted).astype(F32)
    scale_mine = jnp.concatenate([scale_row(xi), scale_row(nx + xi)], axis=0)
    scale_mine = lax.rsqrt(scale_mine / (ny * width) + EPSILON)
    col_a = dot_nt(pick_a, scale_mine, HIGHEST)

    weight_wait(w_a, dn_y, fill, fill, 1)
    if ny > 2:
        weight_wait(w_a, up_y, 0, fill, 3)
        opp_y = (yi + 2) % ny
        weight_wait(w_a, opp_y, 0, fill, 8)
        weight_wait(w_a, opp_y, fill, fill, 9)
    for yy, cc in y_peers():
        wait_va(yy, (cc,))
    own_a.wait()
    own_b.wait()
    wait_vb(xi, (1 - ci,))
    weight_wait(w_b, dn_x, fill, fill, 5)
    if nx > 2:
        weight_wait(w_b, up_x, 0, fill, 7)
        opp_x = (xi + 2) % nx
        weight_wait(w_b, opp_x, 0, fill, 10)
        weight_wait(w_b, opp_x, fill, fill, 11)
    for xx, cc in x_peers()[1:]:
        wait_vb(xx, (cc,))

    def oa_copy(h, xx, cc):
        return remote(
            o_a.at[h, cc, xx],
            ro_a.at[h, xi, ci],
            oa_send.at[h, xx, cc],
            oa_recv.at[h, xi, ci],
            zi * 2 + cc,
            tensor_of(xx, yi),
        )

    def ob_copy(h, yy, cc):
        return remote(
            o_b.at[h, cc, yy],
            ro_b.at[h, yi, ci],
            ob_send.at[h, yy, cc],
            ob_recv.at[h, yi, ci],
            zi * 2 + cc,
            tensor_of(xi, yy),
        )

    for h in range(2):
        cols = slice(h * half, (h + 1) * half)
        total = block_a(0, cols)
        for yy in range(1, ny):
            total = total + block_a(yy, cols)
        for cc in range(2):
            part = total[cc * per_a : (cc + 1) * per_a, :] * col_a[:, cc : cc + 1]
            o_a[h, cc] = part.astype(BF16).reshape(nx, rows_owner, half)
        for xx, cc in x_order:
            oa_copy(h, xx, cc).start()
        total = block_b(0, cols)
        for at in range(1, nx):
            total = total + block_b(at, cols)
        o_b[h] = total.astype(BF16).reshape(2, ny, rows_owner, half)
        for yy, cc in y_order:
            ob_copy(h, yy, cc).start()
    own_out = []
    for h in range(2):
        own_out.append(
            pltpu.make_async_copy(o_a.at[h, ci, xi], ro_a.at[h, xi, ci], own_sem.at[6 + h])
        )
        own_out.append(
            pltpu.make_async_copy(o_b.at[h, ci, yi], ro_b.at[h, yi, ci], own_sem.at[8 + h])
        )
    for copy in own_out:
        copy.start()
    for copy in own_out:
        copy.wait()

    def sent(rr):
        first_copy(rr).wait_send()
        second_copy(rr).wait_send()

        @pl.when(has_tail(rr))
        def _():
            first_tail(rr).wait_send()

        @pl.when(has_tail(me_r))
        def _():
            second_tail(rr).wait_send()

    each_replica(sent)
    for copy in started:
        copy.wait_send()
    for xx, yy, cc in ss_peers:
        ss_copy(xx, yy, cc).wait_send()
    for yy, cc in y_peers():
        va_copy(yy, cc).wait_send()
    for xx, cc in x_peers():
        vb_copy(xx, cc).wait_send()

    for h in range(2):
        for xx, cc in x_peers():
            remote(
                o_a.at[h, cc, xx],
                ro_a.at[h, xx, cc],
                oa_send.at[h, xx, cc],
                oa_recv.at[h, xx, cc],
                zi * 2 + cc,
                tensor_of(xx, yi),
            ).wait_recv()
        for cc in range(2):
            total = ro_a[h, 0, cc].astype(F32)
            for xx in range(1, nx):
                total = total + ro_a[h, xx, cc].astype(F32)
            lo = cc * quarter + h * half
            mixed_o[:, lo : lo + half] = total.astype(BF16)
        for yy, cc in y_peers():
            remote(
                o_b.at[h, cc, yy],
                ro_b.at[h, yy, cc],
                ob_send.at[h, yy, cc],
                ob_recv.at[h, yy, cc],
                zi * 2 + cc,
                tensor_of(xi, yy),
            ).wait_recv()
        for cc in range(2):
            total = ro_b[h, 0, cc].astype(F32)
            for yy in range(1, ny):
                total = total + ro_b[h, yy, cc].astype(F32)
            lo = half_cols + cc * quarter + h * half
            mixed_o[:, lo : lo + half] = total.astype(BF16)

    for h in range(2):
        for yy, cc in y_peers():
            ob_copy(h, yy, cc).wait_send()
        for xx, cc in x_peers():
            oa_copy(h, xx, cc).wait_send()


def store_kernel(mixed_v, final_v, mixed_o, final_o, sem):
    first = pltpu.make_async_copy(mixed_v, mixed_o, sem.at[0])
    second = pltpu.make_async_copy(final_v, final_o, sem.at[1])
    first.start()
    second.start()
    first.wait()
    second.wait()


def local(
    sizes,
    x_input,
    z_input,
    bc_input,
    dt_raw,
    dt_bias,
    decay_rates,
    skip_gain,
    conv_x,
    conv_bc,
    norm_gain,
    out_weight,
    cached_states,
    cached_tail_x,
    cached_tail_bc,
    prefix_block,
    lengths,
):
    nr, nx, ny = sizes
    tokens, width = x_input.shape
    heads = dt_raw.shape[1]
    slot = tokens // 2
    out_cols = out_weight.shape[1]
    quarter = out_cols // 4
    rows_owner = tokens // (nx * ny)
    piece = width // nr
    tail_n = min(nr, TAIL_ROWS)
    tail_p = TAIL_ROWS // tail_n
    vmem = pltpu.VMEM
    dma = pltpu.SemaphoreType.DMA
    smem = pltpu.SMEM
    hbm_spec = pl.BlockSpec(memory_space=pl.ANY)
    vmem_spec = pl.BlockSpec(memory_space=pltpu.VMEM)
    scratch = [
        smem(prefix_block.shape, jnp.int32),
        smem(lengths.shape, jnp.int32),
        smem((heads,), F32),
        smem((heads,), F32),
        smem((heads,), F32),
        vmem((tokens, width), BF16),
        vmem((tokens, width), BF16),
        vmem((tokens, 2 * STATE), BF16),
        vmem((heads, tokens), F32),
        vmem((4, width), F32),
        vmem((4, 2 * STATE), F32),
        vmem((1, width), F32),
        vmem((2, width, STATE), F32),
        vmem((3, 2, width), F32),
        vmem((3, 2, 2 * STATE), F32),
        vmem((nr, 2 * piece, STATE), BF16),
        vmem((nr, 2 * piece, STATE), BF16),
        vmem((nr, 2 * piece, STATE), BF16),
        vmem((nr, 2 * piece, STATE), BF16),
        vmem((tail_n, 2 * tail_p, STATE), BF16),
        vmem((nr, 2 * tail_p, STATE), BF16),
        vmem((nr, 2 * tail_p, STATE), BF16),
        vmem((tail_n, 2 * tail_p, STATE), BF16),
        vmem((ny, width, quarter), BF16),
        vmem((nx, width, quarter), BF16),
        vmem((2, slot, width), F32),
        vmem((2, slot, 2 * STATE), F32),
        vmem((2, slot, width), F32),
        vmem((2, heads, slot, slot), F32),
        vmem((2, slot, width), F32),
        vmem((2, slot, width), F32),
        vmem((2, width, STATE), F32),
        vmem((nx, ny, rows_owner, width), BF16),
        vmem((2, ny, nx, rows_owner, width), BF16),
        vmem((2, nx, ny, rows_owner, width), BF16),
        vmem((1, tokens), F32),
        vmem((2 * nx, ny, 1, tokens), F32),
        vmem((2, 2, nx, rows_owner, quarter // 2), BF16),
        vmem((2, 2, ny, rows_owner, quarter // 2), BF16),
        vmem((2, nx, 2, rows_owner, quarter // 2), BF16),
        vmem((2, ny, 2, rows_owner, quarter // 2), BF16),
        dma((20,)),
        dma((10,)),
        dma((nr,)),
        dma((nr,)),
        dma((nr,)),
        dma((nr,)),
        dma((nr,)),
        dma((nr,)),
        dma((nr,)),
        dma((nr,)),
        dma((12,)),
        dma((12,)),
        dma((2, ny)),
        dma((2, ny)),
        dma((2, nx)),
        dma((2, nx)),
        dma((2 * nx, ny)),
        dma((2 * nx, ny)),
        dma((2, nx, 2)),
        dma((2, nx, 2)),
        dma((2, ny, 2)),
        dma((2, ny, 2)),
    ]
    mixed, final_states = pl.pallas_call(
        functools.partial(layer_kernel, sizes),
        out_shape=(vmem((rows_owner, out_cols), BF16), vmem((2, width, STATE), F32)),
        in_specs=[hbm_spec] * 16,
        out_specs=(vmem_spec, vmem_spec),
        scratch_shapes=scratch,
        compiler_params=pltpu.CompilerParams(
            collective_id=0, has_side_effects=True, vmem_limit_bytes=56 * 1024 * 1024
        ),
        name="prefill_layer",
    )(
        prefix_block,
        lengths,
        dt_bias,
        decay_rates,
        skip_gain,
        x_input,
        z_input,
        bc_input,
        dt_raw.T,
        conv_x,
        conv_bc,
        norm_gain.reshape(1, width),
        out_weight,
        cached_states.reshape(2, width, STATE),
        jnp.transpose(cached_tail_x, (1, 0, 2)),
        jnp.transpose(cached_tail_bc, (1, 0, 2)),
    )
    mixed, final_states = pl.pallas_call(
        store_kernel,
        out_shape=(
            jax.ShapeDtypeStruct((rows_owner, out_cols), BF16),
            jax.ShapeDtypeStruct((2, width, STATE), F32),
        ),
        in_specs=[vmem_spec] * 2,
        out_specs=(hbm_spec, hbm_spec),
        scratch_shapes=[dma((2,))],
        compiler_params=pltpu.CompilerParams(vmem_limit_bytes=4 * 1024 * 1024),
        name="store_results",
    )(mixed, final_states)
    return mixed, final_states.reshape(2, heads, HEAD_DIM, STATE)


def tensor_grid(count):
    side = 1
    while side * side < count:
        side *= 2
    return side, count // side


def solution(mesh):
    placed = (
        P("replica", "tensor"),
        P("replica", "tensor"),
        P("replica", None),
        P("replica", "tensor"),
        P("tensor"),
        P("tensor"),
        P("tensor"),
        P(None, "tensor"),
        P(),
        P("tensor"),
        P("tensor", None),
        P("replica", "tensor", None, None),
        P("replica", None, "tensor"),
        P("replica", None, None),
        P(),
        P("replica"),
    )
    sizes = (mesh.shape["replica"],) + tensor_grid(mesh.shape["tensor"])
    return jax.shard_map(
        functools.partial(local, sizes),
        mesh=mesh,
        in_specs=placed,
        out_specs=(P(("replica", "tensor"), None), P("replica", "tensor", None, None)),
        check_vma=False,
    )
```

```python
import functools

import jax
import jax.numpy as jnp
from jax import lax
from jax.experimental import pallas as pl
from jax.experimental.pallas import tpu as pltpu
from jax.sharding import PartitionSpec as P

MESH = pl.DeviceIdType.MESH
HIGHEST = lax.Precision.HIGHEST
F32 = jnp.float32
BF16 = jnp.bfloat16
HEAD_DIM = 32
STATE = 128
EPSILON = 1e-05
TAIL_ROWS = 12

NT_DIMS = (((1,), (1,)), ((), ()))
TN_DIMS = (((0,), (0,)), ((), ()))


def dot_nt(a, b, precision=None):
    return lax.dot_general(a, b, NT_DIMS, precision=precision, preferred_element_type=F32)


def dot_tn(a, b, precision=None):
    return lax.dot_general(a, b, TN_DIMS, precision=precision, preferred_element_type=F32)


def iota(shape, axis):
    return lax.broadcasted_iota(jnp.int32, shape, axis)


def silu(a):
    return a / (1.0 + jnp.exp(-a))


def layer_kernel(
    sizes,
    prefix_h,
    lengths_h,
    bias_h,
    rates_h,
    skip_h,
    x_h,
    z_h,
    bc_h,
    dt_h,
    convx_h,
    convbc_h,
    gain_h,
    weight_h,
    states_h,
    tailx_h,
    tailbc_h,
    mixed_o,
    final_o,
    prefix_s,
    lengths_s,
    bias_s,
    rates_s,
    skip_s,
    x_v,
    z_v,
    bc_v,
    dt_v,
    convx_v,
    convbc_v,
    gain_v,
    st_v,
    tailx_v,
    tailbc_v,
    send1,
    recv1,
    send2,
    recv2,
    tsend1,
    trecv1,
    tsend2,
    trecv2,
    w_a,
    w_b,
    xraw,
    bcraw,
    gate,
    decay,
    expcum,
    weighin,
    ending,
    v_a,
    r_a,
    r_b,
    ss_send,
    ss_recv,
    o_a,
    o_b,
    ro_a,
    ro_b,
    load_sem,
    own_sem,
    s1_send,
    s1_recv,
    s2_send,
    s2_recv,
    t1_send,
    t1_recv,
    t2_send,
    t2_recv,
    w_send,
    w_recv,
    va_send,
    va_recv,
    vb_send,
    vb_recv,
    ss_ssem,
    ss_rsem,
    oa_send,
    oa_recv,
    ob_send,
    ob_recv,
):
    nr, nx, ny = sizes
    nz = nr // 2
    groups = nx
    tokens, width = x_v.shape
    heads = width // HEAD_DIM
    slot = tokens // 2
    rows_owner = tokens // (nx * ny)
    piece = width // nr
    tail_n = trecv2.shape[0]
    tail_p = TAIL_ROWS // tail_n
    quarter = w_a.shape[2]
    half_cols = 2 * quarter

    me_r = lax.axis_index("replica")
    me_t = lax.axis_index("tensor")
    zi, ci = me_r // 2, me_r % 2
    xi, yi = me_t // ny, me_t % ny

    def far_pair(m):
        k = (m + 1) // 2
        dz = nz // 2 + k * (1 - 2 * (m % 2))
        return (zi + dz) % nz * 2

    def each_replica(fn):
        def step(m, carry):
            base = far_pair(m)
            fn(base)
            fn(base + 1)
            return carry

        lax.fori_loop(0, nz - 1, step, 0)
        fn(zi * 2 + 1 - ci)

    def y_peers():
        out = []
        for d in range(ny):
            for dc in range(2):
                if d or dc:
                    out.append(((yi + d) % ny, (ci + dc) % 2))
        return out

    def x_peers():
        out = []
        for d in range(nx):
            for dc in range(2):
                if d or dc:
                    out.append(((xi + d) % nx, (ci + dc) % 2))
        return out

    def grid_peers():
        out = []
        for dx in range(nx):
            for dy in range(ny):
                for cc in range(2):
                    if dx or dy:
                        out.append(((xi + dx) % nx, (yi + dy) % ny, cc))
        return out

    def tensor_of(xx, yy):
        return xx * ny + yy

    def tail_slot(rr):
        return (rr * tail_n + nr - 1) // nr

    def has_tail(rr):
        return tail_slot(rr) * nr // tail_n == rr

    def remote(src, dst, ssem, rsem, rr, tt):
        return pltpu.make_async_remote_copy(
            src_ref=src,
            dst_ref=dst,
            send_sem=ssem,
            recv_sem=rsem,
            device_id=(rr, tt),
            device_id_type=MESH,
        )

    barrier = pltpu.get_barrier_semaphore()

    def greet(rr, tt):
        pl.semaphore_signal(barrier, inc=1, device_id=(rr, tt), device_id_type=MESH)

    each_replica(lambda rr: greet(rr, me_t))
    for xx, yy, cc in grid_peers():
        greet(zi * 2 + cc, tensor_of(xx, yy))
    expected = 2 * (nz - 1) + 1 + 2 * (nx * ny - 1)

    b_lo = pl.multiple_of(xi * STATE, STATE)
    c_lo = pl.multiple_of((groups + xi) * STATE, STATE)
    cols_a = pl.ds(pl.multiple_of(ci * quarter, quarter), quarter)
    cols_b = pl.ds(pl.multiple_of(half_cols + ci * quarter, quarter), quarter)
    lane_b, lane_c = pl.ds(0, STATE), pl.ds(STATE, STATE)
    loads = []

    def load(src, dst):
        copy = pltpu.make_async_copy(src, dst, load_sem.at[len(loads)])
        copy.start()
        loads.append(copy)
        return copy

    load_states = load(states_h, st_v)
    load_tx = load(tailx_h, tailx_v)
    scalars = [
        load(prefix_h, prefix_s),
        load(lengths_h, lengths_s),
        load(bias_h, bias_s),
        load(rates_h, rates_s),
        load(skip_h, skip_s),
    ]
    load_tb = load(tailbc_h.at[:, :, pl.ds(b_lo, STATE)], tailbc_v.at[:, :, lane_b])
    load_tc = load(tailbc_h.at[:, :, pl.ds(c_lo, STATE)], tailbc_v.at[:, :, lane_c])
    load_dt = load(dt_h, dt_v)
    load_x = load(x_h, x_v)
    load_b = load(bc_h.at[:, pl.ds(b_lo, STATE)], bc_v.at[:, lane_b])
    load_c = load(bc_h.at[:, pl.ds(c_lo, STATE)], bc_v.at[:, lane_c])
    load_cx = load(convx_h, convx_v)
    load_cb = load(convbc_h.at[:, pl.ds(b_lo, STATE)], convbc_v.at[:, lane_b])
    load_cc = load(convbc_h.at[:, pl.ds(c_lo, STATE)], convbc_v.at[:, lane_c])
    load_z = load(z_h, z_v)
    load_g = load(gain_h, gain_v)
    load_wa = load(weight_h.at[:, cols_a], w_a.at[yi])
    load_wb = load(weight_h.at[:, cols_b], w_b.at[xi])

    load_states.wait()
    packed = st_v[...].reshape(2, nr, piece, STATE)
    for b in range(2):
        send1[:, b * piece : (b + 1) * piece, :] = packed[b].astype(BF16)
    load_tx.wait()
    load_tb.wait()
    load_tc.wait()
    for j in range(tail_n):
        lines = []
        for b in range(2):
            for row in range(j * tail_p, (j + 1) * tail_p):
                t, part = row // 4, row % 4
                src = tailx_v if part < 2 else tailbc_v
                lanes = slice((part % 2) * STATE, (part % 2 + 1) * STATE)
                lines.append(src[t, b : b + 1, lanes])
        tsend1[j] = jnp.concatenate(lines, axis=0).astype(BF16)

    for copy in scalars:
        copy.wait()
    pl.semaphore_wait(barrier, expected)

    def first_copy(rr):
        return remote(send1.at[rr], recv1.at[me_r], s1_send.at[rr], s1_recv.at[me_r], rr, me_t)

    def first_tail(rr):
        return remote(tsend1.at[tail_slot(rr)], trecv1.at[me_r], t1_send.at[rr], t1_recv.at[me_r], rr, me_t)

    def start_first(rr):
        first_copy(rr).start()

        @pl.when(has_tail(rr))
        def _():
            first_tail(rr).start()

    each_replica(start_first)
    own1 = pltpu.make_async_copy(send1.at[me_r], recv1.at[me_r], own_sem.at[0])
    own1.start()

    @pl.when(has_tail(me_r))
    def _():
        copy = pltpu.make_async_copy(
            tsend1.at[tail_slot(me_r)], trecv1.at[me_r], own_sem.at[1]
        )
        copy.start()
        copy.wait()

    up_y, dn_y = (yi + 1) % ny, (yi + ny - 1) % ny
    up_x, dn_x = (xi + 1) % nx, (xi + nx - 1) % nx
    fill = w_a.shape[1] // 2

    def weight_copy(buf, at, lo, size, index, tt):
        ref = buf.at[at, pl.ds(lo, size), :]
        return remote(ref, ref, w_send.at[index], w_recv.at[index], me_r, tt)

    load_wa.wait()
    load_wb.wait()
    started = []

    def weight_start(copy):
        copy.start()
        started.append(copy)

    lows = (0, fill)
    for turn in range(2):
        lo, hi = lows[turn], lows[1 - turn]
        weight_start(weight_copy(w_a, yi, lo, fill, turn, tensor_of(xi, up_y)))
        weight_start(weight_copy(w_b, xi, lo, fill, 4 + turn, tensor_of(up_x, yi)))
        if ny > 2:
            weight_start(weight_copy(w_a, yi, hi, fill, 2 + turn, tensor_of(xi, dn_y)))
        if nx > 2:
            weight_start(weight_copy(w_b, xi, hi, fill, 6 + turn, tensor_of(dn_x, yi)))

    def raw_conv(seq, taps):
        total = seq * taps[3:4, :]
        at = iota(seq.shape, 0)
        for n in range(1, 4):
            moved = jnp.where(at >= n, pltpu.roll(seq, n, 0), 0.0)
            total = total + moved * taps[3 - n : 4 - n, :]
        return total

    load_x.wait()
    load_cx.wait()
    load_b.wait()
    load_c.wait()
    load_cb.wait()
    load_cc.wait()
    load_z.wait()
    for q in range(2):
        part = slice(q * slot, (q + 1) * slot)
        xraw[q] = raw_conv(x_v[part, :].astype(F32), convx_v[...])
        bcraw[q] = raw_conv(bc_v[part, :].astype(F32), convbc_v[...])
        gate[q] = silu(z_v[part, :].astype(F32))
    load_g.wait()

    def wait_first(rr):
        remote(send1.at[rr], recv1.at[rr], s1_send.at[rr], s1_recv.at[rr], rr, me_t).wait_recv()

        @pl.when(has_tail(me_r))
        def _():
            remote(
                tsend1.at[0], trecv1.at[rr], t1_send.at[0], t1_recv.at[rr], rr, me_t
            ).wait_recv()

    own1.wait()
    each_replica(wait_first)

    def pick(block):
        both = recv1[block // 2].astype(F32)
        return jnp.where(block % 2 == 1, both[piece:, :], both[:piece, :])

    def choose(rr):
        first = pick(prefix_s[2 * rr])
        second = pick(prefix_s[2 * rr + 1])
        send2[rr] = jnp.concatenate([first, second], axis=0).astype(BF16)

        @pl.when(has_tail(me_r))
        def _():
            chosen = []
            for s in range(2):
                block = prefix_s[2 * rr + s]
                both = trecv1[block // 2].astype(F32)
                chosen.append(jnp.where(block % 2 == 1, both[tail_p:, :], both[:tail_p, :]))
            tsend2[rr] = jnp.concatenate(chosen, axis=0).astype(BF16)

    def second_copy(rr):
        return remote(send2.at[rr], recv2.at[me_r], s2_send.at[rr], s2_recv.at[me_r], rr, me_t)

    def second_tail(rr):
        return remote(
            tsend2.at[rr],
            trecv2.at[tail_slot(me_r)],
            t2_send.at[rr],
            t2_recv.at[tail_slot(me_r)],
            rr,
            me_t,
        )

    def start_second(rr):
        second_copy(rr).start()

        @pl.when(has_tail(me_r))
        def _():
            second_tail(rr).start()

    def second_step(m, carry):
        base = far_pair(m)
        choose(base)
        choose(base + 1)

        @pl.when(m > 0)
        def _():
            before = far_pair(m - 1)
            start_second(before)
            start_second(before + 1)

        return carry

    lax.fori_loop(0, nz - 1, second_step, 0)
    choose(zi * 2)
    choose(zi * 2 + 1)
    start_second(far_pair(nz - 2))
    start_second(far_pair(nz - 2) + 1)
    start_second(zi * 2 + 1 - ci)
    own2 = pltpu.make_async_copy(send2.at[me_r], recv2.at[me_r], own_sem.at[2])
    own2.start()

    @pl.when(has_tail(me_r))
    def _():
        copy = pltpu.make_async_copy(
            tsend2.at[me_r], trecv2.at[tail_slot(me_r)], own_sem.at[3]
        )
        copy.start()
        copy.wait()

    def weight_wait(buf, at, lo, size, index):
        weight_copy(buf, at, lo, size, index, me_t).wait_recv()

    weight_wait(w_a, dn_y, 0, fill, 0)
    if ny > 2:
        weight_start(weight_copy(w_a, dn_y, 0, fill, 8, tensor_of(xi, up_y)))
        weight_wait(w_a, up_y, fill, fill, 2)
        weight_start(weight_copy(w_a, up_y, fill, fill, 9, tensor_of(xi, dn_y)))
    weight_wait(w_b, dn_x, 0, fill, 4)
    if nx > 2:
        weight_start(weight_copy(w_b, dn_x, 0, fill, 10, tensor_of(up_x, yi)))
        weight_wait(w_b, up_x, fill, fill, 6)
        weight_start(weight_copy(w_b, up_x, fill, fill, 11, tensor_of(dn_x, yi)))

    load_dt.wait()
    head_row = iota((heads, 1), 0)
    head_lane = iota((1, heads), 1)
    bias_col = jnp.zeros((heads, 1), F32)
    rate_col = jnp.zeros((heads, 1), F32)
    skip_row = jnp.zeros((1, heads), F32)
    for h in range(heads):
        bias_col = jnp.where(head_row == h, bias_s[h], bias_col)
        rate_col = jnp.where(head_row == h, rates_s[h], rate_col)
        skip_row = jnp.where(head_lane == h, skip_s[h], skip_row)
    spread = (iota((heads, width), 1) // HEAD_DIM == iota((heads, width), 0)).astype(F32)
    row_i = iota((slot, slot), 0)
    col_i = iota((slot, slot), 1)
    causal = row_i >= col_i
    lower = causal.astype(F32)

    for q in range(2):
        raw = dt_v[:, q * slot : (q + 1) * slot] + bias_col
        soft = jnp.maximum(raw, 0.0) + jnp.log1p(jnp.exp(-jnp.abs(raw)))
        live = iota((heads, slot), 1) < lengths_s[q]
        dt_t = jnp.where(live, soft, 0.0)
        logdec = -dt_t * rate_col
        cum = dot_nt(lower, logdec, HIGHEST)
        cum_t = dot_nt(logdec, lower, HIGHEST)
        for h in range(heads):
            differ = cum[:, h : h + 1] - cum_t[h : h + 1, :]
            value = jnp.where(causal, jnp.exp(jnp.minimum(differ, 0.0)), 0.0)
            decay[q, h] = value * dt_t[h : h + 1, :]
        expcum[q] = dot_tn(jnp.exp(cum_t), spread, HIGHEST)
        last = cum_t[:, slot - 1 : slot]
        weighin[q] = dot_tn(jnp.exp(last - cum_t) * dt_t, spread, HIGHEST)
        ending[q] = dot_tn(spread, jnp.broadcast_to(jnp.exp(last), (heads, STATE)), HIGHEST)
    skip_wide = jnp.dot(skip_row, spread, precision=HIGHEST, preferred_element_type=F32)

    def wait_second(rr):
        remote(send2.at[rr], recv2.at[rr], s2_send.at[rr], s2_recv.at[rr], rr, me_t).wait_recv()

        @pl.when(has_tail(rr))
        def _():
            remote(
                tsend2.at[0],
                trecv2.at[tail_slot(rr)],
                t2_send.at[0],
                t2_recv.at[tail_slot(rr)],
                rr,
                me_t,
            ).wait_recv()

    own2.wait()
    each_replica(wait_second)

    lane_head = iota((1, width), 1) // HEAD_DIM
    saved = []
    for q in range(2):
        start_at = recv2[...].astype(F32)[:, q * piece : (q + 1) * piece, :]
        start_at = start_at.reshape(width, STATE)
        at8 = iota((8, STATE), 0)

        def tail_tile(part):
            tile = jnp.zeros((8, STATE), F32)
            for t in range(3):
                row = t * 4 + part
                at = q * tail_p + row % tail_p
                line = trecv2[row // tail_p].astype(F32)[at : at + 1, :]
                tile = jnp.where(at8 == t, line, tile)
            return tile

        def tail_fix(tile, taps):
            total = tile * taps[0:1, :]
            rolled = jnp.where(at8 < 3, pltpu.roll(tile, 7, 0), 0.0)
            total = total + rolled * taps[1:2, :]
            rolled = jnp.where(at8 < 3, pltpu.roll(tile, 6, 0), 0.0)
            return total + rolled * taps[2:3, :]

        for part in range(2):
            lanes = slice(part * STATE, (part + 1) * STATE)
            xraw[q, 0:8, lanes] += tail_fix(tail_tile(part), convx_v[:, lanes])
            bcraw[q, 0:8, lanes] += tail_fix(tail_tile(part + 2), convbc_v[:, lanes])
        xc = silu(xraw[q])
        bcc = silu(bcraw[q])
        b_low = bcc[:, :STATE].astype(BF16)
        c_low = bcc[:, STATE:].astype(BF16)
        scores = dot_nt(c_low, b_low)
        y = expcum[q] * dot_nt(c_low, start_at.astype(BF16)) + skip_wide * xc
        for hp in range(heads // 2):
            left, right = 2 * hp, 2 * hp + 1
            mixing = jnp.concatenate([scores * decay[q, left], scores * decay[q, right]], axis=1)
            held = jnp.concatenate(
                [jnp.where(lane_head == left, xc, 0.0), jnp.where(lane_head == right, xc, 0.0)],
                axis=0,
            )
            y = y + jnp.dot(mixing.astype(BF16), held.astype(BF16), preferred_element_type=F32)
        v = y * gate[q]
        ss_send[:, q * slot : (q + 1) * slot] = dot_nt(
            jnp.ones((8, width), F32), v * v, HIGHEST
        )[0:1]
        live = iota((slot, width), 0) < lengths_s[q]
        v = jnp.where(live, v * gain_v[...], 0.0)
        owners = slot // rows_owner // ny
        v_a[q * owners : (q + 1) * owners] = v.astype(BF16).reshape(owners, ny, rows_owner, width)
        saved.append((start_at, xc, b_low))

    def ss_copy(xx, yy, cc):
        return remote(
            ss_send,
            ss_recv.at[ci * nx + xi, yi],
            ss_ssem.at[cc * nx + xx, yy],
            ss_rsem.at[ci * nx + xi, yi],
            zi * 2 + cc,
            tensor_of(xx, yy),
        )

    def va_copy(yy, cc):
        return remote(
            v_a.at[:, yy],
            r_a.at[ci, yi],
            va_send.at[cc, yy],
            va_recv.at[ci, yi],
            zi * 2 + cc,
            tensor_of(xi, yy),
        )

    def vb_copy(xx, cc):
        return remote(
            v_a.at[xx],
            r_b.at[ci, xi],
            vb_send.at[cc, xx],
            vb_recv.at[ci, xi],
            zi * 2 + cc,
            tensor_of(xx, yi),
        )

    ss_peers = grid_peers() + [(xi, yi, 1 - ci)]
    for xx, yy, cc in ss_peers:
        ss_copy(xx, yy, cc).start()
    for d in (2, 1, 3):
        if d < ny:
            va_copy((yi + d) % ny, ci).start()
        if d < nx:
            vb_copy((xi + d) % nx, ci).start()
    va_copy(yi, 1 - ci).start()
    vb_copy(xi, 1 - ci).start()
    ss_recv[ci * nx + xi, yi] = ss_send[...]
    own_a = pltpu.make_async_copy(v_a.at[:, yi], r_a.at[ci, yi], own_sem.at[4])
    own_a.start()
    own_b = pltpu.make_async_copy(v_a.at[xi], r_b.at[ci, xi], own_sem.at[5])
    own_b.start()

    for q in range(2):
        start_at, xc, b_low = saved[q]
        weighed = (xc * weighin[q]).astype(BF16)
        final_o[q] = ending[q] * start_at + dot_tn(weighed, b_low)

    per_a = nx * rows_owner
    per_b = ny * rows_owner

    half = quarter // 2
    x_order = x_peers()[::-1]
    y_order = y_peers()[::-1]
    if nx > 2:
        x_order = [((xi + d) % nx, (ci + e) % 2) for d in (2, 1, 3) for e in range(2)]
        x_order.append((xi, 1 - ci))
    if ny > 2:
        y_order = [((yi + d) % ny, (ci + e) % 2) for d in (2, 1, 3) for e in range(2)]
        y_order.append((yi, 1 - ci))

    def block_a(yy, cols):
        lhs = jnp.concatenate(
            [r_a[0, yy].reshape(per_a, width), r_a[1, yy].reshape(per_a, width)], axis=0
        )
        return jnp.dot(lhs, w_a[yy, :, cols], preferred_element_type=F32)

    def block_b(at, cols):
        xx = at
        lhs = jnp.concatenate(
            [r_b[0, xx].reshape(per_b, width), r_b[1, xx].reshape(per_b, width)], axis=0
        )
        col = jnp.concatenate([col_b[:, at : at + 1], col_b[:, nx + at : nx + at + 1]], axis=0)
        return jnp.dot(lhs, w_b[xx, :, cols], preferred_element_type=F32) * col

    def wait_va(yy, cores):
        for cc in cores:
            remote(
                v_a.at[:, yi],
                r_a.at[cc, yy],
                va_send.at[cc, yy],
                va_recv.at[cc, yy],
                zi * 2 + cc,
                tensor_of(xi, yy),
            ).wait_recv()

    def wait_vb(xx, cores):
        for cc in cores:
            remote(
                v_a.at[xi],
                r_b.at[cc, xx],
                vb_send.at[cc, xx],
                vb_recv.at[cc, xx],
                zi * 2 + cc,
                tensor_of(xx, yi),
            ).wait_recv()

    handed = []

    def hand_on(buf, at, ssem, rsem):
        ref = buf.at[ci, at]
        copy = remote(ref, ref, ssem.at[1 - ci, at], rsem.at[ci, at], zi * 2 + 1 - ci, me_t)
        copy.start()
        handed.append(copy)

    for d in (1, 3, 2):
        if d < ny:
            yy = (yi + d) % ny
            wait_va(yy, (ci,))
            hand_on(r_a, yy, va_send, va_recv)
        if d < nx:
            xx = (xi + d) % nx
            wait_vb(xx, (ci,))
            hand_on(r_b, xx, vb_send, vb_recv)

    for xx, yy, cc in ss_peers:
        remote(
            ss_send,
            ss_recv.at[cc * nx + xx, yy],
            ss_ssem.at[cc * nx + xx, yy],
            ss_rsem.at[cc * nx + xx, yy],
            zi * 2 + cc,
            tensor_of(xx, yy),
        ).wait_recv()

    def scale_row(k):
        total = ss_recv[k, 0]
        for yy in range(1, ny):
            total = total + ss_recv[k, yy]
        return total

    scale_all = jnp.concatenate(
        [scale_row(cc * nx + xx) for cc in range(2) for xx in range(nx)], axis=0
    )
    scale_all = lax.rsqrt(scale_all / (ny * width) + EPSILON)
    pick_b = (iota((per_b, tokens), 1) == iota((per_b, tokens), 0) + xi * per_b).astype(F32)
    col_b = dot_nt(pick_b, scale_all, HIGHEST)
    where_row = iota((per_a, tokens), 0)
    wanted = (where_row // rows_owner * ny + yi) * rows_owner + where_row % rows_owner
    pick_a = (iota((per_a, tokens), 1) == wanted).astype(F32)
    scale_mine = jnp.concatenate([scale_row(xi), scale_row(nx + xi)], axis=0)
    scale_mine = lax.rsqrt(scale_mine / (ny * width) + EPSILON)
    col_a = dot_nt(pick_a, scale_mine, HIGHEST)

    weight_wait(w_a, dn_y, fill, fill, 1)
    if ny > 2:
        weight_wait(w_a, up_y, 0, fill, 3)
        opp_y = (yi + 2) % ny
        weight_wait(w_a, opp_y, 0, fill, 8)
        weight_wait(w_a, opp_y, fill, fill, 9)
    for d in range(ny):
        wait_va((yi + d) % ny, (1 - ci,))
    own_a.wait()
    own_b.wait()
    wait_vb(xi, (1 - ci,))
    weight_wait(w_b, dn_x, fill, fill, 5)
    if nx > 2:
        weight_wait(w_b, up_x, 0, fill, 7)
        opp_x = (xi + 2) % nx
        weight_wait(w_b, opp_x, 0, fill, 10)
        weight_wait(w_b, opp_x, fill, fill, 11)
    for d in range(1, nx):
        wait_vb((xi + d) % nx, (1 - ci,))

    def oa_copy(h, xx, cc):
        return remote(
            o_a.at[h, cc, xx],
            ro_a.at[h, xi, ci],
            oa_send.at[h, xx, cc],
            oa_recv.at[h, xi, ci],
            zi * 2 + cc,
            tensor_of(xx, yi),
        )

    def ob_copy(h, yy, cc):
        return remote(
            o_b.at[h, cc, yy],
            ro_b.at[h, yi, ci],
            ob_send.at[h, yy, cc],
            ob_recv.at[h, yi, ci],
            zi * 2 + cc,
            tensor_of(xi, yy),
        )

    for h in range(2):
        cols = slice(h * half, (h + 1) * half)
        total = block_a(0, cols)
        for yy in range(1, ny):
            total = total + block_a(yy, cols)
        for cc in range(2):
            part = total[cc * per_a : (cc + 1) * per_a, :] * col_a[:, cc : cc + 1]
            o_a[h, cc] = part.astype(BF16).reshape(nx, rows_owner, half)
        for xx, cc in x_order:
            oa_copy(h, xx, cc).start()
        total = block_b(0, cols)
        for at in range(1, nx):
            total = total + block_b(at, cols)
        o_b[h] = total.astype(BF16).reshape(2, ny, rows_owner, half)
        for yy, cc in y_order:
            ob_copy(h, yy, cc).start()
    own_out = []
    for h in range(2):
        own_out.append(
            pltpu.make_async_copy(o_a.at[h, ci, xi], ro_a.at[h, xi, ci], own_sem.at[6 + h])
        )
        own_out.append(
            pltpu.make_async_copy(o_b.at[h, ci, yi], ro_b.at[h, yi, ci], own_sem.at[8 + h])
        )
    for copy in own_out:
        copy.start()
    for copy in own_out:
        copy.wait()

    def sent(rr):
        first_copy(rr).wait_send()
        second_copy(rr).wait_send()

        @pl.when(has_tail(rr))
        def _():
            first_tail(rr).wait_send()

        @pl.when(has_tail(me_r))
        def _():
            second_tail(rr).wait_send()

    each_replica(sent)
    for copy in started:
        copy.wait_send()
    for xx, yy, cc in ss_peers:
        ss_copy(xx, yy, cc).wait_send()
    for d in range(1, ny):
        va_copy((yi + d) % ny, ci).wait_send()
    for d in range(1, nx):
        vb_copy((xi + d) % nx, ci).wait_send()
    va_copy(yi, 1 - ci).wait_send()
    vb_copy(xi, 1 - ci).wait_send()
    for copy in handed:
        copy.wait_send()

    for h in range(2):
        for xx, cc in x_peers():
            remote(
                o_a.at[h, cc, xx],
                ro_a.at[h, xx, cc],
                oa_send.at[h, xx, cc],
                oa_recv.at[h, xx, cc],
                zi * 2 + cc,
                tensor_of(xx, yi),
            ).wait_recv()
        for cc in range(2):
            total = ro_a[h, 0, cc].astype(F32)
            for xx in range(1, nx):
                total = total + ro_a[h, xx, cc].astype(F32)
            lo = cc * quarter + h * half
            mixed_o[:, lo : lo + half] = total.astype(BF16)
        for yy, cc in y_peers():
            remote(
                o_b.at[h, cc, yy],
                ro_b.at[h, yy, cc],
                ob_send.at[h, yy, cc],
                ob_recv.at[h, yy, cc],
                zi * 2 + cc,
                tensor_of(xi, yy),
            ).wait_recv()
        for cc in range(2):
            total = ro_b[h, 0, cc].astype(F32)
            for yy in range(1, ny):
                total = total + ro_b[h, yy, cc].astype(F32)
            lo = half_cols + cc * quarter + h * half
            mixed_o[:, lo : lo + half] = total.astype(BF16)

    for h in range(2):
        for yy, cc in y_peers():
            ob_copy(h, yy, cc).wait_send()
        for xx, cc in x_peers():
            oa_copy(h, xx, cc).wait_send()


def store_kernel(mixed_v, final_v, mixed_o, final_o, sem):
    first = pltpu.make_async_copy(mixed_v, mixed_o, sem.at[0])
    second = pltpu.make_async_copy(final_v, final_o, sem.at[1])
    first.start()
    second.start()
    first.wait()
    second.wait()


def local(
    sizes,
    x_input,
    z_input,
    bc_input,
    dt_raw,
    dt_bias,
    decay_rates,
    skip_gain,
    conv_x,
    conv_bc,
    norm_gain,
    out_weight,
    cached_states,
    cached_tail_x,
    cached_tail_bc,
    prefix_block,
    lengths,
):
    nr, nx, ny = sizes
    tokens, width = x_input.shape
    heads = dt_raw.shape[1]
    slot = tokens // 2
    out_cols = out_weight.shape[1]
    quarter = out_cols // 4
    rows_owner = tokens // (nx * ny)
    piece = width // nr
    tail_n = min(nr, TAIL_ROWS)
    tail_p = TAIL_ROWS // tail_n
    vmem = pltpu.VMEM
    dma = pltpu.SemaphoreType.DMA
    smem = pltpu.SMEM
    hbm_spec = pl.BlockSpec(memory_space=pl.ANY)
    vmem_spec = pl.BlockSpec(memory_space=pltpu.VMEM)
    scratch = [
        smem(prefix_block.shape, jnp.int32),
        smem(lengths.shape, jnp.int32),
        smem((heads,), F32),
        smem((heads,), F32),
        smem((heads,), F32),
        vmem((tokens, width), BF16),
        vmem((tokens, width), BF16),
        vmem((tokens, 2 * STATE), BF16),
        vmem((heads, tokens), F32),
        vmem((4, width), F32),
        vmem((4, 2 * STATE), F32),
        vmem((1, width), F32),
        vmem((2, width, STATE), F32),
        vmem((3, 2, width), F32),
        vmem((3, 2, 2 * STATE), F32),
        vmem((nr, 2 * piece, STATE), BF16),
        vmem((nr, 2 * piece, STATE), BF16),
        vmem((nr, 2 * piece, STATE), BF16),
        vmem((nr, 2 * piece, STATE), BF16),
        vmem((tail_n, 2 * tail_p, STATE), BF16),
        vmem((nr, 2 * tail_p, STATE), BF16),
        vmem((nr, 2 * tail_p, STATE), BF16),
        vmem((tail_n, 2 * tail_p, STATE), BF16),
        vmem((ny, width, quarter), BF16),
        vmem((nx, width, quarter), BF16),
        vmem((2, slot, width), F32),
        vmem((2, slot, 2 * STATE), F32),
        vmem((2, slot, width), F32),
        vmem((2, heads, slot, slot), F32),
        vmem((2, slot, width), F32),
        vmem((2, slot, width), F32),
        vmem((2, width, STATE), F32),
        vmem((nx, ny, rows_owner, width), BF16),
        vmem((2, ny, nx, rows_owner, width), BF16),
        vmem((2, nx, ny, rows_owner, width), BF16),
        vmem((1, tokens), F32),
        vmem((2 * nx, ny, 1, tokens), F32),
        vmem((2, 2, nx, rows_owner, quarter // 2), BF16),
        vmem((2, 2, ny, rows_owner, quarter // 2), BF16),
        vmem((2, nx, 2, rows_owner, quarter // 2), BF16),
        vmem((2, ny, 2, rows_owner, quarter // 2), BF16),
        dma((20,)),
        dma((10,)),
        dma((nr,)),
        dma((nr,)),
        dma((nr,)),
        dma((nr,)),
        dma((nr,)),
        dma((nr,)),
        dma((nr,)),
        dma((nr,)),
        dma((12,)),
        dma((12,)),
        dma((2, ny)),
        dma((2, ny)),
        dma((2, nx)),
        dma((2, nx)),
        dma((2 * nx, ny)),
        dma((2 * nx, ny)),
        dma((2, nx, 2)),
        dma((2, nx, 2)),
        dma((2, ny, 2)),
        dma((2, ny, 2)),
    ]
    mixed, final_states = pl.pallas_call(
        functools.partial(layer_kernel, sizes),
        out_shape=(vmem((rows_owner, out_cols), BF16), vmem((2, width, STATE), F32)),
        in_specs=[hbm_spec] * 16,
        out_specs=(vmem_spec, vmem_spec),
        scratch_shapes=scratch,
        compiler_params=pltpu.CompilerParams(
            collective_id=0, has_side_effects=True, vmem_limit_bytes=56 * 1024 * 1024
        ),
        name="prefill_layer",
    )(
        prefix_block,
        lengths,
        dt_bias,
        decay_rates,
        skip_gain,
        x_input,
        z_input,
        bc_input,
        dt_raw.T,
        conv_x,
        conv_bc,
        norm_gain.reshape(1, width),
        out_weight,
        cached_states.reshape(2, width, STATE),
        jnp.transpose(cached_tail_x, (1, 0, 2)),
        jnp.transpose(cached_tail_bc, (1, 0, 2)),
    )
    mixed, final_states = pl.pallas_call(
        store_kernel,
        out_shape=(
            jax.ShapeDtypeStruct((rows_owner, out_cols), BF16),
            jax.ShapeDtypeStruct((2, width, STATE), F32),
        ),
        in_specs=[vmem_spec] * 2,
        out_specs=(hbm_spec, hbm_spec),
        scratch_shapes=[dma((2,))],
        compiler_params=pltpu.CompilerParams(vmem_limit_bytes=4 * 1024 * 1024),
        name="store_results",
    )(mixed, final_states)
    return mixed, final_states.reshape(2, heads, HEAD_DIM, STATE)


def tensor_grid(count):
    side = 1
    while side * side < count:
        side *= 2
    return side, count // side


def solution(mesh):
    placed = (
        P("replica", "tensor"),
        P("replica", "tensor"),
        P("replica", None),
        P("replica", "tensor"),
        P("tensor"),
        P("tensor"),
        P("tensor"),
        P(None, "tensor"),
        P(),
        P("tensor"),
        P("tensor", None),
        P("replica", "tensor", None, None),
        P("replica", None, "tensor"),
        P("replica", None, None),
        P(),
        P("replica"),
    )
    sizes = (mesh.shape["replica"],) + tensor_grid(mesh.shape["tensor"])
    return jax.shard_map(
        functools.partial(local, sizes),
        mesh=mesh,
        in_specs=placed,
        out_specs=(P(("replica", "tensor"), None), P("replica", "tensor", None, None)),
        check_vma=False,
    )
```

```python
import functools

import jax
import jax.numpy as jnp
from jax import lax
from jax.experimental import pallas as pl
from jax.experimental.pallas import tpu as pltpu
from jax.sharding import PartitionSpec as P

MESH = pl.DeviceIdType.MESH
HIGHEST = lax.Precision.HIGHEST
F32 = jnp.float32
BF16 = jnp.bfloat16
HEAD_DIM = 32
STATE = 128
EPSILON = 1e-05
TAIL_ROWS = 12

NT_DIMS = (((1,), (1,)), ((), ()))
TN_DIMS = (((0,), (0,)), ((), ()))


def dot_nt(a, b, precision=None):
    return lax.dot_general(a, b, NT_DIMS, precision=precision, preferred_element_type=F32)


def dot_tn(a, b, precision=None):
    return lax.dot_general(a, b, TN_DIMS, precision=precision, preferred_element_type=F32)


def iota(shape, axis):
    return lax.broadcasted_iota(jnp.int32, shape, axis)


def silu(a):
    return a / (1.0 + jnp.exp(-a))


def layer_kernel(
    sizes,
    prefix_h,
    lengths_h,
    bias_h,
    rates_h,
    skip_h,
    x_h,
    z_h,
    bc_h,
    dt_h,
    convx_h,
    convbc_h,
    gain_h,
    weight_h,
    states_h,
    tailx_h,
    tailbc_h,
    mixed_o,
    final_o,
    prefix_s,
    lengths_s,
    bias_s,
    rates_s,
    skip_s,
    x_v,
    z_v,
    bc_v,
    dt_v,
    convx_v,
    convbc_v,
    gain_v,
    st_v,
    tailx_v,
    tailbc_v,
    send1,
    recv1,
    send2,
    recv2,
    tsend1,
    trecv1,
    tsend2,
    trecv2,
    w_a,
    w_b,
    xraw,
    bcraw,
    gate,
    decay,
    expcum,
    weighin,
    ending,
    v_a,
    r_a,
    r_b,
    ss_send,
    ss_recv,
    o_a,
    o_b,
    ro_a,
    ro_b,
    load_sem,
    own_sem,
    s1_send,
    s1_recv,
    s2_send,
    s2_recv,
    t1_send,
    t1_recv,
    t2_send,
    t2_recv,
    w_send,
    w_recv,
    va_send,
    va_recv,
    vb_send,
    vb_recv,
    ss_ssem,
    ss_rsem,
    oa_send,
    oa_recv,
    ob_send,
    ob_recv,
):
    nr, nx, ny = sizes
    nz = nr // 2
    groups = nx
    tokens, width = x_v.shape
    heads = width // HEAD_DIM
    slot = tokens // 2
    rows_owner = tokens // (nx * ny)
    piece = width // nr
    tail_n = trecv2.shape[0]
    tail_p = TAIL_ROWS // tail_n
    quarter = w_a.shape[2]
    half_cols = 2 * quarter

    me_r = lax.axis_index("replica")
    me_t = lax.axis_index("tensor")
    zi, ci = me_r // 2, me_r % 2
    xi, yi = me_t // ny, me_t % ny

    def far_pair(m):
        k = (m + 1) // 2
        dz = nz // 2 + k * (1 - 2 * (m % 2))
        return (zi + dz) % nz * 2

    def each_replica(fn):
        def step(m, carry):
            base = far_pair(m)
            fn(base)
            fn(base + 1)
            return carry

        lax.fori_loop(0, nz - 1, step, 0)
        fn(zi * 2 + 1 - ci)

    def y_peers():
        out = []
        for d in range(ny):
            for dc in range(2):
                if d or dc:
                    out.append(((yi + d) % ny, (ci + dc) % 2))
        return out

    def x_peers():
        out = []
        for d in range(nx):
            for dc in range(2):
                if d or dc:
                    out.append(((xi + d) % nx, (ci + dc) % 2))
        return out

    def grid_peers():
        out = []
        for dx in range(nx):
            for dy in range(ny):
                for cc in range(2):
                    if dx or dy:
                        out.append(((xi + dx) % nx, (yi + dy) % ny, cc))
        return out

    def tensor_of(xx, yy):
        return xx * ny + yy

    def tail_slot(rr):
        return (rr * tail_n + nr - 1) // nr

    def has_tail(rr):
        return tail_slot(rr) * nr // tail_n == rr

    def remote(src, dst, ssem, rsem, rr, tt):
        return pltpu.make_async_remote_copy(
            src_ref=src,
            dst_ref=dst,
            send_sem=ssem,
            recv_sem=rsem,
            device_id=(rr, tt),
            device_id_type=MESH,
        )

    barrier = pltpu.get_barrier_semaphore()

    def greet(rr, tt):
        pl.semaphore_signal(barrier, inc=1, device_id=(rr, tt), device_id_type=MESH)

    each_replica(lambda rr: greet(rr, me_t))
    for xx, yy, cc in grid_peers():
        greet(zi * 2 + cc, tensor_of(xx, yy))
    expected = 2 * (nz - 1) + 1 + 2 * (nx * ny - 1)

    b_lo = pl.multiple_of(xi * STATE, STATE)
    c_lo = pl.multiple_of((groups + xi) * STATE, STATE)
    cols_a = pl.ds(pl.multiple_of(ci * quarter, quarter), quarter)
    cols_b = pl.ds(pl.multiple_of(half_cols + ci * quarter, quarter), quarter)
    lane_b, lane_c = pl.ds(0, STATE), pl.ds(STATE, STATE)
    loads = []

    def load(src, dst):
        copy = pltpu.make_async_copy(src, dst, load_sem.at[len(loads)])
        copy.start()
        loads.append(copy)
        return copy

    load_states = load(states_h, st_v)
    load_tx = load(tailx_h, tailx_v)
    scalars = [
        load(prefix_h, prefix_s),
        load(lengths_h, lengths_s),
        load(bias_h, bias_s),
        load(rates_h, rates_s),
        load(skip_h, skip_s),
    ]
    load_tb = load(tailbc_h.at[:, :, pl.ds(b_lo, STATE)], tailbc_v.at[:, :, lane_b])
    load_tc = load(tailbc_h.at[:, :, pl.ds(c_lo, STATE)], tailbc_v.at[:, :, lane_c])
    load_dt = load(dt_h, dt_v)
    load_x = load(x_h, x_v)
    load_b = load(bc_h.at[:, pl.ds(b_lo, STATE)], bc_v.at[:, lane_b])
    load_c = load(bc_h.at[:, pl.ds(c_lo, STATE)], bc_v.at[:, lane_c])
    load_cx = load(convx_h, convx_v)
    load_cb = load(convbc_h.at[:, pl.ds(b_lo, STATE)], convbc_v.at[:, lane_b])
    load_cc = load(convbc_h.at[:, pl.ds(c_lo, STATE)], convbc_v.at[:, lane_c])
    load_z = load(z_h, z_v)
    load_g = load(gain_h, gain_v)
    load_wa = load(weight_h.at[:, cols_a], w_a.at[yi])
    load_wb = load(weight_h.at[:, cols_b], w_b.at[xi])

    load_states.wait()
    packed = st_v[...].reshape(2, nr, piece, STATE)
    for b in range(2):
        send1[:, b * piece : (b + 1) * piece, :] = packed[b].astype(BF16)
    load_tx.wait()
    load_tb.wait()
    load_tc.wait()
    for j in range(tail_n):
        lines = []
        for b in range(2):
            for row in range(j * tail_p, (j + 1) * tail_p):
                t, part = row // 4, row % 4
                src = tailx_v if part < 2 else tailbc_v
                lanes = slice((part % 2) * STATE, (part % 2 + 1) * STATE)
                lines.append(src[t, b : b + 1, lanes])
        tsend1[j] = jnp.concatenate(lines, axis=0).astype(BF16)

    for copy in scalars:
        copy.wait()
    pl.semaphore_wait(barrier, expected)

    def first_copy(rr):
        return remote(send1.at[rr], recv1.at[me_r], s1_send.at[rr], s1_recv.at[me_r], rr, me_t)

    def first_tail(rr):
        return remote(tsend1.at[tail_slot(rr)], trecv1.at[me_r], t1_send.at[rr], t1_recv.at[me_r], rr, me_t)

    def start_first(rr):
        first_copy(rr).start()

        @pl.when(has_tail(rr))
        def _():
            first_tail(rr).start()

    each_replica(start_first)
    own1 = pltpu.make_async_copy(send1.at[me_r], recv1.at[me_r], own_sem.at[0])
    own1.start()

    @pl.when(has_tail(me_r))
    def _():
        copy = pltpu.make_async_copy(
            tsend1.at[tail_slot(me_r)], trecv1.at[me_r], own_sem.at[1]
        )
        copy.start()
        copy.wait()

    up_y, dn_y = (yi + 1) % ny, (yi + ny - 1) % ny
    up_x, dn_x = (xi + 1) % nx, (xi + nx - 1) % nx
    fill = w_a.shape[1] // 2

    def weight_copy(buf, at, lo, size, index, tt):
        ref = buf.at[at, pl.ds(lo, size), :]
        return remote(ref, ref, w_send.at[index], w_recv.at[index], me_r, tt)

    load_wa.wait()
    load_wb.wait()
    started = []

    def weight_start(copy):
        copy.start()
        started.append(copy)

    lows = (0, fill)
    for turn in range(2):
        lo, hi = lows[turn], lows[1 - turn]
        weight_start(weight_copy(w_a, yi, lo, fill, turn, tensor_of(xi, up_y)))
        weight_start(weight_copy(w_b, xi, lo, fill, 4 + turn, tensor_of(up_x, yi)))
        if ny > 2:
            weight_start(weight_copy(w_a, yi, hi, fill, 2 + turn, tensor_of(xi, dn_y)))
        if nx > 2:
            weight_start(weight_copy(w_b, xi, hi, fill, 6 + turn, tensor_of(dn_x, yi)))

    def raw_conv(seq, taps):
        total = seq * taps[3:4, :]
        at = iota(seq.shape, 0)
        for n in range(1, 4):
            moved = jnp.where(at >= n, pltpu.roll(seq, n, 0), 0.0)
            total = total + moved * taps[3 - n : 4 - n, :]
        return total

    load_x.wait()
    load_cx.wait()
    load_b.wait()
    load_c.wait()
    load_cb.wait()
    load_cc.wait()
    load_z.wait()
    for q in range(2):
        part = slice(q * slot, (q + 1) * slot)
        xraw[q] = raw_conv(x_v[part, :].astype(F32), convx_v[...])
        bcraw[q] = raw_conv(bc_v[part, :].astype(F32), convbc_v[...])
        gate[q] = silu(z_v[part, :].astype(F32))
    load_g.wait()

    def wait_first(rr):
        remote(send1.at[rr], recv1.at[rr], s1_send.at[rr], s1_recv.at[rr], rr, me_t).wait_recv()

        @pl.when(has_tail(me_r))
        def _():
            remote(
                tsend1.at[0], trecv1.at[rr], t1_send.at[0], t1_recv.at[rr], rr, me_t
            ).wait_recv()

    own1.wait()
    each_replica(wait_first)

    def pick(block):
        both = recv1[block // 2].astype(F32)
        return jnp.where(block % 2 == 1, both[piece:, :], both[:piece, :])

    def choose(rr):
        first = pick(prefix_s[2 * rr])
        second = pick(prefix_s[2 * rr + 1])
        send2[rr] = jnp.concatenate([first, second], axis=0).astype(BF16)

        @pl.when(has_tail(me_r))
        def _():
            chosen = []
            for s in range(2):
                block = prefix_s[2 * rr + s]
                both = trecv1[block // 2].astype(F32)
                chosen.append(jnp.where(block % 2 == 1, both[tail_p:, :], both[:tail_p, :]))
            tsend2[rr] = jnp.concatenate(chosen, axis=0).astype(BF16)

    def second_copy(rr):
        return remote(send2.at[rr], recv2.at[me_r], s2_send.at[rr], s2_recv.at[me_r], rr, me_t)

    def second_tail(rr):
        return remote(
            tsend2.at[rr],
            trecv2.at[tail_slot(me_r)],
            t2_send.at[rr],
            t2_recv.at[tail_slot(me_r)],
            rr,
            me_t,
        )

    def start_second(rr):
        second_copy(rr).start()

        @pl.when(has_tail(me_r))
        def _():
            second_tail(rr).start()

    def second_step(m, carry):
        base = far_pair(m)
        choose(base)
        choose(base + 1)

        @pl.when(m > 0)
        def _():
            before = far_pair(m - 1)
            start_second(before)
            start_second(before + 1)

        return carry

    lax.fori_loop(0, nz - 1, second_step, 0)
    choose(zi * 2)
    choose(zi * 2 + 1)
    start_second(far_pair(nz - 2))
    start_second(far_pair(nz - 2) + 1)
    start_second(zi * 2 + 1 - ci)
    own2 = pltpu.make_async_copy(send2.at[me_r], recv2.at[me_r], own_sem.at[2])
    own2.start()

    @pl.when(has_tail(me_r))
    def _():
        copy = pltpu.make_async_copy(
            tsend2.at[me_r], trecv2.at[tail_slot(me_r)], own_sem.at[3]
        )
        copy.start()
        copy.wait()

    def weight_wait(buf, at, lo, size, index):
        weight_copy(buf, at, lo, size, index, me_t).wait_recv()

    weight_wait(w_a, dn_y, 0, fill, 0)
    if ny > 2:
        weight_start(weight_copy(w_a, dn_y, 0, fill, 8, tensor_of(xi, up_y)))
        weight_wait(w_a, up_y, fill, fill, 2)
        weight_start(weight_copy(w_a, up_y, fill, fill, 9, tensor_of(xi, dn_y)))
    weight_wait(w_b, dn_x, 0, fill, 4)
    if nx > 2:
        weight_start(weight_copy(w_b, dn_x, 0, fill, 10, tensor_of(up_x, yi)))
        weight_wait(w_b, up_x, fill, fill, 6)
        weight_start(weight_copy(w_b, up_x, fill, fill, 11, tensor_of(dn_x, yi)))

    load_dt.wait()
    head_row = iota((heads, 1), 0)
    head_lane = iota((1, heads), 1)
    bias_col = jnp.zeros((heads, 1), F32)
    rate_col = jnp.zeros((heads, 1), F32)
    skip_row = jnp.zeros((1, heads), F32)
    for h in range(heads):
        bias_col = jnp.where(head_row == h, bias_s[h], bias_col)
        rate_col = jnp.where(head_row == h, rates_s[h], rate_col)
        skip_row = jnp.where(head_lane == h, skip_s[h], skip_row)
    spread = (iota((heads, width), 1) // HEAD_DIM == iota((heads, width), 0)).astype(F32)
    row_i = iota((slot, slot), 0)
    col_i = iota((slot, slot), 1)
    causal = row_i >= col_i
    lower = causal.astype(F32)

    for q in range(2):
        raw = dt_v[:, q * slot : (q + 1) * slot] + bias_col
        soft = jnp.maximum(raw, 0.0) + jnp.log1p(jnp.exp(-jnp.abs(raw)))
        live = iota((heads, slot), 1) < lengths_s[q]
        dt_t = jnp.where(live, soft, 0.0)
        logdec = -dt_t * rate_col
        cum = dot_nt(lower, logdec, HIGHEST)
        cum_t = dot_nt(logdec, lower, HIGHEST)
        for h in range(heads):
            differ = cum[:, h : h + 1] - cum_t[h : h + 1, :]
            value = jnp.where(causal, jnp.exp(jnp.minimum(differ, 0.0)), 0.0)
            decay[q, h] = value * dt_t[h : h + 1, :]
        expcum[q] = dot_tn(jnp.exp(cum_t), spread, HIGHEST)
        last = cum_t[:, slot - 1 : slot]
        weighin[q] = dot_tn(jnp.exp(last - cum_t) * dt_t, spread, HIGHEST)
        ending[q] = dot_tn(spread, jnp.broadcast_to(jnp.exp(last), (heads, STATE)), HIGHEST)
    skip_wide = jnp.dot(skip_row, spread, precision=HIGHEST, preferred_element_type=F32)

    def wait_second(rr):
        remote(send2.at[rr], recv2.at[rr], s2_send.at[rr], s2_recv.at[rr], rr, me_t).wait_recv()

        @pl.when(has_tail(rr))
        def _():
            remote(
                tsend2.at[0],
                trecv2.at[tail_slot(rr)],
                t2_send.at[0],
                t2_recv.at[tail_slot(rr)],
                rr,
                me_t,
            ).wait_recv()

    own2.wait()
    each_replica(wait_second)

    lane_head = iota((1, width), 1) // HEAD_DIM
    saved = []
    for q in range(2):
        start_at = recv2[...].astype(F32)[:, q * piece : (q + 1) * piece, :]
        start_at = start_at.reshape(width, STATE)
        at8 = iota((8, STATE), 0)

        def tail_tile(part):
            tile = jnp.zeros((8, STATE), F32)
            for t in range(3):
                row = t * 4 + part
                at = q * tail_p + row % tail_p
                line = trecv2[row // tail_p].astype(F32)[at : at + 1, :]
                tile = jnp.where(at8 == t, line, tile)
            return tile

        def tail_fix(tile, taps):
            total = tile * taps[0:1, :]
            rolled = jnp.where(at8 < 3, pltpu.roll(tile, 7, 0), 0.0)
            total = total + rolled * taps[1:2, :]
            rolled = jnp.where(at8 < 3, pltpu.roll(tile, 6, 0), 0.0)
            return total + rolled * taps[2:3, :]

        for part in range(2):
            lanes = slice(part * STATE, (part + 1) * STATE)
            xraw[q, 0:8, lanes] += tail_fix(tail_tile(part), convx_v[:, lanes])
            bcraw[q, 0:8, lanes] += tail_fix(tail_tile(part + 2), convbc_v[:, lanes])
        xc = silu(xraw[q])
        bcc = silu(bcraw[q])
        b_low = bcc[:, :STATE].astype(BF16)
        c_low = bcc[:, STATE:].astype(BF16)
        scores = dot_nt(c_low, b_low)
        y = expcum[q] * dot_nt(c_low, start_at.astype(BF16)) + skip_wide * xc
        for hp in range(heads // 2):
            left, right = 2 * hp, 2 * hp + 1
            mixing = jnp.concatenate([scores * decay[q, left], scores * decay[q, right]], axis=1)
            held = jnp.concatenate(
                [jnp.where(lane_head == left, xc, 0.0), jnp.where(lane_head == right, xc, 0.0)],
                axis=0,
            )
            y = y + jnp.dot(mixing.astype(BF16), held.astype(BF16), preferred_element_type=F32)
        v = y * gate[q]
        ss_send[:, q * slot : (q + 1) * slot] = dot_nt(
            jnp.ones((8, width), F32), v * v, HIGHEST
        )[0:1]
        live = iota((slot, width), 0) < lengths_s[q]
        v = jnp.where(live, v * gain_v[...], 0.0)
        owners = slot // rows_owner // ny
        v_a[q * owners : (q + 1) * owners] = v.astype(BF16).reshape(owners, ny, rows_owner, width)
        saved.append((start_at, xc, b_low))

    def ss_copy(xx, yy, cc):
        return remote(
            ss_send,
            ss_recv.at[ci * nx + xi, yi],
            ss_ssem.at[cc * nx + xx, yy],
            ss_rsem.at[ci * nx + xi, yi],
            zi * 2 + cc,
            tensor_of(xx, yy),
        )

    def va_copy(yy, cc):
        return remote(
            v_a.at[:, yy],
            r_a.at[ci, yi],
            va_send.at[cc, yy],
            va_recv.at[ci, yi],
            zi * 2 + cc,
            tensor_of(xi, yy),
        )

    def vb_copy(xx, cc):
        return remote(
            v_a.at[xx],
            r_b.at[ci, xi],
            vb_send.at[cc, xx],
            vb_recv.at[ci, xi],
            zi * 2 + cc,
            tensor_of(xx, yi),
        )

    ss_peers = grid_peers() + [(xi, yi, 1 - ci)]
    for d in (2, 1, 3):
        if d < ny:
            va_copy((yi + d) % ny, ci).start()
        if d < nx:
            vb_copy((xi + d) % nx, ci).start()
    va_copy(yi, 1 - ci).start()
    vb_copy(xi, 1 - ci).start()
    for xx, yy, cc in ss_peers:
        ss_copy(xx, yy, cc).start()
    ss_recv[ci * nx + xi, yi] = ss_send[...]
    own_a = pltpu.make_async_copy(v_a.at[:, yi], r_a.at[ci, yi], own_sem.at[4])
    own_a.start()
    own_b = pltpu.make_async_copy(v_a.at[xi], r_b.at[ci, xi], own_sem.at[5])
    own_b.start()

    for q in range(2):
        start_at, xc, b_low = saved[q]
        weighed = (xc * weighin[q]).astype(BF16)
        final_o[q] = ending[q] * start_at + dot_tn(weighed, b_low)

    per_a = nx * rows_owner
    per_b = ny * rows_owner

    half = quarter // 2
    x_order = x_peers()[::-1]
    y_order = y_peers()[::-1]
    if nx > 2:
        x_order = [((xi + d) % nx, (ci + e) % 2) for d in (2, 1, 3) for e in range(2)]
        x_order.append((xi, 1 - ci))
    if ny > 2:
        y_order = [((yi + d) % ny, (ci + e) % 2) for d in (2, 1, 3) for e in range(2)]
        y_order.append((yi, 1 - ci))

    def block_a(yy, cols):
        lhs = jnp.concatenate(
            [r_a[0, yy].reshape(per_a, width), r_a[1, yy].reshape(per_a, width)], axis=0
        )
        return jnp.dot(lhs, w_a[yy, :, cols], preferred_element_type=F32)

    def block_b(at, cols):
        xx = at
        lhs = jnp.concatenate(
            [r_b[0, xx].reshape(per_b, width), r_b[1, xx].reshape(per_b, width)], axis=0
        )
        col = jnp.concatenate([col_b[:, at : at + 1], col_b[:, nx + at : nx + at + 1]], axis=0)
        return jnp.dot(lhs, w_b[xx, :, cols], preferred_element_type=F32) * col

    def wait_va(yy, cores):
        for cc in cores:
            remote(
                v_a.at[:, yi],
                r_a.at[cc, yy],
                va_send.at[cc, yy],
                va_recv.at[cc, yy],
                zi * 2 + cc,
                tensor_of(xi, yy),
            ).wait_recv()

    def wait_vb(xx, cores):
        for cc in cores:
            remote(
                v_a.at[xi],
                r_b.at[cc, xx],
                vb_send.at[cc, xx],
                vb_recv.at[cc, xx],
                zi * 2 + cc,
                tensor_of(xx, yi),
            ).wait_recv()

    handed = []

    def hand_on(buf, at, ssem, rsem):
        ref = buf.at[ci, at]
        copy = remote(ref, ref, ssem.at[1 - ci, at], rsem.at[ci, at], zi * 2 + 1 - ci, me_t)
        copy.start()
        handed.append(copy)

    for d in (1, 3, 2):
        if d < ny:
            yy = (yi + d) % ny
            wait_va(yy, (ci,))
            hand_on(r_a, yy, va_send, va_recv)
        if d < nx:
            xx = (xi + d) % nx
            wait_vb(xx, (ci,))
            hand_on(r_b, xx, vb_send, vb_recv)

    for xx, yy, cc in ss_peers:
        remote(
            ss_send,
            ss_recv.at[cc * nx + xx, yy],
            ss_ssem.at[cc * nx + xx, yy],
            ss_rsem.at[cc * nx + xx, yy],
            zi * 2 + cc,
            tensor_of(xx, yy),
        ).wait_recv()

    def scale_row(k):
        total = ss_recv[k, 0]
        for yy in range(1, ny):
            total = total + ss_recv[k, yy]
        return total

    scale_all = jnp.concatenate(
        [scale_row(cc * nx + xx) for cc in range(2) for xx in range(nx)], axis=0
    )
    scale_all = lax.rsqrt(scale_all / (ny * width) + EPSILON)
    pick_b = (iota((per_b, tokens), 1) == iota((per_b, tokens), 0) + xi * per_b).astype(F32)
    col_b = dot_nt(pick_b, scale_all, HIGHEST)
    where_row = iota((per_a, tokens), 0)
    wanted = (where_row // rows_owner * ny + yi) * rows_owner + where_row % rows_owner
    pick_a = (iota((per_a, tokens), 1) == wanted).astype(F32)
    scale_mine = jnp.concatenate([scale_row(xi), scale_row(nx + xi)], axis=0)
    scale_mine = lax.rsqrt(scale_mine / (ny * width) + EPSILON)
    col_a = dot_nt(pick_a, scale_mine, HIGHEST)

    weight_wait(w_a, dn_y, fill, fill, 1)
    if ny > 2:
        weight_wait(w_a, up_y, 0, fill, 3)
        opp_y = (yi + 2) % ny
        weight_wait(w_a, opp_y, 0, fill, 8)
        weight_wait(w_a, opp_y, fill, fill, 9)
    for d in range(ny):
        wait_va((yi + d) % ny, (1 - ci,))
    own_a.wait()
    own_b.wait()
    wait_vb(xi, (1 - ci,))
    weight_wait(w_b, dn_x, fill, fill, 5)
    if nx > 2:
        weight_wait(w_b, up_x, 0, fill, 7)
        opp_x = (xi + 2) % nx
        weight_wait(w_b, opp_x, 0, fill, 10)
        weight_wait(w_b, opp_x, fill, fill, 11)
    for d in range(1, nx):
        wait_vb((xi + d) % nx, (1 - ci,))

    def oa_copy(h, xx, cc):
        return remote(
            o_a.at[h, cc, xx],
            ro_a.at[h, xi, ci],
            oa_send.at[h, xx, cc],
            oa_recv.at[h, xi, ci],
            zi * 2 + cc,
            tensor_of(xx, yi),
        )

    def ob_copy(h, yy, cc):
        return remote(
            o_b.at[h, cc, yy],
            ro_b.at[h, yi, ci],
            ob_send.at[h, yy, cc],
            ob_recv.at[h, yi, ci],
            zi * 2 + cc,
            tensor_of(xi, yy),
        )

    for h in range(2):
        cols = slice(h * half, (h + 1) * half)
        total = block_a(0, cols)
        for yy in range(1, ny):
            total = total + block_a(yy, cols)
        for cc in range(2):
            part = total[cc * per_a : (cc + 1) * per_a, :] * col_a[:, cc : cc + 1]
            o_a[h, cc] = part.astype(BF16).reshape(nx, rows_owner, half)
        for xx, cc in x_order:
            oa_copy(h, xx, cc).start()
        total = block_b(0, cols)
        for at in range(1, nx):
            total = total + block_b(at, cols)
        o_b[h] = total.astype(BF16).reshape(2, ny, rows_owner, half)
        for yy, cc in y_order:
            ob_copy(h, yy, cc).start()
    own_out = []
    for h in range(2):
        own_out.append(
            pltpu.make_async_copy(o_a.at[h, ci, xi], ro_a.at[h, xi, ci], own_sem.at[6 + h])
        )
        own_out.append(
            pltpu.make_async_copy(o_b.at[h, ci, yi], ro_b.at[h, yi, ci], own_sem.at[8 + h])
        )
    for copy in own_out:
        copy.start()
    for copy in own_out:
        copy.wait()

    def sent(rr):
        first_copy(rr).wait_send()
        second_copy(rr).wait_send()

        @pl.when(has_tail(rr))
        def _():
            first_tail(rr).wait_send()

        @pl.when(has_tail(me_r))
        def _():
            second_tail(rr).wait_send()

    each_replica(sent)
    for copy in started:
        copy.wait_send()
    for xx, yy, cc in ss_peers:
        ss_copy(xx, yy, cc).wait_send()
    for d in range(1, ny):
        va_copy((yi + d) % ny, ci).wait_send()
    for d in range(1, nx):
        vb_copy((xi + d) % nx, ci).wait_send()
    va_copy(yi, 1 - ci).wait_send()
    vb_copy(xi, 1 - ci).wait_send()
    for copy in handed:
        copy.wait_send()

    for h in range(2):
        for xx, cc in x_peers():
            remote(
                o_a.at[h, cc, xx],
                ro_a.at[h, xx, cc],
                oa_send.at[h, xx, cc],
                oa_recv.at[h, xx, cc],
                zi * 2 + cc,
                tensor_of(xx, yi),
            ).wait_recv()
        for cc in range(2):
            total = ro_a[h, 0, cc].astype(F32)
            for xx in range(1, nx):
                total = total + ro_a[h, xx, cc].astype(F32)
            lo = cc * quarter + h * half
            mixed_o[:, lo : lo + half] = total.astype(BF16)
        for yy, cc in y_peers():
            remote(
                o_b.at[h, cc, yy],
                ro_b.at[h, yy, cc],
                ob_send.at[h, yy, cc],
                ob_recv.at[h, yy, cc],
                zi * 2 + cc,
                tensor_of(xi, yy),
            ).wait_recv()
        for cc in range(2):
            total = ro_b[h, 0, cc].astype(F32)
            for yy in range(1, ny):
                total = total + ro_b[h, yy, cc].astype(F32)
            lo = half_cols + cc * quarter + h * half
            mixed_o[:, lo : lo + half] = total.astype(BF16)

    for h in range(2):
        for yy, cc in y_peers():
            ob_copy(h, yy, cc).wait_send()
        for xx, cc in x_peers():
            oa_copy(h, xx, cc).wait_send()


def store_kernel(mixed_v, final_v, mixed_o, final_o, sem):
    first = pltpu.make_async_copy(mixed_v, mixed_o, sem.at[0])
    second = pltpu.make_async_copy(final_v, final_o, sem.at[1])
    first.start()
    second.start()
    first.wait()
    second.wait()


def local(
    sizes,
    x_input,
    z_input,
    bc_input,
    dt_raw,
    dt_bias,
    decay_rates,
    skip_gain,
    conv_x,
    conv_bc,
    norm_gain,
    out_weight,
    cached_states,
    cached_tail_x,
    cached_tail_bc,
    prefix_block,
    lengths,
):
    nr, nx, ny = sizes
    tokens, width = x_input.shape
    heads = dt_raw.shape[1]
    slot = tokens // 2
    out_cols = out_weight.shape[1]
    quarter = out_cols // 4
    rows_owner = tokens // (nx * ny)
    piece = width // nr
    tail_n = min(nr, TAIL_ROWS)
    tail_p = TAIL_ROWS // tail_n
    vmem = pltpu.VMEM
    dma = pltpu.SemaphoreType.DMA
    smem = pltpu.SMEM
    hbm_spec = pl.BlockSpec(memory_space=pl.ANY)
    vmem_spec = pl.BlockSpec(memory_space=pltpu.VMEM)
    scratch = [
        smem(prefix_block.shape, jnp.int32),
        smem(lengths.shape, jnp.int32),
        smem((heads,), F32),
        smem((heads,), F32),
        smem((heads,), F32),
        vmem((tokens, width), BF16),
        vmem((tokens, width), BF16),
        vmem((tokens, 2 * STATE), BF16),
        vmem((heads, tokens), F32),
        vmem((4, width), F32),
        vmem((4, 2 * STATE), F32),
        vmem((1, width), F32),
        vmem((2, width, STATE), F32),
        vmem((3, 2, width), F32),
        vmem((3, 2, 2 * STATE), F32),
        vmem((nr, 2 * piece, STATE), BF16),
        vmem((nr, 2 * piece, STATE), BF16),
        vmem((nr, 2 * piece, STATE), BF16),
        vmem((nr, 2 * piece, STATE), BF16),
        vmem((tail_n, 2 * tail_p, STATE), BF16),
        vmem((nr, 2 * tail_p, STATE), BF16),
        vmem((nr, 2 * tail_p, STATE), BF16),
        vmem((tail_n, 2 * tail_p, STATE), BF16),
        vmem((ny, width, quarter), BF16),
        vmem((nx, width, quarter), BF16),
        vmem((2, slot, width), F32),
        vmem((2, slot, 2 * STATE), F32),
        vmem((2, slot, width), F32),
        vmem((2, heads, slot, slot), F32),
        vmem((2, slot, width), F32),
        vmem((2, slot, width), F32),
        vmem((2, width, STATE), F32),
        vmem((nx, ny, rows_owner, width), BF16),
        vmem((2, ny, nx, rows_owner, width), BF16),
        vmem((2, nx, ny, rows_owner, width), BF16),
        vmem((1, tokens), F32),
        vmem((2 * nx, ny, 1, tokens), F32),
        vmem((2, 2, nx, rows_owner, quarter // 2), BF16),
        vmem((2, 2, ny, rows_owner, quarter // 2), BF16),
        vmem((2, nx, 2, rows_owner, quarter // 2), BF16),
        vmem((2, ny, 2, rows_owner, quarter // 2), BF16),
        dma((20,)),
        dma((10,)),
        dma((nr,)),
        dma((nr,)),
        dma((nr,)),
        dma((nr,)),
        dma((nr,)),
        dma((nr,)),
        dma((nr,)),
        dma((nr,)),
        dma((12,)),
        dma((12,)),
        dma((2, ny)),
        dma((2, ny)),
        dma((2, nx)),
        dma((2, nx)),
        dma((2 * nx, ny)),
        dma((2 * nx, ny)),
        dma((2, nx, 2)),
        dma((2, nx, 2)),
        dma((2, ny, 2)),
        dma((2, ny, 2)),
    ]
    mixed, final_states = pl.pallas_call(
        functools.partial(layer_kernel, sizes),
        out_shape=(vmem((rows_owner, out_cols), BF16), vmem((2, width, STATE), F32)),
        in_specs=[hbm_spec] * 16,
        out_specs=(vmem_spec, vmem_spec),
        scratch_shapes=scratch,
        compiler_params=pltpu.CompilerParams(
            collective_id=0, has_side_effects=True, vmem_limit_bytes=56 * 1024 * 1024
        ),
        name="prefill_layer",
    )(
        prefix_block,
        lengths,
        dt_bias,
        decay_rates,
        skip_gain,
        x_input,
        z_input,
        bc_input,
        dt_raw.T,
        conv_x,
        conv_bc,
        norm_gain.reshape(1, width),
        out_weight,
        cached_states.reshape(2, width, STATE),
        jnp.transpose(cached_tail_x, (1, 0, 2)),
        jnp.transpose(cached_tail_bc, (1, 0, 2)),
    )
    mixed, final_states = pl.pallas_call(
        store_kernel,
        out_shape=(
            jax.ShapeDtypeStruct((rows_owner, out_cols), BF16),
            jax.ShapeDtypeStruct((2, width, STATE), F32),
        ),
        in_specs=[vmem_spec] * 2,
        out_specs=(hbm_spec, hbm_spec),
        scratch_shapes=[dma((2,))],
        compiler_params=pltpu.CompilerParams(vmem_limit_bytes=4 * 1024 * 1024),
        name="store_results",
    )(mixed, final_states)
    return mixed, final_states.reshape(2, heads, HEAD_DIM, STATE)


def tensor_grid(count):
    side = 1
    while side * side < count:
        side *= 2
    return side, count // side


def solution(mesh):
    placed = (
        P("replica", "tensor"),
        P("replica", "tensor"),
        P("replica", None),
        P("replica", "tensor"),
        P("tensor"),
        P("tensor"),
        P("tensor"),
        P(None, "tensor"),
        P(),
        P("tensor"),
        P("tensor", None),
        P("replica", "tensor", None, None),
        P("replica", None, "tensor"),
        P("replica", None, None),
        P(),
        P("replica"),
    )
    sizes = (mesh.shape["replica"],) + tensor_grid(mesh.shape["tensor"])
    return jax.shard_map(
        functools.partial(local, sizes),
        mesh=mesh,
        in_specs=placed,
        out_specs=(P(("replica", "tensor"), None), P("replica", "tensor", None, None)),
        check_vma=False,
    )
```
